256 devices in a mesh: band: 32 (over z_lo, x, y), comp: 8 (over z_hi, core).
Axes of the slice: x: 4, y: 4, z: 8 (z_hi: 4, z_lo: 2; z = z_hi * 2 + z_lo), core: 2. Of those that a mesh axis runs over, the one named last changes fastest.
Arguments:
- energy: float32 [1296, 96, 512], P('comp', 'band'), may hold values from 0 to 2
- land_sea: int32 [96, 512], P('band'), may hold values 0 or 1
- group_speed: float32 [36], replicated, may hold values from 0.05 to 0.6
- interp_one: bfloat16 [1296, 1296], replicated, may hold values from -0.15625 to 0.15625
- interp_two: bfloat16 [1296, 1296], replicated, may hold values from -0.15625 to 0.15625
Outputs:
- energy_out: float32 [1296, 96, 512], P('comp', 'band')
The draws below stay inside these ranges and needn't reach their ends.
All inputs are finite; a program needn't handle non-finite values. No bound on the sum of `land_sea` on one device may be relied on, other than what follows from the above.
Results may differ from the reference program's by a relative error of at most 0.00097.
Values may be sent and summed in bfloat16 or wider, within the bound.
No kernel may reach another device: no remote copies, remote signals or barrier semaphores. Data moves between devices by JAX's collectives and lax.ppermute only.
A program may use at most 64 MiB of HBM per device.

```python
import math
import jax
import jax.numpy as jnp
from jax import lax

NDIR = 36
NFREQ = 36
K = 1296
ROWS_DEV = 3
NLON = 512
STEPS = 2
SUBSTEPS = 3
NLAT = 96


def draw_energy(key, part):
    base_key = jax.random.fold_in(key, 11)
    strip_key = jax.random.fold_in(key, 12)
    pick_key = jax.random.fold_in(key, 13)
    levels = jax.random.uniform(base_key, (K, NLAT, NLON), jnp.float32, 0.0, 2.0)
    row_index = jnp.arange(NLAT, dtype=jnp.int32)
    edge_row = (row_index % ROWS_DEV == 0) | (row_index % ROWS_DEV == ROWS_DEV - 1)
    chosen = jax.random.randint(pick_key, (NLAT,), 0, 2) == 1
    begins = jax.random.randint(strip_key, (NLAT,), 0, NLON)
    columns = jnp.arange(NLON, dtype=jnp.int32)
    offset = (columns[None, :] - begins[:, None]) % NLON
    drawn_cells = (edge_row & chosen)[:, None] & (offset < NLON // 4)
    return jnp.where(drawn_cells[None], jnp.zeros_like(levels), levels)


def touch_ends(values, key, least, largest):
    index_at = [jax.random.randint(jax.random.fold_in(key, axis), (), 0, length) for axis, length in enumerate(values.shape)]
    widest = values.shape.index(max(values.shape))
    next_to = index_at[:widest] + [(index_at[widest] + 1) % values.shape[widest]] + index_at[widest + 1:]
    return values.at[tuple(index_at)].set(least).at[tuple(next_to)].set(largest)


def bell_draw(rng, extent, scale, reach, kind=jnp.bfloat16):
    result = scale * jax.random.normal(rng, extent, jnp.float32)
    return jnp.clip(result, min=-reach, max=reach).astype(kind)


def setup_inputs(seed: int = 0) -> dict:
    key_of = jax.random.split(jax.random.key(seed), 6)
    energy = draw_energy(jax.random.fold_in(key_of[5], 71), 0)
    land_sea = touch_ends((jax.random.randint(key_of[1], (NLAT, NLON), 0, 5) < 4).astype(jnp.int32), jax.random.fold_in(key_of[1], 1), 0, 1)
    group_speed = jnp.clip(jnp.exp(jax.random.uniform(key_of[2], (NFREQ,), jnp.float32, math.log(0.05), math.log(0.6))), 0.05, 0.6)
    interp_one = bell_draw(key_of[3], (K, K), K ** -0.5, 0.15625)
    interp_two = bell_draw(key_of[4], (K, K), K ** -0.5, 0.15625)
    return dict(energy=energy, land_sea=land_sea, group_speed=group_speed, interp_one=interp_one, interp_two=interp_two)


source_rate = 0.05


def geometry(group_speed, first_comp, comp_count, first_row, row_count, total_rows):
    component = first_comp + jnp.arange(comp_count, dtype=jnp.int32)
    freq_idx = component // NDIR
    dir_idx = component % NDIR
    direction = (2.0 * math.pi / NDIR) * (dir_idx.astype(jnp.float32) + 0.5)
    choose = freq_idx[:, None] == jnp.arange(NFREQ, dtype=jnp.int32)[None, :]
    picked = jnp.sum(jnp.where(choose, group_speed[None, :], jnp.zeros_like(group_speed)[None, :]), axis=1)
    row_index = (first_row + jnp.arange(row_count, dtype=jnp.int32)).astype(jnp.float32)
    latitude = (math.pi / 180.0) * (-70.0 + 140.0 * (row_index + 0.5) / total_rows)
    along_x = (picked * jnp.cos(direction))[:, None] * jnp.cos(latitude)[None, :]
    along_y = picked * jnp.sin(direction)
    eastward = (4 * dir_idx + 2 < NDIR) | (4 * dir_idx + 2 > 3 * NDIR)
    northward = 2 * dir_idx + 1 < NDIR
    return along_x[:, :, None], along_y[:, None, None], eastward[:, None, None], northward[:, None, None]


def advect(energy_now, padded, geometry_here, sea_mask):
    along_x, along_y, eastward, northward = geometry_here
    from_west = jnp.roll(energy_now, 1, axis=2)
    from_east = jnp.roll(energy_now, -1, axis=2)
    upwind_x = jnp.where(eastward, from_west, from_east)
    upwind_y = jnp.where(northward, padded[:, :-2], padded[:, 2:])
    advected = energy_now - jnp.abs(along_x) * (energy_now - upwind_x) - jnp.abs(along_y) * (energy_now - upwind_y)
    return advected * sea_mask


def sources(columns, interp_one, interp_two):
    lowered = columns.astype(jnp.bfloat16)
    first_image = jnp.dot(interp_one, lowered, preferred_element_type=jnp.float32)
    second = jnp.dot(interp_two, lowered, preferred_element_type=jnp.float32)
    widened = lowered.astype(jnp.float32)
    weight_one = (widened * second * second).astype(jnp.bfloat16)
    weight_two = (widened * first_image * first_image).astype(jnp.bfloat16)
    dims = (((0,), (0,)), ((), ()))
    return (lax.dot_general(interp_one, weight_one, dims, preferred_element_type=jnp.float32)
            - lax.dot_general(interp_two, weight_two, dims, preferred_element_type=jnp.float32))


def reference(energy, land_sea, group_speed, interp_one, interp_two):
    sea_mask = land_sea.astype(jnp.float32)[None]
    geometry_here = geometry(group_speed, 0, K, 0, NLAT, NLAT)
    energy_now = energy * sea_mask
    for time_step in range(STEPS):
        for substep in range(SUBSTEPS):
            padded = jnp.pad(energy_now, ((0, 0), (1, 1), (0, 0)))
            energy_now = advect(energy_now, padded, geometry_here, sea_mask)
        by_rows = jnp.transpose(energy_now, (1, 0, 2))
        change = lax.map(lambda row_block: sources(row_block, interp_one, interp_two), by_rows)
        change = jnp.transpose(change, (1, 0, 2))
        energy_now = energy_now + source_rate * sea_mask * change
    return energy_now
```

```python
import functools
import math

import jax
import jax.numpy as jnp
import numpy as np
from jax import lax
from jax.experimental import pallas as pl
from jax.experimental.pallas import tpu as pltpu
from jax.sharding import Mesh
from jax.sharding import PartitionSpec as P

NDIR = 36
NFREQ = 36
K = NDIR * NFREQ
ROWS = 3
NLON = 512
HALF = NDIR // 2
LOCAL = 162
PAD = 168
SOURCE_RATE = 0.05
COMP = ("comp_0", "comp_1")
EVERY = ("band", "comp_0", "comp_1")
LEVELS = 2 * ROWS
HOPS = ((0, 0), (2, 0), (2, 1), (1, 0), (3, 0), (1, 1), (3, 1), (0, 1))
TOP = 32767.0
F32 = jnp.float32
I16 = jnp.int16


def code_of(largest):
    return jnp.ceil(jnp.log2(jnp.maximum(largest, 1e-30)) * 128.0)


def to_wire(code):
    return jnp.exp2(code * (-1.0 / 128.0)) * TOP


def from_wire(code):
    return jnp.exp2(code * (1.0 / 128.0)) * (1.0 / TOP)


def rounded(values):
    return jnp.floor(values + 0.5).astype(jnp.int32).astype(I16)


def iota(shape, dim):
    return lax.broadcasted_iota(jnp.int32, shape, dim)


def halo_kernel(where_ref, e_ref, sea_ref, a_ref, b_ref, scr):
    core = where_ref[1]
    for level in range(ROWS):
        row_a = level + core * (2 - 2 * level)
        for row, groups, out in (
            (row_a, (0, 2, 4, 6, 8), a_ref),
            (2 - row_a, (1, 3, 5, 7), b_ref),
        ):
            n = HALF * len(groups)
            total = out.shape[1]
            sea = sea_ref[row]
            for i, g in enumerate(groups):
                scr[HALF * i : HALF * i + HALF, :] = (
                    e_ref[row, HALF * g : HALF * g + HALF, :] * sea
                )
            scr[n : scr.shape[0], :] = jnp.zeros((scr.shape[0] - n, NLON), F32)
            x = scr[0:total, :]
            code = code_of(jnp.max(jnp.abs(x), axis=0, keepdims=True))
            at = iota((total, NLON), 0)
            q = jnp.where(at == n, sea, x * to_wire(code))
            q = jnp.where(at == n + 1, code, q)
            out[level] = rounded(q)


def one_substep(level, here, upstream, east, cx, cy, sea, width):
    shifted = jnp.where(east, pltpu.roll(here, 1, 1), pltpu.roll(here, width - 1, 1))
    return (here - cx[level] * (here - shifted) - cy * (here - upstream)) * sea


def advected(levels, east, cx, cy, sea, width):
    for substep in range(ROWS):
        levels = [
            one_substep(i, levels[i], levels[i - 1], east, cx, cy, sea[i], width)
            if i > substep
            else levels[i]
            for i in range(LEVELS)
        ]
    return levels[ROWS:]


def first_kernel(where_ref, e_ref, sea_ref, a_ref, b_ref, geo_ref, *rest):
    outs, (own, halo, wide, peak) = rest[:8], rest[8:]
    chip, core = where_ref[0], where_ref[1]
    masks = {}
    for name, ref, groups in (("a", a_ref, (0, 2, 4, 6, 8)), ("b", b_ref, (1, 3, 5, 7))):
        n = HALF * len(groups)
        total = ref.shape[1]
        for level in range(ROWS):
            wide[0, 0:total, :] = ref[level, :, 0:256].astype(F32)
            wide[1, 0:total, :] = ref[level, :, 256:512].astype(F32)
            for side in range(2):
                lanes = slice(256 * side, 256 * side + 256)
                scale = from_wire(wide[side, n + 1 : n + 2, :])
                masks[name, level, side] = wide[side, n : n + 1, :]
                for i, g in enumerate(groups):
                    halo[level, HALF * g : HALF * g + HALF, lanes] = (
                        wide[side, HALF * i : HALF * i + HALF, :] * scale
                    )
    for level in range(ROWS):
        halo[level, LOCAL:PAD, :] = jnp.zeros((PAD - LOCAL, NLON), F32)
        own[level, 0:LOCAL, :] = e_ref[level] * sea_ref[level]
        own[level, LOCAL:PAD, :] = jnp.zeros((PAD - LOCAL, NLON), F32)
    mask_a = [jnp.concatenate([masks["a", r, 0], masks["a", r, 1]], axis=1) for r in range(ROWS)]
    mask_b = [jnp.concatenate([masks["b", r, 0], masks["b", r, 1]], axis=1) for r in range(ROWS)]
    peak[...] = jnp.zeros_like(peak)
    sea_rows = [sea_ref[r] for r in range(ROWS)]
    lane = iota((8, 128), 1)

    @pl.loop(0, PAD // 8)
    def _(block):
        rows = pl.ds(pl.multiple_of(block * 8, 8), 8)
        geo = geo_ref[rows, :]

        def column(i, width):
            return jnp.broadcast_to(geo[:, i : i + 1], (8, width))

        cx = [column(i, NLON) for i in range(LEVELS)]
        cy = column(6, NLON)
        east = column(7, NLON) > 0.5
        north = column(8, NLON) > 0.5
        is_a = column(9, NLON) > 0.5
        e = [own[r, rows, :] for r in range(ROWS)]
        levels = [halo[r, rows, :] for r in range(ROWS)] + [
            jnp.where(north, e[0], e[2]),
            e[1],
            jnp.where(north, e[2], e[0]),
        ]
        sea = [jnp.where(is_a, mask_a[r], mask_b[r]) for r in range(ROWS)] + [
            jnp.where(north, sea_rows[0], sea_rows[2]),
            jnp.broadcast_to(sea_rows[1], (8, NLON)),
            jnp.where(north, sea_rows[2], sea_rows[0]),
        ]
        down = advected(levels, east, cx, cy, sea, NLON)
        new = [jnp.where(north, down[0], down[2]), down[1], jnp.where(north, down[2], down[0])]
        at = iota((8, NLON), 0) + block * 8
        new = [jnp.where(at == LOCAL, sea_rows[r], new[r]) for r in range(ROWS)]
        counts = (iota((8, 256), 0) + block * 8) < LOCAL
        tiles = [[new[r][:, 128 * t : 128 * t + 128] for t in range(4)] for r in range(ROWS)]
        turned = [[pltpu.roll(tiles[r][t], 64, 1) for t in range(4)] for r in range(ROWS)]
        for p in range(8):
            t = p // 2
            if p % 2 == 0:
                f = [jnp.where(lane < 96, tiles[r][t], tiles[r][(t + 3) % 4]) for r in range(ROWS)]
            else:
                f = [
                    jnp.where((lane >= 64) & (lane < 96), turned[r][(t + 1) % 4], turned[r][t])
                    for r in range(ROWS)
                ]
            low = jnp.where(lane < 64, f[0], pltpu.roll(f[1], 64, 1))
            high = f[2]
            high = jnp.where((lane >= 67) & (lane < 70), pltpu.roll(f[0], 3, 1), high)
            high = jnp.where((lane >= 70) & (lane < 73), pltpu.roll(f[1], 6, 1), high)
            high = jnp.where((lane >= 119) & (lane < 122), pltpu.roll(f[1], 122, 1), high)
            high = jnp.where((lane >= 122) & (lane < 125), pltpu.roll(f[0], 125, 1), high)
            both = jnp.concatenate([low, high], axis=1)
            wide[p, rows, :] = both
            peak[p] = jnp.maximum(peak[p], jnp.where(counts, jnp.abs(both), 0.0))

    for out, (k, t) in zip(outs, HOPS):
        p = ((chip + k) % 4) * 2 + lax.bitwise_xor(core, t)
        code = code_of(jnp.max(peak[p], axis=0, keepdims=True))
        x = wide[p]
        at = iota((PAD, 256), 0)
        q = jnp.where(at < LOCAL, x * to_wire(code), x)
        q = jnp.where(at == LOCAL + 1, code, q)
        out[...] = rounded(q)


CHUNK = 432


def add_sources(state, mask, one, two, one_t, two_t, xs, h1, h2):
    xs[...] = state[...].astype(jnp.bfloat16)

    @pl.loop(0, K // CHUNK)
    def _(i):
        rows = pl.ds(pl.multiple_of(i * CHUNK, 16), CHUNK)
        u = jnp.dot(one[rows, :], xs[...], preferred_element_type=F32)
        v = jnp.dot(two[rows, :], xs[...], preferred_element_type=F32)
        x = xs[rows, :].astype(F32)
        h1[rows, :] = (x * v * v).astype(jnp.bfloat16)
        h2[rows, :] = (x * u * u).astype(jnp.bfloat16)

    @pl.loop(0, K // CHUNK)
    def _(i):
        rows = pl.ds(pl.multiple_of(i * CHUNK, 16), CHUNK)
        src = jnp.dot(one_t[rows, :], h1[...], preferred_element_type=F32) - jnp.dot(
            two_t[rows, :], h2[...], preferred_element_type=F32
        )
        state[rows, :] = state[rows, :] + (SOURCE_RATE * mask) * src


SEND = 656


def second_kernel(where_ref, *refs):
    ins, (one, two, one_t, two_t), rest = refs[:8], refs[8:12], refs[12:]
    own, north, south, state, blocks, xs, h1, h2, scr = rest
    chip, core = where_ref[0], where_ref[1]
    for ref, (k, t) in zip(ins, HOPS):
        s = ((chip + 4 - k) % 4) * 2 + lax.bitwise_xor(core, t)
        scr[0:PAD, :] = ref[...].astype(F32)
        scale = from_wire(scr[LOCAL + 1 : LOCAL + 2, :])
        blocks[s] = scr[0:PAD, :] * scale
    mask = scr[LOCAL : LOCAL + 1, :]
    for s in range(8):
        state[LOCAL * s : LOCAL * s + LOCAL, :] = blocks[s, 0:LOCAL, :]
    add_sources(state, mask, one, two, one_t, two_t, xs, h1, h2)
    n = K // 2
    for side, out in enumerate((north, south)):
        for f in range(NFREQ):
            first = NDIR * f + HALF * side
            own[side, HALF * f : HALF * f + HALF, :] = state[first : first + HALF, :]
        x = own[side, 0:n, :]
        code = code_of(jnp.max(jnp.abs(x), axis=0, keepdims=True))
        scr[0:n, :] = x * to_wire(code)
        at = iota((SEND - n, 256), 0)
        scr[n:SEND, :] = jnp.where(at == 0, mask, jnp.where(at == 1, code, 0.0))
        out[...] = rounded(scr[...])
    own[0, n : n + 8, :] = jnp.broadcast_to(mask, (8, 256))
    own[1, n : n + 8, :] = jnp.broadcast_to(mask, (8, 256))


def spread(low, high, lane):
    out = []
    for body, by in ((low, 3), (pltpu.roll(low, 64, 1), 6)):
        side = jnp.where(lane < 96, pltpu.roll(high, 128 - by, 1), pltpu.roll(high, by, 1))
        out.append(jnp.where(lane < 64, body, side))
    return [out[0], out[1], high]


def third_kernel(where_ref, own, north, south, geo_ref, one, two, one_t, two_t, *rest):
    outs, (state, parts, blocks, xs, h1, h2, scr, seas) = rest[:8], rest[8:]
    chip, core = where_ref[0], where_ref[1]
    lane = iota((8, 128), 1)
    n = K // 2
    for side, ref in enumerate((north, south)):
        scr[...] = ref[...].astype(F32)
        scale = from_wire(scr[n + 1 : n + 2, :])
        far = jnp.broadcast_to(scr[n : n + 1, :], (8, 256))
        near = own[side, n : n + 8, :]
        order = (0, 1, 2) if side == 0 else (2, 1, 0)
        far, near = (spread(m[:, :128], m[:, 128:], lane) for m in (far, near))
        for i, r in enumerate(order):
            seas[i] = far[r]
            seas[ROWS + i] = near[r]
        scale = jnp.broadcast_to(scale, (8, 256))

        @pl.loop(0, n // 8)
        def _(block):
            rows = pl.ds(pl.multiple_of(block * 8, 8), 8)
            geo = geo_ref[side, rows, :]

            def column(i):
                return jnp.broadcast_to(geo[:, i : i + 1], (8, 128))

            cx = [column(i) for i in range(LEVELS)]
            cy = column(6)
            east = column(7) > 0.5
            h = scr[rows, :] * scale
            e = own[side, rows, :]
            h, e = (spread(m[:, :128], m[:, 128:], lane) for m in (h, e))
            levels = [h[r] for r in order] + [e[r] for r in order]
            sea = [seas[i] for i in range(LEVELS)]
            down = advected(levels, east, cx, cy, sea, 128)
            new = [down[r] for r in order]
            low = jnp.where(lane < 64, new[0], pltpu.roll(new[1], 64, 1))
            high = jnp.where(lane < 64, new[2], 0.0)
            parts[side, rows, :] = jnp.concatenate([low, high], axis=1)

        for f in range(NFREQ):
            first = NDIR * f + HALF * side
            state[first : first + HALF, :] = parts[side, HALF * f : HALF * f + HALF, :]
    mask = own[0, n : n + 1, :]
    add_sources(state, mask, one, two, one_t, two_t, xs, h1, h2)
    for s in range(8):
        blocks[s, 0:LOCAL, :] = state[LOCAL * s : LOCAL * s + LOCAL, :]
        blocks[s, LOCAL:PAD, :] = jnp.zeros((PAD - LOCAL, 256), F32)
    for out, (k, t) in zip(outs, HOPS):
        s = ((chip + k) % 4) * 2 + lax.bitwise_xor(core, t)
        x = blocks[s]
        low, high = x[:, :128], x[:, 128:]
        paired = jnp.where(iota((88, 128), 1) < 64, high[0:88], pltpu.roll(high[80:168], 64, 1))
        for part, first, used in ((low, 0, LOCAL), (paired, PAD, 82)):
            size = part.shape[0]
            code = code_of(jnp.max(jnp.abs(part), axis=0, keepdims=True))
            q = jnp.where(iota((size, 128), 0) == used, code, part * to_wire(code))
            scr[first : first + size, 0:128] = q
        out[...] = rounded(scr[0:256, 0:128])


def last_kernel(where_ref, *refs):
    ins, (out, tiles, scr) = refs[:8], refs[8:]
    chip, core = where_ref[0], where_ref[1]
    for ref, (k, t) in zip(ins, HOPS):
        p = ((chip + 4 - k) % 4) * 2 + lax.bitwise_xor(core, t)
        scr[...] = ref[...].astype(F32)
        for first, size, used in ((0, PAD, LOCAL), (PAD, 88, 82)):
            scale = from_wire(scr[first + used : first + used + 1, :])
            tiles[p, first : first + size, :] = scr[first : first + size, :] * scale
    lane = iota((256, 128), 1)
    for t in range(4):
        a, b = tiles[2 * t], tiles[2 * t + 1]
        first = jnp.where(lane < 64, a, pltpu.roll(b, 64, 1))
        second = jnp.where(lane < 64, pltpu.roll(a, 64, 1), b)
        lanes = slice(128 * t, 128 * t + 128)
        out[0, :, lanes] = first[0:LOCAL]
        out[1, :, lanes] = second[0:LOCAL]
        out[2, 0:80, lanes] = first[PAD : PAD + 80]
        out[2, 80:LOCAL, lanes] = second[PAD : PAD + 82]


def call(kernel, out, ins, scratch, limit):
    vmem = pl.BlockSpec(memory_space=pltpu.VMEM)
    smem = pl.BlockSpec(memory_space=pltpu.SMEM)
    return pl.pallas_call(
        kernel,
        out_shape=out,
        in_specs=[smem] + [vmem] * (len(ins) - 1),
        out_specs=jax.tree.map(lambda _: vmem, out),
        scratch_shapes=[pltpu.VMEM(s, d) for s, d in scratch],
        compiler_params=pltpu.CompilerParams(vmem_limit_bytes=limit << 20),
    )(*ins)


def geometry(group_speed, first_row, total_rows):
    comp = np.arange(K)
    d = comp % NDIR
    theta = 2.0 * math.pi / NDIR * (d + 0.5)
    east = (4 * d + 2 < NDIR) | (4 * d + 2 > 3 * NDIR)
    north = 2 * d + 1 < NDIR
    speed = jnp.broadcast_to(group_speed[:, None], (NFREQ, NDIR)).reshape(K)
    along_x = speed * jnp.asarray(np.abs(np.cos(theta)), F32)
    along_y = speed * jnp.asarray(np.abs(np.sin(theta)), F32)
    step = jnp.arange(LEVELS, dtype=jnp.int32)
    rows = jnp.stack([first_row - ROWS + step, first_row + LEVELS - 1 - step]).astype(F32)
    cosine = jnp.cos(math.pi / 180.0 * (-70.0 + 140.0 * (rows + 0.5) / total_rows))
    across = jnp.where(jnp.asarray(north)[:, None], cosine[0], cosine[1])
    flags = np.stack([east, north, (comp // HALF) % 2 == 0], axis=1).astype(np.float32)
    return jnp.concatenate(
        [along_x[:, None] * across, along_y[:, None], jnp.asarray(flags), jnp.zeros((K, 6), F32)],
        axis=1,
    )


def exchanged(arrays):
    done = [arrays[0]]
    for x, (k, t) in list(zip(arrays, HOPS))[1:]:
        pairs = [
            (chip * 2 + core, ((chip + k) % 4) * 2 + (core ^ t)) for chip in range(4) for core in range(2)
        ]
        done.append(lax.ppermute(x, COMP, pairs))
    return done


def body(energy, land_sea, group_speed, interp_one, interp_two):
    bands = lax.axis_size("band")
    band = lax.axis_index("band")
    chip = lax.axis_index("comp_0")
    core = lax.axis_index("comp_1")
    here = jnp.stack([chip, core]).astype(jnp.int32)
    e = jnp.transpose(energy, (1, 0, 2))
    sea = land_sea.astype(F32)[:, None, :]
    shape = jax.ShapeDtypeStruct

    a, b = call(
        halo_kernel,
        (shape((ROWS, 96, NLON), I16), shape((ROWS, 80, NLON), I16)),
        (here, e, sea),
        [((96, NLON), F32)],
        8,
    )
    up, down = ([], [])
    for i in range(bands):
        for g in range(4):
            for side in range(2):
                j = i * 8 + g * 2 + side
                for way, step in ((up, 1 - 2 * side), (down, 2 * side - 1)):
                    if 0 <= i + step < bands:
                        way.append((j, j + 8 * step))
    a = lax.ppermute(a, EVERY, up)
    b = lax.ppermute(b, EVERY, down)

    geo = geometry(group_speed, band * ROWS, bands * ROWS)
    geo_here = lax.dynamic_slice_in_dim(geo, (chip * 2 + core) * LOCAL, LOCAL, 0)
    local_a = (np.arange(LOCAL) // HALF % 2 == 0).astype(np.float32)
    geo_here = jnp.concatenate([geo_here[:, :9], jnp.asarray(local_a)[:, None], geo_here[:, 10:]], axis=1)
    geo_here = jnp.pad(geo_here, ((0, PAD - LOCAL), (0, 0)))
    geo_sides = geo.reshape(NFREQ, 2, HALF, 16).transpose(1, 0, 2, 3).reshape(2, K // 2, 16)
    one_t, two_t = interp_one.T, interp_two.T

    packed = call(
        first_kernel,
        [shape((PAD, 256), I16)] * 8,
        (here, e, sea, a, b, geo_here),
        [
            ((ROWS, PAD, NLON), F32),
            ((ROWS, PAD, NLON), F32),
            ((8, PAD, 256), F32),
            ((8, 8, 256), F32),
        ],
        16,
    )
    packed = exchanged(packed)

    half = K // 2
    matmul_scratch = [((K, 256), jnp.bfloat16)] * 3
    own, north, south = call(
        second_kernel,
        (shape((2, half + 8, 256), F32), shape((SEND, 256), I16), shape((SEND, 256), I16)),
        (here, *packed, interp_one, interp_two, one_t, two_t),
        [((K, 256), F32), ((8, PAD, 256), F32)] + matmul_scratch + [((SEND, 256), F32)],
        30,
    )
    north = lax.ppermute(north, "band", [(i, i + 1) for i in range(bands - 1)])
    south = lax.ppermute(south, "band", [(i + 1, i) for i in range(bands - 1)])

    final = call(
        third_kernel,
        [shape((256, 128), I16)] * 8,
        (here, own, north, south, geo_sides, interp_one, interp_two, one_t, two_t),
        [((K, 256), F32), ((2, half, 256), F32), ((8, PAD, 256), F32)]
        + matmul_scratch
        + [((SEND, 256), F32), ((LEVELS, 8, 128), F32)],
        34,
    )
    final = exchanged(final)
    out = call(
        last_kernel,
        shape((ROWS, LOCAL, NLON), F32),
        (here, *final),
        [((8, 256, 128), F32), ((256, 128), F32)],
        8,
    )
    return jnp.transpose(out, (1, 0, 2))


def solution(mesh):
    finer = Mesh(mesh.devices.reshape(mesh.shape["band"], 4, 2), EVERY)
    return jax.shard_map(
        body,
        mesh=finer,
        in_specs=(P(COMP, "band", None), P("band", None), P(), P(), P()),
        out_specs=P(COMP, "band", None),
        check_vma=False,
    )
```

```python
import functools
import math

import jax
import jax.numpy as jnp
import numpy as np
from jax import lax
from jax.experimental import pallas as pl
from jax.experimental.pallas import tpu as pltpu
from jax.sharding import Mesh
from jax.sharding import PartitionSpec as P

NDIR = 36
NFREQ = 36
K = NDIR * NFREQ
ROWS = 3
NLON = 512
HALF = NDIR // 2
LOCAL = 162
PAD = 168
SOURCE_RATE = 0.05
COMP = ("comp_0", "comp_1")
EVERY = ("band", "comp_0", "comp_1")
LEVELS = 2 * ROWS
HOPS = ((0, 0), (2, 0), (2, 1), (1, 0), (3, 0), (1, 1), (3, 1), (0, 1))
TRIP1 = 56
TRIP3 = 216
TOP = 32767.0
F32 = jnp.float32
I16 = jnp.int16


def code_of(largest):
    return jnp.ceil(jnp.log2(jnp.maximum(largest, 1e-30)) * 128.0)


def to_wire(code):
    return jnp.exp2(code * (-1.0 / 128.0)) * TOP


def from_wire(code):
    return jnp.exp2(code * (1.0 / 128.0)) * (1.0 / TOP)


def rounded(values):
    return jnp.floor(values + 0.5).astype(jnp.int32).astype(I16)


def iota(shape, dim):
    return lax.broadcasted_iota(jnp.int32, shape, dim)


def halo_kernel(where_ref, e_ref, sea_ref, own, a_ref, b_ref, scr):
    core = where_ref[1]
    sea = [sea_ref[r : r + 1, :].astype(F32) for r in range(ROWS)]
    for row in range(ROWS):
        own[row, 0:LOCAL, :] = e_ref[row] * sea[row]
        own[row, LOCAL:PAD, :] = jnp.broadcast_to(sea[row], (PAD - LOCAL, NLON))
    for level in range(ROWS):
        row_a = level + core * (2 - 2 * level)
        for row, groups, out in (
            (row_a, (0, 2, 4, 6, 8), a_ref),
            (2 - row_a, (1, 3, 5, 7), b_ref),
        ):
            n = HALF * len(groups)
            total = out.shape[1]
            for i, g in enumerate(groups):
                scr[HALF * i : HALF * i + HALF, :] = own[row, HALF * g : HALF * g + HALF, :]
            scr[n:total, :] = jnp.zeros((total - n, NLON), F32)
            x = scr[0:total, :]
            code = code_of(jnp.max(jnp.abs(x), axis=0, keepdims=True))
            at = iota((total, NLON), 0)
            q = jnp.where(at == n, own[row, LOCAL : LOCAL + 1, :], x * to_wire(code))
            q = jnp.where(at == n + 1, code, q)
            out[level] = rounded(q)


def one_substep(level, here, upstream, east, cx, cy, sea, width):
    shifted = jnp.where(east, pltpu.roll(here, 1, 1), pltpu.roll(here, width - 1, 1))
    return (here - cx[level] * (here - shifted) - cy * (here - upstream)) * sea


def advected(levels, east, cx, cy, sea, width):
    for substep in range(ROWS):
        levels = [
            one_substep(i, levels[i], levels[i - 1], east, cx, cy, sea[i], width)
            if i > substep
            else levels[i]
            for i in range(LEVELS)
        ]
    return levels[ROWS:]


def first_kernel(where_ref, own, a_ref, b_ref, geo_ref, *rest):
    outs, (halo, wide, peak) = rest[:8], rest[8:]
    chip, core = where_ref[0], where_ref[1]
    masks = {}
    for name, ref, groups in (("a", a_ref, (0, 2, 4, 6, 8)), ("b", b_ref, (1, 3, 5, 7))):
        n = HALF * len(groups)
        total = ref.shape[1]
        for level in range(ROWS):
            wide[0, 0:total, :] = ref[level, :, 0:256].astype(F32)
            wide[1, 0:total, :] = ref[level, :, 256:512].astype(F32)
            for side in range(2):
                lanes = slice(256 * side, 256 * side + 256)
                scale = from_wire(wide[side, n + 1 : n + 2, :])
                masks[name, level, side] = wide[side, n : n + 1, :]
                for i, g in enumerate(groups):
                    halo[level, HALF * g : HALF * g + HALF, lanes] = (
                        wide[side, HALF * i : HALF * i + HALF, :] * scale
                    )
    for level in range(ROWS):
        halo[level, LOCAL:PAD, :] = jnp.zeros((PAD - LOCAL, NLON), F32)
    mask_a = [jnp.concatenate([masks["a", r, 0], masks["a", r, 1]], axis=1) for r in range(ROWS)]
    mask_b = [jnp.concatenate([masks["b", r, 0], masks["b", r, 1]], axis=1) for r in range(ROWS)]
    peak[...] = jnp.zeros_like(peak)
    sea_rows = [own[r, LOCAL : LOCAL + 1, :] for r in range(ROWS)]
    lane = iota((TRIP1, 128), 1)

    @pl.loop(0, PAD // TRIP1)
    def _(block):
        rows = pl.ds(pl.multiple_of(block * TRIP1, 8), TRIP1)
        geo = geo_ref[rows, :]

        def column(i, width):
            return jnp.broadcast_to(geo[:, i : i + 1], (TRIP1, width))

        cx = [column(i, NLON) for i in range(LEVELS)]
        cy = column(6, NLON)
        east = column(7, NLON) > 0.5
        north = column(8, NLON) > 0.5
        is_a = column(9, NLON) > 0.5
        e = [own[r, rows, :] for r in range(ROWS)]
        levels = [halo[r, rows, :] for r in range(ROWS)] + [
            jnp.where(north, e[0], e[2]),
            e[1],
            jnp.where(north, e[2], e[0]),
        ]
        sea = [jnp.where(is_a, mask_a[r], mask_b[r]) for r in range(ROWS)] + [
            jnp.where(north, sea_rows[0], sea_rows[2]),
            jnp.broadcast_to(sea_rows[1], (TRIP1, NLON)),
            jnp.where(north, sea_rows[2], sea_rows[0]),
        ]
        down = advected(levels, east, cx, cy, sea, NLON)
        new = [jnp.where(north, down[0], down[2]), down[1], jnp.where(north, down[2], down[0])]
        at = iota((TRIP1, NLON), 0) + block * TRIP1
        new = [jnp.where(at == LOCAL, sea_rows[r], new[r]) for r in range(ROWS)]
        counts = (iota((TRIP1, 256), 0) + block * TRIP1) < LOCAL
        tiles = [[new[r][:, 128 * t : 128 * t + 128] for t in range(4)] for r in range(ROWS)]
        turned = [[pltpu.roll(tiles[r][t], 64, 1) for t in range(4)] for r in range(ROWS)]
        for p in range(8):
            t = p // 2
            if p % 2 == 0:
                f = [jnp.where(lane < 96, tiles[r][t], tiles[r][(t + 3) % 4]) for r in range(ROWS)]
            else:
                f = [
                    jnp.where((lane >= 64) & (lane < 96), turned[r][(t + 1) % 4], turned[r][t])
                    for r in range(ROWS)
                ]
            low = jnp.where(lane < 64, f[0], pltpu.roll(f[1], 64, 1))
            high = f[2]
            high = jnp.where((lane >= 67) & (lane < 70), pltpu.roll(f[0], 3, 1), high)
            high = jnp.where((lane >= 70) & (lane < 73), pltpu.roll(f[1], 6, 1), high)
            high = jnp.where((lane >= 119) & (lane < 122), pltpu.roll(f[1], 122, 1), high)
            high = jnp.where((lane >= 122) & (lane < 125), pltpu.roll(f[0], 125, 1), high)
            both = jnp.concatenate([low, high], axis=1)
            wide[p, rows, :] = both
            peak[p] = jnp.maximum(peak[p], jnp.where(counts, jnp.abs(both), 0.0))

    for out, (k, t) in zip(outs, HOPS):
        p = ((chip + k) % 4) * 2 + lax.bitwise_xor(core, t)
        code = code_of(jnp.max(peak[p], axis=0, keepdims=True))
        x = wide[p]
        at = iota((PAD, 256), 0)
        q = jnp.where(at < LOCAL, x * to_wire(code), x)
        q = jnp.where(at == LOCAL + 1, code, q)
        out[...] = rounded(q)


CHUNK = 432


def started(weights, held):
    copies = [pltpu.make_async_copy(w, v, m) for w, v, m in zip(weights, held[:2], held[2:])]
    for c in copies:
        c.start()
    return copies


def add_sources(state, mask, copies, held, xs, h1, h2):
    one, two = held[:2]
    xs[...] = state[...].astype(jnp.bfloat16)
    for c in copies:
        c.wait()

    @pl.loop(0, K // CHUNK)
    def _(i):
        rows = pl.ds(pl.multiple_of(i * CHUNK, 16), CHUNK)
        u = jnp.dot(one[rows, :], xs[...], preferred_element_type=F32)
        v = jnp.dot(two[rows, :], xs[...], preferred_element_type=F32)
        x = xs[rows, :].astype(F32)
        h1[rows, :] = (x * v * v).astype(jnp.bfloat16)
        h2[rows, :] = (x * u * u).astype(jnp.bfloat16)

    over = (((0,), (0,)), ((), ()))
    for first in range(0, K, 512):
        size = min(512, K - first)
        src = lax.dot_general(one[:, first : first + size], h1[...], over, preferred_element_type=F32)
        src = src - lax.dot_general(two[:, first : first + size], h2[...], over, preferred_element_type=F32)
        rows = slice(first, first + size)
        state[rows, :] = state[rows, :] + (SOURCE_RATE * mask) * src


SEND = 656


def second_kernel(where_ref, *refs):
    ins, weights, rest = refs[:8], refs[8:10], refs[10:]
    own, north, south, state, blocks, xs, h1, h2, scr, *held = rest
    copies = started(weights, held)
    chip, core = where_ref[0], where_ref[1]
    for ref, (k, t) in zip(ins, HOPS):
        s = ((chip + 4 - k) % 4) * 2 + lax.bitwise_xor(core, t)
        scr[0:PAD, :] = ref[...].astype(F32)
        scale = from_wire(scr[LOCAL + 1 : LOCAL + 2, :])
        blocks[s] = scr[0:PAD, :] * scale
    mask = scr[LOCAL : LOCAL + 1, :]
    for s in range(8):
        state[LOCAL * s : LOCAL * s + LOCAL, :] = blocks[s, 0:LOCAL, :]
    add_sources(state, mask, copies, held, xs, h1, h2)
    n = K // 2
    for side, out in enumerate((north, south)):
        for f in range(NFREQ):
            first = NDIR * f + HALF * side
            own[side, HALF * f : HALF * f + HALF, :] = state[first : first + HALF, :]
        x = own[side, 0:n, :]
        code = code_of(jnp.max(jnp.abs(x), axis=0, keepdims=True))
        scr[0:n, :] = x * to_wire(code)
        at = iota((SEND - n, 256), 0)
        scr[n:SEND, :] = jnp.where(at == 0, mask, jnp.where(at == 1, code, 0.0))
        out[...] = rounded(scr[...])
    own[0, n : n + 8, :] = jnp.broadcast_to(mask, (8, 256))
    own[1, n : n + 8, :] = jnp.broadcast_to(mask, (8, 256))


def spread(low, high, lane):
    out = []
    for body, by in ((low, 3), (pltpu.roll(low, 64, 1), 6)):
        side = jnp.where(lane < 96, pltpu.roll(high, 128 - by, 1), pltpu.roll(high, by, 1))
        out.append(jnp.where(lane < 64, body, side))
    return [out[0], out[1], high]


def third_kernel(where_ref, own, north, south, geo_ref, one_hbm, two_hbm, *rest):
    outs, (state, parts, blocks, xs, h1, h2, scr, seas, *held) = rest[:8], rest[8:]
    copies = started((one_hbm, two_hbm), held)
    chip, core = where_ref[0], where_ref[1]
    lane = iota((8, 128), 1)
    lanes = iota((TRIP3, 128), 1)
    n = K // 2
    for side, ref in enumerate((north, south)):
        scr[...] = ref[...].astype(F32)
        scale = from_wire(scr[n + 1 : n + 2, :])
        far = jnp.broadcast_to(scr[n : n + 1, :], (8, 256))
        near = own[side, n : n + 8, :]
        order = (0, 1, 2) if side == 0 else (2, 1, 0)
        far, near = (spread(m[:, :128], m[:, 128:], lane) for m in (far, near))
        for i, r in enumerate(order):
            seas[i] = far[r]
            seas[ROWS + i] = near[r]
        scale = jnp.broadcast_to(scale, (TRIP3, 256))

        @pl.loop(0, n // TRIP3)
        def _(block):
            rows = pl.ds(pl.multiple_of(block * TRIP3, 8), TRIP3)
            geo = geo_ref[side, rows, :]

            def column(i):
                return jnp.broadcast_to(geo[:, i : i + 1], (TRIP3, 128))

            cx = [column(i) for i in range(LEVELS)]
            cy = column(6)
            east = column(7) > 0.5
            h = scr[rows, :] * scale
            e = own[side, rows, :]
            h, e = (spread(m[:, :128], m[:, 128:], lanes) for m in (h, e))
            levels = [h[r] for r in order] + [e[r] for r in order]
            sea = [jnp.tile(seas[i], (TRIP3 // 8, 1)) for i in range(LEVELS)]
            down = advected(levels, east, cx, cy, sea, 128)
            new = [down[r] for r in order]
            low = jnp.where(lanes < 64, new[0], pltpu.roll(new[1], 64, 1))
            high = jnp.where(lanes < 64, new[2], 0.0)
            parts[side, rows, :] = jnp.concatenate([low, high], axis=1)

        for f in range(NFREQ):
            first = NDIR * f + HALF * side
            state[first : first + HALF, :] = parts[side, HALF * f : HALF * f + HALF, :]
    mask = own[0, n : n + 1, :]
    add_sources(state, mask, copies, held, xs, h1, h2)
    for s in range(8):
        blocks[s, 0:LOCAL, :] = state[LOCAL * s : LOCAL * s + LOCAL, :]
        blocks[s, LOCAL:PAD, :] = jnp.zeros((PAD - LOCAL, 256), F32)
    for out, (k, t) in zip(outs, HOPS):
        s = ((chip + k) % 4) * 2 + lax.bitwise_xor(core, t)
        x = blocks[s]
        low, high = x[:, :128], x[:, 128:]
        paired = jnp.where(iota((88, 128), 1) < 64, high[0:88], pltpu.roll(high[80:168], 64, 1))
        for part, first, used in ((low, 0, LOCAL), (paired, PAD, 82)):
            size = part.shape[0]
            code = code_of(jnp.max(jnp.abs(part), axis=0, keepdims=True))
            q = jnp.where(iota((size, 128), 0) == used, code, part * to_wire(code))
            scr[first : first + size, 0:128] = q
        out[...] = rounded(scr[0:256, 0:128])


def last_kernel(where_ref, *refs):
    ins, (out, tiles, scr) = refs[:8], refs[8:]
    chip, core = where_ref[0], where_ref[1]
    for ref, (k, t) in zip(ins, HOPS):
        p = ((chip + 4 - k) % 4) * 2 + lax.bitwise_xor(core, t)
        scr[...] = ref[...].astype(F32)
        for first, size, used in ((0, PAD, LOCAL), (PAD, 88, 82)):
            scale = from_wire(scr[first + used : first + used + 1, :])
            tiles[p, first : first + size, :] = scr[first : first + size, :] * scale
    lane = iota((256, 128), 1)
    for t in range(4):
        a, b = tiles[2 * t], tiles[2 * t + 1]
        first = jnp.where(lane < 64, a, pltpu.roll(b, 64, 1))
        second = jnp.where(lane < 64, pltpu.roll(a, 64, 1), b)
        lanes = slice(128 * t, 128 * t + 128)
        out[0, :, lanes] = first[0:LOCAL]
        out[1, :, lanes] = second[0:LOCAL]
        out[2, 0:80, lanes] = first[PAD : PAD + 80]
        out[2, 80:LOCAL, lanes] = second[PAD : PAD + 82]


def call(kernel, out, ins, scratch, limit, weights=()):
    vmem = pl.BlockSpec(memory_space=pltpu.VMEM)
    smem = pl.BlockSpec(memory_space=pltpu.SMEM)
    return pl.pallas_call(
        kernel,
        out_shape=out,
        in_specs=[smem]
        + [vmem] * (len(ins) - 1)
        + [pl.BlockSpec(memory_space=pl.ANY)] * len(weights),
        out_specs=jax.tree.map(lambda _: vmem, out),
        scratch_shapes=[pltpu.VMEM(s, d) for s, d in scratch]
        + [pltpu.VMEM(w.shape, w.dtype) for w in weights]
        + [pltpu.SemaphoreType.DMA] * len(weights),
        compiler_params=pltpu.CompilerParams(vmem_limit_bytes=limit << 20),
    )(*ins, *weights)


def geometry(group_speed, first_row, total_rows):
    comp = np.arange(K)
    d = comp % NDIR
    theta = 2.0 * math.pi / NDIR * (d + 0.5)
    east = (4 * d + 2 < NDIR) | (4 * d + 2 > 3 * NDIR)
    north = 2 * d + 1 < NDIR
    speed = jnp.broadcast_to(group_speed[:, None], (NFREQ, NDIR)).reshape(K)
    along_x = speed * jnp.asarray(np.abs(np.cos(theta)), F32)
    along_y = speed * jnp.asarray(np.abs(np.sin(theta)), F32)
    step = jnp.arange(LEVELS, dtype=jnp.int32)
    rows = jnp.stack([first_row - ROWS + step, first_row + LEVELS - 1 - step]).astype(F32)
    cosine = jnp.cos(math.pi / 180.0 * (-70.0 + 140.0 * (rows + 0.5) / total_rows))
    across = jnp.where(jnp.asarray(north)[:, None], cosine[0], cosine[1])
    flags = np.stack([east, north, (comp // HALF) % 2 == 0], axis=1).astype(np.float32)
    return jnp.concatenate(
        [along_x[:, None] * across, along_y[:, None], jnp.asarray(flags), jnp.zeros((K, 6), F32)],
        axis=1,
    )


def exchanged(arrays):
    done = [arrays[0]]
    for x, (k, t) in list(zip(arrays, HOPS))[1:]:
        pairs = [
            (chip * 2 + core, ((chip + k) % 4) * 2 + (core ^ t)) for chip in range(4) for core in range(2)
        ]
        done.append(lax.ppermute(x, COMP, pairs))
    return done


def body(energy, land_sea, group_speed, interp_one, interp_two):
    bands = lax.axis_size("band")
    band = lax.axis_index("band")
    chip = lax.axis_index("comp_0")
    core = lax.axis_index("comp_1")
    here = jnp.stack([chip, core]).astype(jnp.int32)
    e = jnp.transpose(energy, (1, 0, 2))
    shape = jax.ShapeDtypeStruct

    own, a, b = call(
        halo_kernel,
        (
            shape((ROWS, PAD, NLON), F32),
            shape((ROWS, 96, NLON), I16),
            shape((ROWS, 80, NLON), I16),
        ),
        (here, e, land_sea),
        [((96, NLON), F32)],
        8,
    )
    up, down = ([], [])
    for i in range(bands):
        for g in range(4):
            for side in range(2):
                j = i * 8 + g * 2 + side
                for way, step in ((up, 1 - 2 * side), (down, 2 * side - 1)):
                    if 0 <= i + step < bands:
                        way.append((j, j + 8 * step))
    a = lax.ppermute(a, EVERY, up)
    b = lax.ppermute(b, EVERY, down)

    geo = geometry(group_speed, band * ROWS, bands * ROWS)
    geo_here = lax.dynamic_slice_in_dim(geo, (chip * 2 + core) * LOCAL, LOCAL, 0)
    local_a = (np.arange(LOCAL) // HALF % 2 == 0).astype(np.float32)
    geo_here = jnp.concatenate([geo_here[:, :9], jnp.asarray(local_a)[:, None], geo_here[:, 10:]], axis=1)
    geo_here = jnp.pad(geo_here, ((0, PAD - LOCAL), (0, 0)))
    geo_sides = geo.reshape(NFREQ, 2, HALF, 16).transpose(1, 0, 2, 3).reshape(2, K // 2, 16)

    packed = call(
        first_kernel,
        [shape((PAD, 256), I16)] * 8,
        (here, own, a, b, geo_here),
        [
            ((ROWS, PAD, NLON), F32),
            ((8, PAD, 256), F32),
            ((8, TRIP1, 256), F32),
        ],
        10,
    )
    packed = exchanged(packed)

    half = K // 2
    matmul_scratch = [((K, 256), jnp.bfloat16)] * 3
    own, north, south = call(
        second_kernel,
        (shape((2, half + 8, 256), F32), shape((SEND, 256), I16), shape((SEND, 256), I16)),
        (here, *packed),
        [((K, 256), F32), ((8, PAD, 256), F32)] + matmul_scratch + [((SEND, 256), F32)],
        20,
        (interp_one, interp_two),
    )
    north = lax.ppermute(north, "band", [(i, i + 1) for i in range(bands - 1)])
    south = lax.ppermute(south, "band", [(i + 1, i) for i in range(bands - 1)])

    final = call(
        third_kernel,
        [shape((256, 128), I16)] * 8,
        (here, own, north, south, geo_sides),
        [((K, 256), F32), ((2, half, 256), F32), ((8, PAD, 256), F32)]
        + matmul_scratch
        + [((SEND, 256), F32), ((LEVELS, 8, 128), F32)],
        24,
        (interp_one, interp_two),
    )
    final = exchanged(final)
    out = call(
        last_kernel,
        shape((ROWS, LOCAL, NLON), F32),
        (here, *final),
        [((8, 256, 128), F32), ((256, 128), F32)],
        8,
    )
    return jnp.transpose(out, (1, 0, 2))


def solution(mesh):
    finer = Mesh(mesh.devices.reshape(mesh.shape["band"], 4, 2), EVERY)
    return jax.shard_map(
        body,
        mesh=finer,
        in_specs=(P(COMP, "band", None), P("band", None), P(), P(), P()),
        out_specs=P(COMP, "band", None),
        check_vma=False,
    )
```

```python
import functools
import math

import jax
import jax.numpy as jnp
import numpy as np
from jax import lax
from jax.experimental import pallas as pl
from jax.experimental.pallas import tpu as pltpu
from jax.sharding import Mesh
from jax.sharding import PartitionSpec as P

NDIR = 36
NFREQ = 36
K = NDIR * NFREQ
ROWS = 3
NLON = 512
HALF = NDIR // 2
LOCAL = 162
PAD = 168
SOURCE_RATE = 0.05
COMP = ("comp_0", "comp_1")
EVERY = ("band", "comp_0", "comp_1")
LEVELS = 2 * ROWS
HOPS = ((0, 0), (2, 0), (2, 1), (1, 0), (3, 0), (1, 1), (3, 1), (0, 1))
TRIP1 = 56
TRIP3 = 216
TOP = 32767.0
F32 = jnp.float32
I16 = jnp.int16


def code_of(largest):
    return jnp.ceil(jnp.log2(jnp.maximum(largest, 1e-30)) * 128.0)


def to_wire(code):
    return jnp.exp2(code * (-1.0 / 128.0)) * TOP


def from_wire(code):
    return jnp.exp2(code * (1.0 / 128.0)) * (1.0 / TOP)


def rounded(values):
    return jnp.floor(values + 0.5).astype(jnp.int32).astype(I16)


def iota(shape, dim):
    return lax.broadcasted_iota(jnp.int32, shape, dim)


def halo_kernel(where_ref, e_ref, sea_ref, own, a_ref, b_ref, scr):
    core = where_ref[1]
    sea = [sea_ref[r : r + 1, :].astype(F32) for r in range(ROWS)]
    for row in range(ROWS):
        own[row, 0:LOCAL, :] = e_ref[row] * sea[row]
        own[row, LOCAL:PAD, :] = jnp.broadcast_to(sea[row], (PAD - LOCAL, NLON))
    for level in range(ROWS):
        row_a = level + core * (2 - 2 * level)
        for row, groups, out in (
            (row_a, (0, 2, 4, 6, 8), a_ref),
            (2 - row_a, (1, 3, 5, 7), b_ref),
        ):
            n = HALF * len(groups)
            total = out.shape[1]
            for i, g in enumerate(groups):
                scr[HALF * i : HALF * i + HALF, :] = own[row, HALF * g : HALF * g + HALF, :]
            scr[n:total, :] = jnp.zeros((total - n, NLON), F32)
            x = scr[0:total, :]
            code = code_of(jnp.max(jnp.abs(x), axis=0, keepdims=True))
            at = iota((total, NLON), 0)
            q = jnp.where(at == n, own[row, LOCAL : LOCAL + 1, :], x * to_wire(code))
            q = jnp.where(at == n + 1, code, q)
            out[level] = rounded(q)


def one_substep(level, here, upstream, east, cx, cy, sea, width):
    shifted = jnp.where(east, pltpu.roll(here, 1, 1), pltpu.roll(here, width - 1, 1))
    return (here - cx[level] * (here - shifted) - cy * (here - upstream)) * sea


def advected(levels, east, cx, cy, sea, width):
    for substep in range(ROWS):
        levels = [
            one_substep(i, levels[i], levels[i - 1], east, cx, cy, sea[i], width)
            if i > substep
            else levels[i]
            for i in range(LEVELS)
        ]
    return levels[ROWS:]


def first_kernel(where_ref, own, a_ref, b_ref, geo_ref, *rest):
    outs, (halo, wide, peak) = rest[:8], rest[8:]
    chip, core = where_ref[0], where_ref[1]
    masks = {}
    for name, ref, groups in (("a", a_ref, (0, 2, 4, 6, 8)), ("b", b_ref, (1, 3, 5, 7))):
        n = HALF * len(groups)
        total = ref.shape[1]
        for level in range(ROWS):
            wide[0, 0:total, :] = ref[level, :, 0:256].astype(F32)
            wide[1, 0:total, :] = ref[level, :, 256:512].astype(F32)
            for side in range(2):
                lanes = slice(256 * side, 256 * side + 256)
                scale = from_wire(wide[side, n + 1 : n + 2, :])
                masks[name, level, side] = wide[side, n : n + 1, :]
                for i, g in enumerate(groups):
                    halo[level, HALF * g : HALF * g + HALF, lanes] = (
                        wide[side, HALF * i : HALF * i + HALF, :] * scale
                    )
    for level in range(ROWS):
        halo[level, LOCAL:PAD, :] = jnp.zeros((PAD - LOCAL, NLON), F32)
    mask_a = [jnp.concatenate([masks["a", r, 0], masks["a", r, 1]], axis=1) for r in range(ROWS)]
    mask_b = [jnp.concatenate([masks["b", r, 0], masks["b", r, 1]], axis=1) for r in range(ROWS)]
    peak[...] = jnp.zeros_like(peak)
    sea_rows = [own[r, LOCAL : LOCAL + 1, :] for r in range(ROWS)]
    lane = iota((TRIP1, 128), 1)

    @pl.loop(0, PAD // TRIP1)
    def _(block):
        rows = pl.ds(pl.multiple_of(block * TRIP1, 8), TRIP1)
        geo = geo_ref[rows, :]

        def column(i, width):
            return jnp.broadcast_to(geo[:, i : i + 1], (TRIP1, width))

        cx = [column(i, NLON) for i in range(LEVELS)]
        cy = column(6, NLON)
        east = column(7, NLON) > 0.5
        north = column(8, NLON) > 0.5
        is_a = column(9, NLON) > 0.5
        e = [own[r, rows, :] for r in range(ROWS)]
        levels = [halo[r, rows, :] for r in range(ROWS)] + [
            jnp.where(north, e[0], e[2]),
            e[1],
            jnp.where(north, e[2], e[0]),
        ]
        sea = [jnp.where(is_a, mask_a[r], mask_b[r]) for r in range(ROWS)] + [
            jnp.where(north, sea_rows[0], sea_rows[2]),
            jnp.broadcast_to(sea_rows[1], (TRIP1, NLON)),
            jnp.where(north, sea_rows[2], sea_rows[0]),
        ]
        down = advected(levels, east, cx, cy, sea, NLON)
        new = [jnp.where(north, down[0], down[2]), down[1], jnp.where(north, down[2], down[0])]
        at = iota((TRIP1, NLON), 0) + block * TRIP1
        new = [jnp.where(at == LOCAL, sea_rows[r], new[r]) for r in range(ROWS)]
        counts = (iota((TRIP1, 256), 0) + block * TRIP1) < LOCAL
        tiles = [[new[r][:, 128 * t : 128 * t + 128] for t in range(4)] for r in range(ROWS)]
        turned = [[pltpu.roll(tiles[r][t], 64, 1) for t in range(4)] for r in range(ROWS)]
        for p in range(8):
            t = p // 2
            if p % 2 == 0:
                f = [jnp.where(lane < 96, tiles[r][t], tiles[r][(t + 3) % 4]) for r in range(ROWS)]
            else:
                f = [
                    jnp.where((lane >= 64) & (lane < 96), turned[r][(t + 1) % 4], turned[r][t])
                    for r in range(ROWS)
                ]
            low = jnp.where(lane < 64, f[0], pltpu.roll(f[1], 64, 1))
            high = f[2]
            high = jnp.where((lane >= 67) & (lane < 70), pltpu.roll(f[0], 3, 1), high)
            high = jnp.where((lane >= 70) & (lane < 73), pltpu.roll(f[1], 6, 1), high)
            high = jnp.where((lane >= 119) & (lane < 122), pltpu.roll(f[1], 122, 1), high)
            high = jnp.where((lane >= 122) & (lane < 125), pltpu.roll(f[0], 125, 1), high)
            both = jnp.concatenate([low, high], axis=1)
            wide[p, rows, :] = both
            peak[p] = jnp.maximum(peak[p], jnp.where(counts, jnp.abs(both), 0.0))

    for out, (k, t) in zip(outs, HOPS):
        p = ((chip + k) % 4) * 2 + lax.bitwise_xor(core, t)
        code = code_of(jnp.max(peak[p], axis=0, keepdims=True))
        x = wide[p]
        at = iota((PAD, 256), 0)
        q = jnp.where(at < LOCAL, x * to_wire(code), x)
        q = jnp.where(at == LOCAL + 1, code, q)
        out[...] = rounded(q)


CHUNK = 432


def add_sources(state, mask, one, two, xs, h1, h2):
    xs[...] = state[...].astype(jnp.bfloat16)

    @pl.loop(0, K // CHUNK)
    def _(i):
        rows = pl.ds(pl.multiple_of(i * CHUNK, 16), CHUNK)
        u = jnp.dot(one[rows, :], xs[...], preferred_element_type=F32)
        v = jnp.dot(two[rows, :], xs[...], preferred_element_type=F32)
        x = xs[rows, :].astype(F32)
        h1[rows, :] = (x * v * v).astype(jnp.bfloat16)
        h2[rows, :] = (x * u * u).astype(jnp.bfloat16)

    over = (((0,), (0,)), ((), ()))
    for first in range(0, K, 512):
        size = min(512, K - first)
        src = lax.dot_general(one[:, first : first + size], h1[...], over, preferred_element_type=F32)
        src = src - lax.dot_general(two[:, first : first + size], h2[...], over, preferred_element_type=F32)
        rows = slice(first, first + size)
        state[rows, :] = state[rows, :] + (SOURCE_RATE * mask) * src


SEND = 656


def second_kernel(where_ref, *refs):
    ins, (one, two), rest = refs[:8], refs[8:10], refs[10:]
    own, north, south, state, blocks, xs, h1, h2, scr = rest
    chip, core = where_ref[0], where_ref[1]
    for ref, (k, t) in zip(ins, HOPS):
        s = ((chip + 4 - k) % 4) * 2 + lax.bitwise_xor(core, t)
        scr[0:PAD, :] = ref[...].astype(F32)
        scale = from_wire(scr[LOCAL + 1 : LOCAL + 2, :])
        blocks[s] = scr[0:PAD, :] * scale
    mask = scr[LOCAL : LOCAL + 1, :]
    for s in range(8):
        state[LOCAL * s : LOCAL * s + LOCAL, :] = blocks[s, 0:LOCAL, :]
    add_sources(state, mask, one, two, xs, h1, h2)
    n = K // 2
    for side, out in enumerate((north, south)):
        for f in range(NFREQ):
            first = NDIR * f + HALF * side
            own[side, HALF * f : HALF * f + HALF, :] = state[first : first + HALF, :]
        x = own[side, 0:n, :]
        code = code_of(jnp.max(jnp.abs(x), axis=0, keepdims=True))
        scr[0:n, :] = x * to_wire(code)
        at = iota((SEND - n, 256), 0)
        scr[n:SEND, :] = jnp.where(at == 0, mask, jnp.where(at == 1, code, 0.0))
        out[...] = rounded(scr[...])
    own[0, n : n + 8, :] = jnp.broadcast_to(mask, (8, 256))
    own[1, n : n + 8, :] = jnp.broadcast_to(mask, (8, 256))


def spread(low, high, lane):
    out = []
    for body, by in ((low, 3), (pltpu.roll(low, 64, 1), 6)):
        side = jnp.where(lane < 96, pltpu.roll(high, 128 - by, 1), pltpu.roll(high, by, 1))
        out.append(jnp.where(lane < 64, body, side))
    return [out[0], out[1], high]


def third_kernel(where_ref, own, north, south, geo_ref, one, two, *rest):
    outs, (state, parts, blocks, xs, h1, h2, scr, seas) = rest[:8], rest[8:]
    chip, core = where_ref[0], where_ref[1]
    lane = iota((8, 128), 1)
    lanes = iota((TRIP3, 128), 1)
    n = K // 2
    for side, ref in enumerate((north, south)):
        scr[...] = ref[...].astype(F32)
        scale = from_wire(scr[n + 1 : n + 2, :])
        far = jnp.broadcast_to(scr[n : n + 1, :], (8, 256))
        near = own[side, n : n + 8, :]
        order = (0, 1, 2) if side == 0 else (2, 1, 0)
        far, near = (spread(m[:, :128], m[:, 128:], lane) for m in (far, near))
        for i, r in enumerate(order):
            seas[i] = far[r]
            seas[ROWS + i] = near[r]
        scale = jnp.broadcast_to(scale, (TRIP3, 256))

        @pl.loop(0, n // TRIP3)
        def _(block):
            rows = pl.ds(pl.multiple_of(block * TRIP3, 8), TRIP3)
            geo = geo_ref[side, rows, :]

            def column(i):
                return jnp.broadcast_to(geo[:, i : i + 1], (TRIP3, 128))

            cx = [column(i) for i in range(LEVELS)]
            cy = column(6)
            east = column(7) > 0.5
            h = scr[rows, :] * scale
            e = own[side, rows, :]
            h, e = (spread(m[:, :128], m[:, 128:], lanes) for m in (h, e))
            levels = [h[r] for r in order] + [e[r] for r in order]
            sea = [jnp.tile(seas[i], (TRIP3 // 8, 1)) for i in range(LEVELS)]
            down = advected(levels, east, cx, cy, sea, 128)
            new = [down[r] for r in order]
            low = jnp.where(lanes < 64, new[0], pltpu.roll(new[1], 64, 1))
            high = jnp.where(lanes < 64, new[2], 0.0)
            parts[side, rows, :] = jnp.concatenate([low, high], axis=1)

        for f in range(NFREQ):
            first = NDIR * f + HALF * side
            state[first : first + HALF, :] = parts[side, HALF * f : HALF * f + HALF, :]
    mask = own[0, n : n + 1, :]
    add_sources(state, mask, one, two, xs, h1, h2)
    for s in range(8):
        blocks[s, 0:LOCAL, :] = state[LOCAL * s : LOCAL * s + LOCAL, :]
        blocks[s, LOCAL:PAD, :] = jnp.zeros((PAD - LOCAL, 256), F32)
    for out, (k, t) in zip(outs, HOPS):
        s = ((chip + k) % 4) * 2 + lax.bitwise_xor(core, t)
        x = blocks[s]
        low, high = x[:, :128], x[:, 128:]
        paired = jnp.where(iota((88, 128), 1) < 64, high[0:88], pltpu.roll(high[80:168], 64, 1))
        for part, first, used in ((low, 0, LOCAL), (paired, PAD, 82)):
            size = part.shape[0]
            code = code_of(jnp.max(jnp.abs(part), axis=0, keepdims=True))
            q = jnp.where(iota((size, 128), 0) == used, code, part * to_wire(code))
            scr[first : first + size, 0:128] = q
        out[...] = rounded(scr[0:256, 0:128])


def last_kernel(where_ref, *refs):
    ins, (out, tiles, scr) = refs[:8], refs[8:]
    chip, core = where_ref[0], where_ref[1]
    for ref, (k, t) in zip(ins, HOPS):
        p = ((chip + 4 - k) % 4) * 2 + lax.bitwise_xor(core, t)
        scr[...] = ref[...].astype(F32)
        for first, size, used in ((0, PAD, LOCAL), (PAD, 88, 82)):
            scale = from_wire(scr[first + used : first + used + 1, :])
            tiles[p, first : first + size, :] = scr[first : first + size, :] * scale
    lane = iota((256, 128), 1)
    for t in range(4):
        a, b = tiles[2 * t], tiles[2 * t + 1]
        first = jnp.where(lane < 64, a, pltpu.roll(b, 64, 1))
        second = jnp.where(lane < 64, pltpu.roll(a, 64, 1), b)
        lanes = slice(128 * t, 128 * t + 128)
        out[0, :, lanes] = first[0:LOCAL]
        out[1, :, lanes] = second[0:LOCAL]
        out[2, 0:80, lanes] = first[PAD : PAD + 80]
        out[2, 80:LOCAL, lanes] = second[PAD : PAD + 82]


def call(kernel, out, ins, scratch, limit, weights=(), us=2):
    vmem = pl.BlockSpec(memory_space=pltpu.VMEM)
    smem = pl.BlockSpec(memory_space=pltpu.SMEM)
    return pl.pallas_call(
        kernel,
        out_shape=out,
        in_specs=[smem]
        + [vmem] * (len(ins) - 1)
        + [vmem] * len(weights),
        out_specs=jax.tree.map(lambda _: vmem, out),
        scratch_shapes=[pltpu.VMEM(s, d) for s, d in scratch],
        compiler_params=pltpu.CompilerParams(vmem_limit_bytes=limit << 20),
        cost_estimate=pl.CostEstimate(flops=0, bytes_accessed=us * 3_500_000, transcendentals=0),
    )(*ins, *weights)


def geometry(group_speed, first_row, total_rows):
    comp = np.arange(K)
    d = comp % NDIR
    theta = 2.0 * math.pi / NDIR * (d + 0.5)
    east = (4 * d + 2 < NDIR) | (4 * d + 2 > 3 * NDIR)
    north = 2 * d + 1 < NDIR
    speed = jnp.broadcast_to(group_speed[:, None], (NFREQ, NDIR)).reshape(K)
    along_x = speed * jnp.asarray(np.abs(np.cos(theta)), F32)
    along_y = speed * jnp.asarray(np.abs(np.sin(theta)), F32)
    step = jnp.arange(LEVELS, dtype=jnp.int32)
    rows = jnp.stack([first_row - ROWS + step, first_row + LEVELS - 1 - step]).astype(F32)
    cosine = jnp.cos(math.pi / 180.0 * (-70.0 + 140.0 * (rows + 0.5) / total_rows))
    across = jnp.where(jnp.asarray(north)[:, None], cosine[0], cosine[1])
    flags = np.stack([east, north, (comp // HALF) % 2 == 0], axis=1).astype(np.float32)
    return jnp.concatenate(
        [along_x[:, None] * across, along_y[:, None], jnp.asarray(flags), jnp.zeros((K, 6), F32)],
        axis=1,
    )


def exchanged(arrays):
    done = [arrays[0]]
    for x, (k, t) in list(zip(arrays, HOPS))[1:]:
        pairs = [
            (chip * 2 + core, ((chip + k) % 4) * 2 + (core ^ t)) for chip in range(4) for core in range(2)
        ]
        done.append(lax.ppermute(x, COMP, pairs))
    return done


def body(energy, land_sea, group_speed, interp_one, interp_two):
    bands = lax.axis_size("band")
    band = lax.axis_index("band")
    chip = lax.axis_index("comp_0")
    core = lax.axis_index("comp_1")
    here = jnp.stack([chip, core]).astype(jnp.int32)
    e = jnp.transpose(energy, (1, 0, 2))
    shape = jax.ShapeDtypeStruct

    own, a, b = call(
        halo_kernel,
        (
            shape((ROWS, PAD, NLON), F32),
            shape((ROWS, 96, NLON), I16),
            shape((ROWS, 80, NLON), I16),
        ),
        (here, e, land_sea),
        [((96, NLON), F32)],
        8,
    )
    up, down = ([], [])
    for i in range(bands):
        for g in range(4):
            for side in range(2):
                j = i * 8 + g * 2 + side
                for way, step in ((up, 1 - 2 * side), (down, 2 * side - 1)):
                    if 0 <= i + step < bands:
                        way.append((j, j + 8 * step))
    a = lax.ppermute(a, EVERY, up)
    b = lax.ppermute(b, EVERY, down)

    geo = geometry(group_speed, band * ROWS, bands * ROWS)
    geo_here = lax.dynamic_slice_in_dim(geo, (chip * 2 + core) * LOCAL, LOCAL, 0)
    local_a = (np.arange(LOCAL) // HALF % 2 == 0).astype(np.float32)
    geo_here = jnp.concatenate([geo_here[:, :9], jnp.asarray(local_a)[:, None], geo_here[:, 10:]], axis=1)
    geo_here = jnp.pad(geo_here, ((0, PAD - LOCAL), (0, 0)))
    geo_sides = geo.reshape(NFREQ, 2, HALF, 16).transpose(1, 0, 2, 3).reshape(2, K // 2, 16)

    packed = call(
        first_kernel,
        [shape((PAD, 256), I16)] * 8,
        (here, own, a, b, geo_here),
        [
            ((ROWS, PAD, NLON), F32),
            ((8, PAD, 256), F32),
            ((8, TRIP1, 256), F32),
        ],
        10,
        us=6,
    )
    nothing = jnp.minimum(packed[0][LOCAL, 0], 0).astype(jnp.bfloat16)
    weights = (interp_one + nothing, interp_two + nothing)
    packed = exchanged(packed)

    half = K // 2
    matmul_scratch = [((K, 256), jnp.bfloat16)] * 3
    own, north, south = call(
        second_kernel,
        (shape((2, half + 8, 256), F32), shape((SEND, 256), I16), shape((SEND, 256), I16)),
        (here, *packed),
        [((K, 256), F32), ((8, PAD, 256), F32)] + matmul_scratch + [((SEND, 256), F32)],
        14,
        weights,
        8,
    )
    nothing = jnp.minimum(own[0, half, 0], 0).astype(jnp.bfloat16)
    weights = (interp_one + nothing, interp_two + nothing)
    north = lax.ppermute(north, "band", [(i, i + 1) for i in range(bands - 1)])
    south = lax.ppermute(south, "band", [(i + 1, i) for i in range(bands - 1)])

    final = call(
        third_kernel,
        [shape((256, 128), I16)] * 8,
        (here, own, north, south, geo_sides),
        [((K, 256), F32), ((2, half, 256), F32), ((8, PAD, 256), F32)]
        + matmul_scratch
        + [((SEND, 256), F32), ((LEVELS, 8, 128), F32)],
        16,
        weights,
        16,
    )
    final = exchanged(final)
    out = call(
        last_kernel,
        shape((ROWS, LOCAL, NLON), F32),
        (here, *final),
        [((8, 256, 128), F32), ((256, 128), F32)],
        8,
    )
    return jnp.transpose(out, (1, 0, 2))


def solution(mesh):
    finer = Mesh(mesh.devices.reshape(mesh.shape["band"], 4, 2), EVERY)
    return jax.shard_map(
        body,
        mesh=finer,
        in_specs=(P(COMP, "band", None), P("band", None), P(), P(), P()),
        out_specs=P(COMP, "band", None),
        check_vma=False,
    )
```

```python
import functools
import math

import jax
import jax.numpy as jnp
import numpy as np
from jax import lax
from jax.experimental import pallas as pl
from jax.experimental.pallas import tpu as pltpu
from jax.sharding import Mesh
from jax.sharding import PartitionSpec as P

NDIR = 36
NFREQ = 36
K = NDIR * NFREQ
ROWS = 3
NLON = 512
HALF = NDIR // 2
LOCAL = 162
PAD = 168
SOURCE_RATE = 0.05
COMP = ("comp_0", "comp_1")
EVERY = ("band", "comp_0", "comp_1")
LEVELS = 2 * ROWS
HOPS = ((0, 0), (1, 0), (3, 0), (2, 0), (2, 1), (1, 1), (3, 1), (0, 1))
WIRE = 280
GROUP = 24
TRIP1 = 56
TRIP3 = 216
TOP = 32767.0
F32 = jnp.float32
I16 = jnp.int16


def code_of(largest):
    return jnp.ceil(jnp.log2(jnp.maximum(largest, 1e-30)) * 128.0)


def to_wire(code):
    return jnp.exp2(code * (-1.0 / 128.0)) * TOP


def from_wire(code):
    return jnp.exp2(code * (1.0 / 128.0)) * (1.0 / TOP)


def to_code(values):
    code = code_of(jnp.max(jnp.abs(values), axis=0, keepdims=True))
    return values * to_wire(code), code


def rounded(values):
    return jnp.floor(values + 0.5).astype(jnp.int32).astype(I16)


def iota(shape, dim):
    return lax.broadcasted_iota(jnp.int32, shape, dim)


def halo_kernel(where_ref, e_ref, sea_ref, own, a_ref, b_ref, scr):
    core = where_ref[1]
    sea = [sea_ref[r : r + 1, :].astype(F32) for r in range(ROWS)]
    for row in range(ROWS):
        own[row, 0:LOCAL, :] = e_ref[row] * sea[row]
        own[row, LOCAL:PAD, :] = jnp.broadcast_to(sea[row], (PAD - LOCAL, NLON))
    for level in range(ROWS):
        row_a = level + core * (2 - 2 * level)
        for row, groups, out in (
            (row_a, (0, 2, 4, 6, 8), a_ref),
            (2 - row_a, (1, 3, 5, 7), b_ref),
        ):
            n = HALF * len(groups)
            total = out.shape[1]
            for i, g in enumerate(groups):
                scr[HALF * i : HALF * i + HALF, :] = own[row, HALF * g : HALF * g + HALF, :]
            scr[n:total, :] = jnp.zeros((total - n, NLON), F32)
            x = scr[0:total, :]
            code = code_of(jnp.max(jnp.abs(x), axis=0, keepdims=True))
            at = iota((total, NLON), 0)
            q = jnp.where(at == n, own[row, LOCAL : LOCAL + 1, :], x * to_wire(code))
            q = jnp.where(at == n + 1, code, q)
            out[level] = rounded(q)


def one_substep(level, here, upstream, east, cx, cy, sea, width):
    shifted = jnp.where(east, pltpu.roll(here, 1, 1), pltpu.roll(here, width - 1, 1))
    return (here - cx[level] * (here - shifted) - cy * (here - upstream)) * sea


def advected(levels, east, cx, cy, sea, width):
    for substep in range(ROWS):
        levels = [
            one_substep(i, levels[i], levels[i - 1], east, cx, cy, sea[i], width)
            if i > substep
            else levels[i]
            for i in range(LEVELS)
        ]
    return levels[ROWS:]


def first_kernel(where_ref, own, a_ref, b_ref, geo_ref, *rest):
    outs, (halo, wide, packed) = rest[:8], rest[8:]
    chip, core = where_ref[0], where_ref[1]
    masks = {}
    for name, ref, groups in (("a", a_ref, (0, 2, 4, 6, 8)), ("b", b_ref, (1, 3, 5, 7))):
        n = HALF * len(groups)
        total = ref.shape[1]
        for level in range(ROWS):
            wide[0, 0:total, :] = ref[level, :, 0:256].astype(F32)
            wide[1, 0:total, :] = ref[level, :, 256:512].astype(F32)
            for side in range(2):
                lanes = slice(256 * side, 256 * side + 256)
                scale = from_wire(wide[side, n + 1 : n + 2, :])
                masks[name, level, side] = wide[side, n : n + 1, :]
                for i, g in enumerate(groups):
                    halo[level, HALF * g : HALF * g + HALF, lanes] = (
                        wide[side, HALF * i : HALF * i + HALF, :] * scale
                    )
    for level in range(ROWS):
        halo[level, LOCAL:PAD, :] = jnp.zeros((PAD - LOCAL, NLON), F32)
    mask_a = [jnp.concatenate([masks["a", r, 0], masks["a", r, 1]], axis=1) for r in range(ROWS)]
    mask_b = [jnp.concatenate([masks["b", r, 0], masks["b", r, 1]], axis=1) for r in range(ROWS)]
    sea_rows = [own[r, LOCAL : LOCAL + 1, :] for r in range(ROWS)]
    lane = iota((TRIP1, 128), 1)

    @pl.loop(0, PAD // TRIP1)
    def _(block):
        rows = pl.ds(pl.multiple_of(block * TRIP1, 8), TRIP1)
        geo = geo_ref[rows, :]

        def column(i, width):
            return jnp.broadcast_to(geo[:, i : i + 1], (TRIP1, width))

        cx = [column(i, NLON) for i in range(LEVELS)]
        cy = column(6, NLON)
        east = column(7, NLON) > 0.5
        north = column(8, NLON) > 0.5
        is_a = column(9, NLON) > 0.5
        e = [own[r, rows, :] for r in range(ROWS)]
        levels = [halo[r, rows, :] for r in range(ROWS)] + [
            jnp.where(north, e[0], e[2]),
            e[1],
            jnp.where(north, e[2], e[0]),
        ]
        sea = [jnp.where(is_a, mask_a[r], mask_b[r]) for r in range(ROWS)] + [
            jnp.where(north, sea_rows[0], sea_rows[2]),
            jnp.broadcast_to(sea_rows[1], (TRIP1, NLON)),
            jnp.where(north, sea_rows[2], sea_rows[0]),
        ]
        down = advected(levels, east, cx, cy, sea, NLON)
        new = [jnp.where(north, down[0], down[2]), down[1], jnp.where(north, down[2], down[0])]
        at = iota((TRIP1, NLON), 0) + block * TRIP1
        new = [jnp.where(at == LOCAL, sea_rows[r], new[r]) for r in range(ROWS)]
        tiles = [[new[r][:, 128 * t : 128 * t + 128] for t in range(4)] for r in range(ROWS)]
        turned = [[pltpu.roll(tiles[r][t], 64, 1) for t in range(4)] for r in range(ROWS)]
        for p in range(8):
            t = p // 2
            if p % 2 == 0:
                f = [jnp.where(lane < 96, tiles[r][t], tiles[r][(t + 3) % 4]) for r in range(ROWS)]
            else:
                f = [
                    jnp.where((lane >= 64) & (lane < 96), turned[r][(t + 1) % 4], turned[r][t])
                    for r in range(ROWS)
                ]
            low = jnp.where(lane < 64, f[0], pltpu.roll(f[1], 64, 1))
            high = f[2]
            high = jnp.where((lane >= 67) & (lane < 70), pltpu.roll(f[0], 3, 1), high)
            high = jnp.where((lane >= 70) & (lane < 73), pltpu.roll(f[1], 6, 1), high)
            high = jnp.where((lane >= 119) & (lane < 122), pltpu.roll(f[1], 122, 1), high)
            high = jnp.where((lane >= 122) & (lane < 125), pltpu.roll(f[0], 125, 1), high)
            wide[p, rows, 0:128] = low
            wide[p, rows, 128:256] = high

    at = iota((PAD, 128), 0)
    for out, (k, t) in zip(outs, HOPS):
        p = ((chip + k) % 4) * 2 + lax.bitwise_xor(core, t)
        low_mask, high_mask = (wide[p, LOCAL : LOCAL + 1, 128 * i : 128 * i + 128] for i in range(2))
        low, high = (jnp.where(at < LOCAL, wide[p, :, 128 * i : 128 * i + 128], 0.0) for i in range(2))
        q, code = to_code(low)
        paired = jnp.where(iota((88, 128), 1) < 64, high[0:88], pltpu.roll(high[80:168], 64, 1))
        q_pair, code_pair = to_code(paired)
        sides = jnp.where(iota((PAD, 128), 1) < 9, pltpu.roll(high, 64, 1), pltpu.roll(high, 18, 1))
        side_lane = iota((GROUP, 128), 1)
        side = jnp.zeros((GROUP, 128), F32)
        for g in range(7):
            part = sides[GROUP * g : GROUP * g + GROUP]
            part = pltpu.roll(part, 18 * g, 1) if g else part
            side = jnp.where((side_lane >= 18 * g) & (side_lane < 18 * g + 18), part, side)
        q_side, code_side = to_code(side)
        for i, row in enumerate((low_mask, code, code_side, high_mask)):
            q = jnp.where(at == LOCAL + i, row, q)
        packed[0:PAD, :] = q
        packed[PAD : PAD + 88, :] = jnp.where(iota((88, 128), 0) == 82, code_pair, q_pair)
        packed[PAD + 88 : WIRE, :] = q_side
        out[...] = rounded(packed[...])


CHUNK = 432


def add_sources(state, mask, one, two, xs, h1, h2):
    xs[...] = state[...].astype(jnp.bfloat16)

    @pl.loop(0, K // CHUNK)
    def _(i):
        rows = pl.ds(pl.multiple_of(i * CHUNK, 16), CHUNK)
        u = jnp.dot(one[rows, :], xs[...], preferred_element_type=F32)
        v = jnp.dot(two[rows, :], xs[...], preferred_element_type=F32)
        x = xs[rows, :].astype(F32)
        h1[rows, :] = (x * v * v).astype(jnp.bfloat16)
        h2[rows, :] = (x * u * u).astype(jnp.bfloat16)

    over = (((0,), (0,)), ((), ()))
    for first in range(0, K, 512):
        size = min(512, K - first)
        src = lax.dot_general(one[:, first : first + size], h1[...], over, preferred_element_type=F32)
        src = src - lax.dot_general(two[:, first : first + size], h2[...], over, preferred_element_type=F32)
        rows = slice(first, first + size)
        state[rows, :] = state[rows, :] + (SOURCE_RATE * mask) * src


SEND = 656


def second_kernel(where_ref, *refs):
    ins, (one, two), rest = refs[:8], refs[8:10], refs[10:]
    own, north, south, state, blocks, xs, h1, h2, scr, wire = rest
    lane = iota((GROUP, 128), 1)
    chip, core = where_ref[0], where_ref[1]
    for ref, (k, t) in zip(ins, HOPS):
        s = ((chip + 4 - k) % 4) * 2 + lax.bitwise_xor(core, t)
        wire[...] = ref[...].astype(F32)

        def scale(row):
            return from_wire(wire[row : row + 1, :])

        blocks[s, :, 0:128] = wire[0:PAD, :] * scale(LOCAL + 1)
        paired = wire[PAD : PAD + 88, :] * scale(PAD + 82)
        scr[0:88, 0:128] = paired
        scr[80:168, 0:128] = pltpu.roll(paired, 64, 1)
        side = wire[PAD + 88 : WIRE, :] * scale(LOCAL + 2)
        for g in range(7):
            rows = slice(GROUP * g, GROUP * g + GROUP)
            east = pltpu.roll(side, (64 - 18 * g) % 128, 1)
            west = pltpu.roll(side, (110 - 18 * g) % 128, 1)
            blocks[s, rows, 128:256] = jnp.where(
                lane < 64, scr[rows, 0:128], jnp.where(lane < 96, east, west)
            )
    mask = jnp.concatenate([wire[LOCAL : LOCAL + 1, :], wire[LOCAL + 3 : LOCAL + 4, :]], axis=1)
    for s in range(8):
        state[LOCAL * s : LOCAL * s + LOCAL, :] = blocks[s, 0:LOCAL, :]
    add_sources(state, mask, one, two, xs, h1, h2)
    n = K // 2
    for side, out in enumerate((north, south)):
        for f in range(NFREQ):
            first = NDIR * f + HALF * side
            own[side, HALF * f : HALF * f + HALF, :] = state[first : first + HALF, :]
        x = own[side, 0:n, :]
        code = code_of(jnp.max(jnp.abs(x), axis=0, keepdims=True))
        scr[0:n, :] = x * to_wire(code)
        at = iota((SEND - n, 256), 0)
        scr[n:SEND, :] = jnp.where(at == 0, mask, jnp.where(at == 1, code, 0.0))
        out[...] = rounded(scr[...])
    own[0, n : n + 8, :] = jnp.broadcast_to(mask, (8, 256))
    own[1, n : n + 8, :] = jnp.broadcast_to(mask, (8, 256))


def spread(low, high, lane):
    out = []
    for body, by in ((low, 3), (pltpu.roll(low, 64, 1), 6)):
        side = jnp.where(lane < 96, pltpu.roll(high, 128 - by, 1), pltpu.roll(high, by, 1))
        out.append(jnp.where(lane < 64, body, side))
    return [out[0], out[1], high]


def advect_half(side, own, far_ref, geo_ref, out, scr, seas):
    lane = iota((8, 128), 1)
    lanes = iota((TRIP3, 128), 1)
    n = K // 2
    scr[...] = far_ref[...].astype(F32)
    scale = from_wire(scr[n + 1 : n + 2, :])
    far = jnp.broadcast_to(scr[n : n + 1, :], (8, 256))
    near = own[side, n : n + 8, :]
    order = (0, 1, 2) if side == 0 else (2, 1, 0)
    far, near = (spread(m[:, :128], m[:, 128:], lane) for m in (far, near))
    for i, r in enumerate(order):
        seas[i] = far[r]
        seas[ROWS + i] = near[r]
    scale = jnp.broadcast_to(scale, (TRIP3, 256))

    @pl.loop(0, n // TRIP3)
    def _(block):
        rows = pl.ds(pl.multiple_of(block * TRIP3, 8), TRIP3)
        geo = geo_ref[side, rows, :]

        def column(i):
            return jnp.broadcast_to(geo[:, i : i + 1], (TRIP3, 128))

        cx = [column(i) for i in range(LEVELS)]
        cy = column(6)
        east = column(7) > 0.5
        h = scr[rows, :] * scale
        e = own[side, rows, :]
        h, e = (spread(m[:, :128], m[:, 128:], lanes) for m in (h, e))
        levels = [h[r] for r in order] + [e[r] for r in order]
        sea = [jnp.tile(seas[i], (TRIP3 // 8, 1)) for i in range(LEVELS)]
        down = advected(levels, east, cx, cy, sea, 128)
        new = [down[r] for r in order]
        low = jnp.where(lanes < 64, new[0], pltpu.roll(new[1], 64, 1))
        high = jnp.where(lanes < 64, new[2], 0.0)
        out[rows, :] = jnp.concatenate([low, high], axis=1)


def north_kernel(own, far_ref, geo_ref, out, scr, seas):
    advect_half(0, own, far_ref, geo_ref, out, scr, seas)


def third_kernel(where_ref, own, moved, far_ref, geo_ref, one, two, *rest):
    outs, (state, parts, blocks, xs, h1, h2, scr, seas) = rest[:8], rest[8:]
    chip, core = where_ref[0], where_ref[1]
    n = K // 2
    advect_half(1, own, far_ref, geo_ref, parts, scr, seas)
    for side, ref in enumerate((moved, parts)):
        for f in range(NFREQ):
            first = NDIR * f + HALF * side
            state[first : first + HALF, :] = ref[HALF * f : HALF * f + HALF, :]
    mask = own[0, n : n + 1, :]
    add_sources(state, mask, one, two, xs, h1, h2)
    for s in range(8):
        blocks[s, 0:LOCAL, :] = state[LOCAL * s : LOCAL * s + LOCAL, :]
        blocks[s, LOCAL:PAD, :] = jnp.zeros((PAD - LOCAL, 256), F32)
    for out, (k, t) in zip(outs, HOPS):
        s = ((chip + k) % 4) * 2 + lax.bitwise_xor(core, t)
        x = blocks[s]
        low, high = x[:, :128], x[:, 128:]
        paired = jnp.where(iota((88, 128), 1) < 64, high[0:88], pltpu.roll(high[80:168], 64, 1))
        for part, first, used in ((low, 0, LOCAL), (paired, PAD, 82)):
            size = part.shape[0]
            code = code_of(jnp.max(jnp.abs(part), axis=0, keepdims=True))
            q = jnp.where(iota((size, 128), 0) == used, code, part * to_wire(code))
            scr[first : first + size, 0:128] = q
        out[...] = rounded(scr[0:256, 0:128])


def last_kernel(where_ref, *refs):
    ins, (out, tiles, scr) = refs[:8], refs[8:]
    chip, core = where_ref[0], where_ref[1]
    for ref, (k, t) in zip(ins, HOPS):
        p = ((chip + 4 - k) % 4) * 2 + lax.bitwise_xor(core, t)
        scr[...] = ref[...].astype(F32)
        for first, size, used in ((0, PAD, LOCAL), (PAD, 88, 82)):
            scale = from_wire(scr[first + used : first + used + 1, :])
            tiles[p, first : first + size, :] = scr[first : first + size, :] * scale
    lane = iota((256, 128), 1)
    for t in range(4):
        a, b = tiles[2 * t], tiles[2 * t + 1]
        first = jnp.where(lane < 64, a, pltpu.roll(b, 64, 1))
        second = jnp.where(lane < 64, pltpu.roll(a, 64, 1), b)
        lanes = slice(128 * t, 128 * t + 128)
        out[0, :, lanes] = first[0:LOCAL]
        out[1, :, lanes] = second[0:LOCAL]
        out[2, 0:80, lanes] = first[PAD : PAD + 80]
        out[2, 80:LOCAL, lanes] = second[PAD : PAD + 82]


def call(kernel, out, ins, scratch, limit, weights=(), us=2, scalars=1):
    vmem = pl.BlockSpec(memory_space=pltpu.VMEM)
    smem = pl.BlockSpec(memory_space=pltpu.SMEM)
    return pl.pallas_call(
        kernel,
        out_shape=out,
        in_specs=[smem] * scalars + [vmem] * (len(ins) + len(weights) - scalars),
        out_specs=jax.tree.map(lambda _: vmem, out),
        scratch_shapes=[pltpu.VMEM(s, d) for s, d in scratch],
        compiler_params=pltpu.CompilerParams(vmem_limit_bytes=limit << 20),
        cost_estimate=pl.CostEstimate(flops=0, bytes_accessed=us * 3_500_000, transcendentals=0),
    )(*ins, *weights)


def geometry(group_speed, first_row, total_rows):
    comp = np.arange(K)
    d = comp % NDIR
    theta = 2.0 * math.pi / NDIR * (d + 0.5)
    east = (4 * d + 2 < NDIR) | (4 * d + 2 > 3 * NDIR)
    north = 2 * d + 1 < NDIR
    speed = jnp.broadcast_to(group_speed[:, None], (NFREQ, NDIR)).reshape(K)
    along_x = speed * jnp.asarray(np.abs(np.cos(theta)), F32)
    along_y = speed * jnp.asarray(np.abs(np.sin(theta)), F32)
    step = jnp.arange(LEVELS, dtype=jnp.int32)
    rows = jnp.stack([first_row - ROWS + step, first_row + LEVELS - 1 - step]).astype(F32)
    cosine = jnp.cos(math.pi / 180.0 * (-70.0 + 140.0 * (rows + 0.5) / total_rows))
    across = jnp.where(jnp.asarray(north)[:, None], cosine[0], cosine[1])
    flags = np.stack([east, north, (comp // HALF) % 2 == 0], axis=1).astype(np.float32)
    return jnp.concatenate(
        [along_x[:, None] * across, along_y[:, None], jnp.asarray(flags), jnp.zeros((K, 6), F32)],
        axis=1,
    )


def exchanged(arrays):
    done = [arrays[0]]
    for x, (k, t) in list(zip(arrays, HOPS))[1:]:
        pairs = [
            (chip * 2 + core, ((chip + k) % 4) * 2 + (core ^ t)) for chip in range(4) for core in range(2)
        ]
        done.append(lax.ppermute(x, COMP, pairs))
    return done


def body(energy, land_sea, group_speed, interp_one, interp_two):
    bands = lax.axis_size("band")
    band = lax.axis_index("band")
    chip = lax.axis_index("comp_0")
    core = lax.axis_index("comp_1")
    here = jnp.stack([chip, core]).astype(jnp.int32)
    e = jnp.transpose(energy, (1, 0, 2))
    shape = jax.ShapeDtypeStruct

    own, a, b = call(
        halo_kernel,
        (
            shape((ROWS, PAD, NLON), F32),
            shape((ROWS, 96, NLON), I16),
            shape((ROWS, 80, NLON), I16),
        ),
        (here, e, land_sea),
        [((96, NLON), F32)],
        8,
    )
    up, down = ([], [])
    for i in range(bands):
        for g in range(4):
            for side in range(2):
                j = i * 8 + g * 2 + side
                for way, step in ((up, 1 - 2 * side), (down, 2 * side - 1)):
                    if 0 <= i + step < bands:
                        way.append((j, j + 8 * step))
    a = lax.ppermute(a, EVERY, up)
    b = lax.ppermute(b, EVERY, down)

    geo = geometry(group_speed, band * ROWS, bands * ROWS)
    geo_here = lax.dynamic_slice_in_dim(geo, (chip * 2 + core) * LOCAL, LOCAL, 0)
    local_a = (np.arange(LOCAL) // HALF % 2 == 0).astype(np.float32)
    geo_here = jnp.concatenate([geo_here[:, :9], jnp.asarray(local_a)[:, None], geo_here[:, 10:]], axis=1)
    geo_here = jnp.pad(geo_here, ((0, PAD - LOCAL), (0, 0)))
    geo_sides = geo.reshape(NFREQ, 2, HALF, 16).transpose(1, 0, 2, 3).reshape(2, K // 2, 16)

    packed = call(
        first_kernel,
        [shape((WIRE, 128), I16)] * 8,
        (here, own, a, b, geo_here),
        [
            ((ROWS, PAD, NLON), F32),
            ((8, PAD, 256), F32),
            ((WIRE, 128), F32),
        ],
        10,
        us=6,
    )
    nothing = jnp.minimum(packed[0][LOCAL, 0], 0).astype(jnp.bfloat16)
    weights = (interp_one + nothing, interp_two + nothing)
    packed = exchanged(packed)

    half = K // 2
    matmul_scratch = [((K, 256), jnp.bfloat16)] * 3
    own, north, south = call(
        second_kernel,
        (shape((2, half + 8, 256), F32), shape((SEND, 256), I16), shape((SEND, 256), I16)),
        (here, *packed),
        [((K, 256), F32), ((8, PAD, 256), F32)] + matmul_scratch + [((SEND, 256), F32), ((WIRE, 128), F32)],
        14,
        weights,
        8,
    )
    nothing = jnp.minimum(own[0, half, 0], 0).astype(jnp.bfloat16)
    weights = (interp_one + nothing, interp_two + nothing)
    north = lax.ppermute(north, "band", [(i, i + 1) for i in range(bands - 1)])
    south = lax.ppermute(south, "band", [(i + 1, i) for i in range(bands - 1)])

    advect_scratch = [((SEND, 256), F32), ((LEVELS, 8, 128), F32)]
    moved = call(
        north_kernel,
        shape((half, 256), F32),
        (own, north, geo_sides),
        advect_scratch,
        8,
        us=5,
        scalars=0,
    )
    final = call(
        third_kernel,
        [shape((256, 128), I16)] * 8,
        (here, own, moved, south, geo_sides),
        [((K, 256), F32), ((half, 256), F32), ((8, PAD, 256), F32)]
        + matmul_scratch
        + advect_scratch,
        16,
        weights,
        16,
    )
    final = exchanged(final)
    out = call(
        last_kernel,
        shape((ROWS, LOCAL, NLON), F32),
        (here, *final),
        [((8, 256, 128), F32), ((256, 128), F32)],
        8,
    )
    return jnp.transpose(out, (1, 0, 2))


def solution(mesh):
    finer = Mesh(mesh.devices.reshape(mesh.shape["band"], 4, 2), EVERY)
    return jax.shard_map(
        body,
        mesh=finer,
        in_specs=(P(COMP, "band", None), P("band", None), P(), P(), P()),
        out_specs=P(COMP, "band", None),
        check_vma=False,
    )
```

```python
import functools
import math

import jax
import jax.numpy as jnp
import numpy as np
from jax import lax
from jax.experimental import pallas as pl
from jax.experimental.pallas import tpu as pltpu
from jax.sharding import Mesh
from jax.sharding import PartitionSpec as P

NDIR = 36
NFREQ = 36
K = NDIR * NFREQ
ROWS = 3
NLON = 512
HALF = NDIR // 2
LOCAL = 162
PAD = 168
SOURCE_RATE = 0.05
COMP = ("comp_0", "comp_1")
EVERY = ("band", "comp_0", "comp_1")
LEVELS = 2 * ROWS
HOPS = ((0, 0), (1, 0), (3, 0), (2, 0), (2, 1), (1, 1), (3, 1), (0, 1))
A_RUNS, B_RUNS = (0, 2, 4, 6, 8), (1, 3, 5, 7)
FAR = 96
WIRE = 280
GROUP = 24
TRIP1 = 56
TRIP3 = 216
TOP = 32767.0
F32 = jnp.float32
I16 = jnp.int16


def code_of(largest):
    return jnp.ceil(jnp.log2(jnp.maximum(largest, 1e-30)) * 128.0)


def to_wire(code):
    return jnp.exp2(code * (-1.0 / 128.0)) * TOP


def from_wire(code):
    return jnp.exp2(code * (1.0 / 128.0)) * (1.0 / TOP)


def to_code(values):
    code = code_of(jnp.max(jnp.abs(values), axis=0, keepdims=True))
    return values * to_wire(code), code


def rounded(values):
    return jnp.floor(values + 0.5).astype(jnp.int32).astype(I16)


def iota(shape, dim):
    return lax.broadcasted_iota(jnp.int32, shape, dim)


def halo_kernel(where_ref, e_ref, sea_ref, own, first_ref, second_ref, scr):
    core = where_ref[1]
    sea = [sea_ref[r : r + 1, :].astype(F32) for r in range(ROWS)]
    for row in range(ROWS):
        own[row, 0:LOCAL, :] = e_ref[row] * sea[row]
        own[row, LOCAL:PAD, :] = jnp.broadcast_to(sea[row], (PAD - LOCAL, NLON))
    a_first = core == where_ref[2]
    for level in range(ROWS):
        row_a = level + core * (2 - 2 * level)
        made = []
        for row, groups in ((row_a, A_RUNS), (2 - row_a, B_RUNS)):
            n = HALF * len(groups)
            for i, g in enumerate(groups):
                scr[HALF * i : HALF * i + HALF, :] = own[row, HALF * g : HALF * g + HALF, :]
            scr[n:FAR, :] = jnp.zeros((FAR - n, NLON), F32)
            q, code = to_code(scr[...])
            at = iota((FAR, NLON), 0)
            q = jnp.where(at == FAR - 6, own[row, LOCAL : LOCAL + 1, :], q)
            made.append(jnp.where(at == FAR - 5, code, q))
        first_ref[level] = rounded(jnp.where(a_first, made[0], made[1]))
        second_ref[level] = rounded(jnp.where(a_first, made[1], made[0]))


def one_substep(level, here, upstream, east, cx, cy, sea, width):
    shifted = jnp.where(east, pltpu.roll(here, 1, 1), pltpu.roll(here, width - 1, 1))
    return (here - cx[level] * (here - shifted) - cy * (here - upstream)) * sea


def advected(levels, east, cx, cy, sea, width):
    for substep in range(ROWS):
        levels = [
            one_substep(i, levels[i], levels[i - 1], east, cx, cy, sea[i], width)
            if i > substep
            else levels[i]
            for i in range(LEVELS)
        ]
    return levels[ROWS:]


def first_kernel(where_ref, own, first_ref, second_ref, geo_ref, *rest):
    outs, (halo, wide, packed) = rest[:8], rest[8:]
    chip, core = where_ref[0], where_ref[1]
    a_second = core == where_ref[2]
    masks = {}
    for level in range(ROWS):
        for side in range(2):
            lanes = slice(256 * side, 256 * side + 256)
            came = [ref[level, :, lanes].astype(F32) for ref in (first_ref, second_ref)]
            for name, groups, x in (
                ("a", A_RUNS, jnp.where(a_second, came[1], came[0])),
                ("b", B_RUNS, jnp.where(a_second, came[0], came[1])),
            ):
                wide[0, 0:FAR, :] = x
                scale = from_wire(wide[0, FAR - 5 : FAR - 4, :])
                masks[name, level, side] = wide[0, FAR - 6 : FAR - 5, :]
                for i, g in enumerate(groups):
                    halo[level, HALF * g : HALF * g + HALF, lanes] = (
                        wide[0, HALF * i : HALF * i + HALF, :] * scale
                    )
    for level in range(ROWS):
        halo[level, LOCAL:PAD, :] = jnp.zeros((PAD - LOCAL, NLON), F32)
    mask_a = [jnp.concatenate([masks["a", r, 0], masks["a", r, 1]], axis=1) for r in range(ROWS)]
    mask_b = [jnp.concatenate([masks["b", r, 0], masks["b", r, 1]], axis=1) for r in range(ROWS)]
    sea_rows = [own[r, LOCAL : LOCAL + 1, :] for r in range(ROWS)]
    lane = iota((TRIP1, 128), 1)

    @pl.loop(0, PAD // TRIP1)
    def _(block):
        rows = pl.ds(pl.multiple_of(block * TRIP1, 8), TRIP1)
        geo = geo_ref[rows, :]

        def column(i, width):
            return jnp.broadcast_to(geo[:, i : i + 1], (TRIP1, width))

        cx = [column(i, NLON) for i in range(LEVELS)]
        cy = column(6, NLON)
        east = column(7, NLON) > 0.5
        north = column(8, NLON) > 0.5
        is_a = column(9, NLON) > 0.5
        e = [own[r, rows, :] for r in range(ROWS)]
        levels = [halo[r, rows, :] for r in range(ROWS)] + [
            jnp.where(north, e[0], e[2]),
            e[1],
            jnp.where(north, e[2], e[0]),
        ]
        sea = [jnp.where(is_a, mask_a[r], mask_b[r]) for r in range(ROWS)] + [
            jnp.where(north, sea_rows[0], sea_rows[2]),
            jnp.broadcast_to(sea_rows[1], (TRIP1, NLON)),
            jnp.where(north, sea_rows[2], sea_rows[0]),
        ]
        down = advected(levels, east, cx, cy, sea, NLON)
        new = [jnp.where(north, down[0], down[2]), down[1], jnp.where(north, down[2], down[0])]
        at = iota((TRIP1, NLON), 0) + block * TRIP1
        new = [jnp.where(at == LOCAL, sea_rows[r], new[r]) for r in range(ROWS)]
        tiles = [[new[r][:, 128 * t : 128 * t + 128] for t in range(4)] for r in range(ROWS)]
        turned = [[pltpu.roll(tiles[r][t], 64, 1) for t in range(4)] for r in range(ROWS)]
        for p in range(8):
            t = p // 2
            if p % 2 == 0:
                f = [jnp.where(lane < 96, tiles[r][t], tiles[r][(t + 3) % 4]) for r in range(ROWS)]
            else:
                f = [
                    jnp.where((lane >= 64) & (lane < 96), turned[r][(t + 1) % 4], turned[r][t])
                    for r in range(ROWS)
                ]
            low = jnp.where(lane < 64, f[0], pltpu.roll(f[1], 64, 1))
            high = f[2]
            high = jnp.where((lane >= 67) & (lane < 70), pltpu.roll(f[0], 3, 1), high)
            high = jnp.where((lane >= 70) & (lane < 73), pltpu.roll(f[1], 6, 1), high)
            high = jnp.where((lane >= 119) & (lane < 122), pltpu.roll(f[1], 122, 1), high)
            high = jnp.where((lane >= 122) & (lane < 125), pltpu.roll(f[0], 125, 1), high)
            wide[p, rows, 0:128] = low
            wide[p, rows, 128:256] = high

    at = iota((PAD, 128), 0)
    for out, (k, t) in zip(outs, HOPS):
        p = ((chip + k) % 4) * 2 + lax.bitwise_xor(core, t)
        low_mask, high_mask = (wide[p, LOCAL : LOCAL + 1, 128 * i : 128 * i + 128] for i in range(2))
        low, high = (jnp.where(at < LOCAL, wide[p, :, 128 * i : 128 * i + 128], 0.0) for i in range(2))
        q, code = to_code(low)
        paired = jnp.where(iota((88, 128), 1) < 64, high[0:88], pltpu.roll(high[80:168], 64, 1))
        q_pair, code_pair = to_code(paired)
        sides = jnp.where(iota((PAD, 128), 1) < 9, pltpu.roll(high, 64, 1), pltpu.roll(high, 18, 1))
        side_lane = iota((GROUP, 128), 1)
        side = jnp.zeros((GROUP, 128), F32)
        for g in range(7):
            part = sides[GROUP * g : GROUP * g + GROUP]
            part = pltpu.roll(part, 18 * g, 1) if g else part
            side = jnp.where((side_lane >= 18 * g) & (side_lane < 18 * g + 18), part, side)
        q_side, code_side = to_code(side)
        for i, row in enumerate((low_mask, code, code_side, high_mask)):
            q = jnp.where(at == LOCAL + i, row, q)
        packed[0:PAD, :] = q
        packed[PAD : PAD + 88, :] = jnp.where(iota((88, 128), 0) == 82, code_pair, q_pair)
        packed[PAD + 88 : WIRE, :] = q_side
        out[...] = rounded(packed[...])


CHUNK = 432


def add_sources(state, mask, one, two, xs, h1, h2):
    xs[...] = state[...].astype(jnp.bfloat16)

    @pl.loop(0, K // CHUNK)
    def _(i):
        rows = pl.ds(pl.multiple_of(i * CHUNK, 16), CHUNK)
        u = jnp.dot(one[rows, :], xs[...], preferred_element_type=F32)
        v = jnp.dot(two[rows, :], xs[...], preferred_element_type=F32)
        x = xs[rows, :].astype(F32)
        h1[rows, :] = (x * v * v).astype(jnp.bfloat16)
        h2[rows, :] = (x * u * u).astype(jnp.bfloat16)

    over = (((0,), (0,)), ((), ()))
    for first in range(0, K, 512):
        size = min(512, K - first)
        src = lax.dot_general(one[:, first : first + size], h1[...], over, preferred_element_type=F32)
        src = src - lax.dot_general(two[:, first : first + size], h2[...], over, preferred_element_type=F32)
        rows = slice(first, first + size)
        state[rows, :] = state[rows, :] + (SOURCE_RATE * mask) * src


SEND = 656


def second_kernel(where_ref, *refs):
    ins, (one, two), rest = refs[:8], refs[8:10], refs[10:]
    own, first_ref, second_ref, state, blocks, xs, h1, h2, scr, wire = rest
    lane = iota((GROUP, 128), 1)
    chip, core = where_ref[0], where_ref[1]
    for ref, (k, t) in zip(ins, HOPS):
        s = ((chip + 4 - k) % 4) * 2 + lax.bitwise_xor(core, t)
        wire[...] = ref[...].astype(F32)

        def scale(row):
            return from_wire(wire[row : row + 1, :])

        blocks[s, :, 0:128] = wire[0:PAD, :] * scale(LOCAL + 1)
        paired = wire[PAD : PAD + 88, :] * scale(PAD + 82)
        scr[0:88, 0:128] = paired
        scr[80:168, 0:128] = pltpu.roll(paired, 64, 1)
        side = wire[PAD + 88 : WIRE, :] * scale(LOCAL + 2)
        for g in range(7):
            rows = slice(GROUP * g, GROUP * g + GROUP)
            east = pltpu.roll(side, (64 - 18 * g) % 128, 1)
            west = pltpu.roll(side, (110 - 18 * g) % 128, 1)
            blocks[s, rows, 128:256] = jnp.where(
                lane < 64, scr[rows, 0:128], jnp.where(lane < 96, east, west)
            )
    mask = jnp.concatenate([wire[LOCAL : LOCAL + 1, :], wire[LOCAL + 3 : LOCAL + 4, :]], axis=1)
    for s in range(8):
        state[LOCAL * s : LOCAL * s + LOCAL, :] = blocks[s, 0:LOCAL, :]
    add_sources(state, mask, one, two, xs, h1, h2)
    n = K // 2
    odd = where_ref[2]
    for side in range(2):
        for f in range(NFREQ):
            first = NDIR * f + HALF * side
            own[side, HALF * f : HALF * f + HALF, :] = state[first : first + HALF, :]
    for side, out in ((odd, first_ref), (1 - odd, second_ref)):
        q, code = to_code(own[side, 0:n, :])
        scr[0:n, :] = q
        at = iota((SEND - n, 256), 0)
        scr[n:SEND, :] = jnp.where(at == 0, mask, jnp.where(at == 1, code, 0.0))
        out[...] = rounded(scr[...])
    own[0, n : n + 8, :] = jnp.broadcast_to(mask, (8, 256))
    own[1, n : n + 8, :] = jnp.broadcast_to(mask, (8, 256))


def spread(low, high, lane):
    out = []
    for body, by in ((low, 3), (pltpu.roll(low, 64, 1), 6)):
        side = jnp.where(lane < 96, pltpu.roll(high, 128 - by, 1), pltpu.roll(high, by, 1))
        out.append(jnp.where(lane < 64, body, side))
    return [out[0], out[1], high]


def advect_half(side, own, far_ref, geo_ref, out, scr, seas):
    lane = iota((8, 128), 1)
    lanes = iota((TRIP3, 128), 1)
    n = K // 2
    scr[...] = far_ref[...].astype(F32)
    scale = from_wire(scr[n + 1 : n + 2, :])
    far = jnp.broadcast_to(scr[n : n + 1, :], (8, 256))
    near = own[side, n : n + 8, :]
    south = side == 1

    def ordered(rows):
        return [jnp.where(south, rows[2], rows[0]), rows[1], jnp.where(south, rows[0], rows[2])]

    far, near = (spread(m[:, :128], m[:, 128:], lane) for m in (far, near))
    for i, row in enumerate(ordered(far) + ordered(near)):
        seas[i] = row
    scale = jnp.broadcast_to(scale, (TRIP3, 256))

    @pl.loop(0, n // TRIP3)
    def _(block):
        rows = pl.ds(pl.multiple_of(block * TRIP3, 8), TRIP3)
        geo = geo_ref[side, rows, :]

        def column(i):
            return jnp.broadcast_to(geo[:, i : i + 1], (TRIP3, 128))

        cx = [column(i) for i in range(LEVELS)]
        cy = column(6)
        east = column(7) > 0.5
        h = scr[rows, :] * scale
        e = own[side, rows, :]
        h, e = (spread(m[:, :128], m[:, 128:], lanes) for m in (h, e))
        levels = ordered(h) + ordered(e)
        sea = [jnp.tile(seas[i], (TRIP3 // 8, 1)) for i in range(LEVELS)]
        down = advected(levels, east, cx, cy, sea, 128)
        new = ordered(down)
        low = jnp.where(lanes < 64, new[0], pltpu.roll(new[1], 64, 1))
        high = jnp.where(lanes < 64, new[2], 0.0)
        out[rows, :] = jnp.concatenate([low, high], axis=1)


def half_kernel(where_ref, own, far_ref, geo_ref, out, scr, seas):
    advect_half(1 - where_ref[2], own, far_ref, geo_ref, out, scr, seas)


def third_kernel(where_ref, own, moved, far_ref, geo_ref, one, two, *rest):
    outs, (state, parts, blocks, xs, h1, h2, scr, seas) = rest[:8], rest[8:]
    chip, core = where_ref[0], where_ref[1]
    n = K // 2
    odd = where_ref[2]
    parts[1 - odd] = moved[...]
    advect_half(odd, own, far_ref, geo_ref, parts.at[odd], scr, seas)
    for side in range(2):
        for f in range(NFREQ):
            first = NDIR * f + HALF * side
            state[first : first + HALF, :] = parts[side, HALF * f : HALF * f + HALF, :]
    mask = own[0, n : n + 1, :]
    add_sources(state, mask, one, two, xs, h1, h2)
    for s in range(8):
        blocks[s, 0:LOCAL, :] = state[LOCAL * s : LOCAL * s + LOCAL, :]
        blocks[s, LOCAL:PAD, :] = jnp.zeros((PAD - LOCAL, 256), F32)
    for out, (k, t) in zip(outs, HOPS):
        s = ((chip + k) % 4) * 2 + lax.bitwise_xor(core, t)
        x = blocks[s]
        low, high = x[:, :128], x[:, 128:]
        paired = jnp.where(iota((88, 128), 1) < 64, high[0:88], pltpu.roll(high[80:168], 64, 1))
        for part, first, used in ((low, 0, LOCAL), (paired, PAD, 82)):
            size = part.shape[0]
            code = code_of(jnp.max(jnp.abs(part), axis=0, keepdims=True))
            q = jnp.where(iota((size, 128), 0) == used, code, part * to_wire(code))
            scr[first : first + size, 0:128] = q
        out[...] = rounded(scr[0:256, 0:128])


def last_kernel(where_ref, *refs):
    ins, (out, tiles, scr) = refs[:8], refs[8:]
    chip, core = where_ref[0], where_ref[1]
    for ref, (k, t) in zip(ins, HOPS):
        p = ((chip + 4 - k) % 4) * 2 + lax.bitwise_xor(core, t)
        scr[...] = ref[...].astype(F32)
        for first, size, used in ((0, PAD, LOCAL), (PAD, 88, 82)):
            scale = from_wire(scr[first + used : first + used + 1, :])
            tiles[p, first : first + size, :] = scr[first : first + size, :] * scale
    lane = iota((256, 128), 1)
    for t in range(4):
        a, b = tiles[2 * t], tiles[2 * t + 1]
        first = jnp.where(lane < 64, a, pltpu.roll(b, 64, 1))
        second = jnp.where(lane < 64, pltpu.roll(a, 64, 1), b)
        lanes = slice(128 * t, 128 * t + 128)
        out[0, :, lanes] = first[0:LOCAL]
        out[1, :, lanes] = second[0:LOCAL]
        out[2, 0:80, lanes] = first[PAD : PAD + 80]
        out[2, 80:LOCAL, lanes] = second[PAD : PAD + 82]


def call(kernel, out, ins, scratch, limit, weights=(), us=2):
    vmem = pl.BlockSpec(memory_space=pltpu.VMEM)
    smem = pl.BlockSpec(memory_space=pltpu.SMEM)
    return pl.pallas_call(
        kernel,
        out_shape=out,
        in_specs=[smem] + [vmem] * (len(ins) + len(weights) - 1),
        out_specs=jax.tree.map(lambda _: vmem, out),
        scratch_shapes=[pltpu.VMEM(s, d) for s, d in scratch],
        compiler_params=pltpu.CompilerParams(vmem_limit_bytes=limit << 20),
        cost_estimate=pl.CostEstimate(flops=0, bytes_accessed=us * 3_500_000, transcendentals=0),
    )(*ins, *weights)


def geometry(group_speed, first_row, total_rows):
    comp = np.arange(K)
    d = comp % NDIR
    theta = 2.0 * math.pi / NDIR * (d + 0.5)
    east = (4 * d + 2 < NDIR) | (4 * d + 2 > 3 * NDIR)
    north = 2 * d + 1 < NDIR
    speed = jnp.broadcast_to(group_speed[:, None], (NFREQ, NDIR)).reshape(K)
    along_x = speed * jnp.asarray(np.abs(np.cos(theta)), F32)
    along_y = speed * jnp.asarray(np.abs(np.sin(theta)), F32)
    step = jnp.arange(LEVELS, dtype=jnp.int32)
    rows = jnp.stack([first_row - ROWS + step, first_row + LEVELS - 1 - step]).astype(F32)
    cosine = jnp.cos(math.pi / 180.0 * (-70.0 + 140.0 * (rows + 0.5) / total_rows))
    across = jnp.where(jnp.asarray(north)[:, None], cosine[0], cosine[1])
    flags = np.stack([east, north, (comp // HALF) % 2 == 0], axis=1).astype(np.float32)
    return jnp.concatenate(
        [along_x[:, None] * across, along_y[:, None], jnp.asarray(flags), jnp.zeros((K, 6), F32)],
        axis=1,
    )


def exchanged(arrays):
    done = [arrays[0]]
    for x, (k, t) in list(zip(arrays, HOPS))[1:]:
        pairs = [
            (chip * 2 + core, ((chip + k) % 4) * 2 + (core ^ t)) for chip in range(4) for core in range(2)
        ]
        done.append(lax.ppermute(x, COMP, pairs))
    return done


def body(energy, land_sea, group_speed, interp_one, interp_two):
    bands = lax.axis_size("band")
    band = lax.axis_index("band")
    chip = lax.axis_index("comp_0")
    core = lax.axis_index("comp_1")
    here = jnp.stack([chip, core, band % 2]).astype(jnp.int32)
    e = jnp.transpose(energy, (1, 0, 2))
    shape = jax.ShapeDtypeStruct

    own, first, second = call(
        halo_kernel,
        (
            shape((ROWS, PAD, NLON), F32),
            shape((ROWS, FAR, NLON), I16),
            shape((ROWS, FAR, NLON), I16),
        ),
        (here, e, land_sea),
        [((FAR, NLON), F32)],
        8,
    )
    pairs = [
        [(i + j, i + 1 - j) for i in range(start, bands - 1, 2) for j in range(2)] for start in range(2)
    ]
    first = lax.ppermute(first, "band", pairs[0])
    second = lax.ppermute(second, "band", pairs[1])

    geo = geometry(group_speed, band * ROWS, bands * ROWS)
    geo_sides = geo.reshape(NFREQ, 2, HALF, 16).transpose(1, 0, 2, 3).reshape(2, K // 2, 16)
    geo_here = lax.dynamic_slice_in_dim(geo, (chip * 2 + core) * LOCAL, LOCAL, 0)
    local_a = (np.arange(LOCAL) // HALF % 2 == 0).astype(np.float32)
    geo_here = jnp.concatenate([geo_here[:, :9], jnp.asarray(local_a)[:, None], geo_here[:, 10:]], axis=1)
    geo_here = jnp.pad(geo_here, ((0, PAD - LOCAL), (0, 0)))

    packed = call(
        first_kernel,
        [shape((WIRE, 128), I16)] * 8,
        (here, own, first, second, geo_here),
        [
            ((ROWS, PAD, NLON), F32),
            ((8, PAD, 256), F32),
            ((WIRE, 128), F32),
        ],
        10,
        us=6,
    )
    nothing = jnp.minimum(packed[0][LOCAL, 0], 0).astype(jnp.bfloat16)
    weights = (interp_one + nothing, interp_two + nothing)
    packed = exchanged(packed)

    half = K // 2
    matmul_scratch = [((K, 256), jnp.bfloat16)] * 3
    own, first, second = call(
        second_kernel,
        (shape((2, half + 8, 256), F32), shape((SEND, 256), I16), shape((SEND, 256), I16)),
        (here, *packed),
        [((K, 256), F32), ((8, PAD, 256), F32)] + matmul_scratch + [((SEND, 256), F32), ((WIRE, 128), F32)],
        14,
        weights,
        8,
    )
    nothing = jnp.minimum(own[0, half, 0], 0).astype(jnp.bfloat16)
    weights = (interp_one + nothing, interp_two + nothing)
    first = lax.ppermute(first, "band", pairs[0])
    second = lax.ppermute(second, "band", pairs[1])

    advect_scratch = [((SEND, 256), F32), ((LEVELS, 8, 128), F32)]
    moved = call(
        half_kernel,
        shape((half, 256), F32),
        (here, own, first, geo_sides),
        advect_scratch,
        8,
        us=5,
    )
    final = call(
        third_kernel,
        [shape((256, 128), I16)] * 8,
        (here, own, moved, second, geo_sides),
        [((K, 256), F32), ((2, half, 256), F32), ((8, PAD, 256), F32)]
        + matmul_scratch
        + advect_scratch,
        16,
        weights,
        16,
    )
    final = exchanged(final)
    out = call(
        last_kernel,
        shape((ROWS, LOCAL, NLON), F32),
        (here, *final),
        [((8, 256, 128), F32), ((256, 128), F32)],
        8,
    )
    return jnp.transpose(out, (1, 0, 2))


def solution(mesh):
    finer = Mesh(mesh.devices.reshape(mesh.shape["band"], 4, 2), EVERY)
    return jax.shard_map(
        body,
        mesh=finer,
        in_specs=(P(COMP, "band", None), P("band", None), P(), P(), P()),
        out_specs=P(COMP, "band", None),
        check_vma=False,
    )
```

```python
import math

import jax
import jax.numpy as jnp
import numpy as np
from jax import lax
from jax.experimental import pallas as pl
from jax.experimental.pallas import tpu as pltpu
from jax.sharding import Mesh
from jax.sharding import PartitionSpec as P

NDIR = 36
NFREQ = 36
K = NDIR * NFREQ
ROWS = 3
NLON = 512
HALF = NDIR // 2
LOCAL = 162
PAD = 168
SOURCE_RATE = 0.05
COMP = ("comp_0", "comp_1")
EVERY = ("band", "comp_0", "comp_1")
LEVELS = 2 * ROWS
HOPS = ((0, 0), (1, 0), (3, 0), (2, 0), (2, 1), (1, 1), (3, 1), (0, 1))
A_RUNS, B_RUNS = (0, 2, 4, 6, 8), (1, 3, 5, 7)
FAR = 96
WIRE = 280
GROUP = 24
TRIP1 = 56
TRIP3 = 216
TOP = 32767.0
F32 = jnp.float32
I16 = jnp.int16


def code_of(largest):
    return jnp.ceil(jnp.log2(jnp.maximum(largest, 1e-30)) * 128.0)


def to_wire(code):
    return jnp.exp2(code * (-1.0 / 128.0)) * TOP


def from_wire(code):
    return jnp.exp2(code * (1.0 / 128.0)) * (1.0 / TOP)


def to_code(values):
    code = code_of(jnp.max(jnp.abs(values), axis=0, keepdims=True))
    return values * to_wire(code), code


def rounded(values):
    return jnp.floor(values + 0.5).astype(jnp.int32).astype(I16)


def iota(shape, dim):
    return lax.broadcasted_iota(jnp.int32, shape, dim)


def halo_kernel(where_ref, e_ref, sea_ref, own, first_ref, second_ref, scr):
    core = where_ref[1]
    sea = [sea_ref[r : r + 1, :].astype(F32) for r in range(ROWS)]
    for row in range(ROWS):
        own[row, 0:LOCAL, :] = e_ref[row] * sea[row]
        own[row, LOCAL:PAD, :] = jnp.broadcast_to(sea[row], (PAD - LOCAL, NLON))
    a_first = core == where_ref[2]
    for level in range(ROWS):
        row_a = level + core * (2 - 2 * level)
        made = []
        for row, groups in ((row_a, A_RUNS), (2 - row_a, B_RUNS)):
            n = HALF * len(groups)
            for i, g in enumerate(groups):
                scr[HALF * i : HALF * i + HALF, :] = own[row, HALF * g : HALF * g + HALF, :]
            scr[n:FAR, :] = jnp.zeros((FAR - n, NLON), F32)
            q, code = to_code(scr[...])
            at = iota((FAR, NLON), 0)
            q = jnp.where(at == FAR - 6, own[row, LOCAL : LOCAL + 1, :], q)
            made.append(jnp.where(at == FAR - 5, code, q))
        first_ref[level] = rounded(jnp.where(a_first, made[0], made[1]))
        second_ref[level] = rounded(jnp.where(a_first, made[1], made[0]))


def one_substep(level, here, upstream, east, cx, cy, sea, width):
    shifted = jnp.where(east, pltpu.roll(here, 1, 1), pltpu.roll(here, width - 1, 1))
    return (here - cx[level] * (here - shifted) - cy * (here - upstream)) * sea


def advected(levels, east, cx, cy, sea, width):
    for substep in range(ROWS):
        levels = [
            one_substep(i, levels[i], levels[i - 1], east, cx, cy, sea[i], width)
            if i > substep
            else levels[i]
            for i in range(LEVELS)
        ]
    return levels[ROWS:]


def first_kernel(where_ref, own, first_ref, second_ref, geo_ref, *rest):
    outs, (halo, wide, packed) = rest[:8], rest[8:]
    chip, core = where_ref[0], where_ref[1]
    a_second = core == where_ref[2]
    masks = {}
    for level in range(ROWS):
        for side in range(2):
            lanes = slice(256 * side, 256 * side + 256)
            came = [ref[level, :, lanes].astype(F32) for ref in (first_ref, second_ref)]
            for name, groups, x in (
                ("a", A_RUNS, jnp.where(a_second, came[1], came[0])),
                ("b", B_RUNS, jnp.where(a_second, came[0], came[1])),
            ):
                wide[0, 0:FAR, :] = x
                scale = from_wire(wide[0, FAR - 5 : FAR - 4, :])
                masks[name, level, side] = wide[0, FAR - 6 : FAR - 5, :]
                for i, g in enumerate(groups):
                    halo[level, HALF * g : HALF * g + HALF, lanes] = (
                        wide[0, HALF * i : HALF * i + HALF, :] * scale
                    )
    for level in range(ROWS):
        halo[level, LOCAL:PAD, :] = jnp.zeros((PAD - LOCAL, NLON), F32)
    mask_a = [jnp.concatenate([masks["a", r, 0], masks["a", r, 1]], axis=1) for r in range(ROWS)]
    mask_b = [jnp.concatenate([masks["b", r, 0], masks["b", r, 1]], axis=1) for r in range(ROWS)]
    sea_rows = [own[r, LOCAL : LOCAL + 1, :] for r in range(ROWS)]
    lane = iota((TRIP1, 128), 1)

    @pl.loop(0, PAD // TRIP1)
    def _(block):
        rows = pl.ds(pl.multiple_of(block * TRIP1, 8), TRIP1)
        geo = geo_ref[rows, :]

        def column(i, width):
            return jnp.broadcast_to(geo[:, i : i + 1], (TRIP1, width))

        cx = [column(i, NLON) for i in range(LEVELS)]
        cy = column(6, NLON)
        east = column(7, NLON) > 0.5
        north = column(8, NLON) > 0.5
        is_a = column(9, NLON) > 0.5
        e = [own[r, rows, :] for r in range(ROWS)]
        levels = [halo[r, rows, :] for r in range(ROWS)] + [
            jnp.where(north, e[0], e[2]),
            e[1],
            jnp.where(north, e[2], e[0]),
        ]
        sea = [jnp.where(is_a, mask_a[r], mask_b[r]) for r in range(ROWS)] + [
            jnp.where(north, sea_rows[0], sea_rows[2]),
            jnp.broadcast_to(sea_rows[1], (TRIP1, NLON)),
            jnp.where(north, sea_rows[2], sea_rows[0]),
        ]
        down = advected(levels, east, cx, cy, sea, NLON)
        new = [jnp.where(north, down[0], down[2]), down[1], jnp.where(north, down[2], down[0])]
        at = iota((TRIP1, NLON), 0) + block * TRIP1
        new = [jnp.where(at == LOCAL, sea_rows[r], new[r]) for r in range(ROWS)]
        tiles = [[new[r][:, 128 * t : 128 * t + 128] for t in range(4)] for r in range(ROWS)]
        turned = [[pltpu.roll(tiles[r][t], 64, 1) for t in range(4)] for r in range(ROWS)]
        for p in range(8):
            t = p // 2
            if p % 2 == 0:
                f = [jnp.where(lane < 96, tiles[r][t], tiles[r][(t + 3) % 4]) for r in range(ROWS)]
            else:
                f = [
                    jnp.where((lane >= 64) & (lane < 96), turned[r][(t + 1) % 4], turned[r][t])
                    for r in range(ROWS)
                ]
            low = jnp.where(lane < 64, f[0], pltpu.roll(f[1], 64, 1))
            high = f[2]
            high = jnp.where((lane >= 67) & (lane < 70), pltpu.roll(f[0], 3, 1), high)
            high = jnp.where((lane >= 70) & (lane < 73), pltpu.roll(f[1], 6, 1), high)
            high = jnp.where((lane >= 119) & (lane < 122), pltpu.roll(f[1], 122, 1), high)
            high = jnp.where((lane >= 122) & (lane < 125), pltpu.roll(f[0], 125, 1), high)
            wide[p, rows, 0:128] = low
            wide[p, rows, 128:256] = high

    at = iota((PAD, 128), 0)
    for out, (k, t) in zip(outs, HOPS):
        p = ((chip + k) % 4) * 2 + lax.bitwise_xor(core, t)
        low_mask, high_mask = (wide[p, LOCAL : LOCAL + 1, 128 * i : 128 * i + 128] for i in range(2))
        low, high = (jnp.where(at < LOCAL, wide[p, :, 128 * i : 128 * i + 128], 0.0) for i in range(2))
        q, code = to_code(low)
        paired = jnp.where(iota((88, 128), 1) < 64, high[0:88], pltpu.roll(high[80:168], 64, 1))
        q_pair, code_pair = to_code(paired)
        sides = jnp.where(iota((PAD, 128), 1) < 9, pltpu.roll(high, 64, 1), pltpu.roll(high, 18, 1))
        side_lane = iota((GROUP, 128), 1)
        side = jnp.zeros((GROUP, 128), F32)
        for g in range(7):
            part = sides[GROUP * g : GROUP * g + GROUP]
            part = pltpu.roll(part, 18 * g, 1) if g else part
            side = jnp.where((side_lane >= 18 * g) & (side_lane < 18 * g + 18), part, side)
        q_side, code_side = to_code(side)
        for i, row in enumerate((low_mask, code, code_side, high_mask)):
            q = jnp.where(at == LOCAL + i, row, q)
        packed[0:PAD, :] = q
        packed[PAD : PAD + 88, :] = jnp.where(iota((88, 128), 0) == 82, code_pair, q_pair)
        packed[PAD + 88 : WIRE, :] = q_side
        out[...] = rounded(packed[...])


CHUNK = 432


def add_sources(state, mask, one, two, xs, h1, h2):
    xs[...] = state[...].astype(jnp.bfloat16)

    @pl.loop(0, K // CHUNK)
    def _(i):
        rows = pl.ds(pl.multiple_of(i * CHUNK, 16), CHUNK)
        u = jnp.dot(one[rows, :], xs[...], preferred_element_type=F32)
        v = jnp.dot(two[rows, :], xs[...], preferred_element_type=F32)
        x = xs[rows, :].astype(F32)
        h1[rows, :] = (x * v * v).astype(jnp.bfloat16)
        h2[rows, :] = (x * u * u).astype(jnp.bfloat16)

    over = (((0,), (0,)), ((), ()))
    for first in range(0, K, 512):
        size = min(512, K - first)
        src = lax.dot_general(one[:, first : first + size], h1[...], over, preferred_element_type=F32)
        src = src - lax.dot_general(two[:, first : first + size], h2[...], over, preferred_element_type=F32)
        rows = slice(first, first + size)
        state[rows, :] = state[rows, :] + (SOURCE_RATE * mask) * src


SEND = 656


def second_kernel(where_ref, *refs):
    ins, (one, two), rest = refs[:8], refs[8:10], refs[10:]
    own, first_ref, second_ref, state, blocks, xs, h1, h2, scr, wire = rest
    lane = iota((GROUP, 128), 1)
    chip, core = where_ref[0], where_ref[1]
    for ref, (k, t) in zip(ins, HOPS):
        s = ((chip + 4 - k) % 4) * 2 + lax.bitwise_xor(core, t)
        wire[...] = ref[...].astype(F32)

        def scale(row):
            return from_wire(wire[row : row + 1, :])

        blocks[s, :, 0:128] = wire[0:PAD, :] * scale(LOCAL + 1)
        paired = wire[PAD : PAD + 88, :] * scale(PAD + 82)
        scr[0:88, 0:128] = paired
        scr[80:168, 0:128] = pltpu.roll(paired, 64, 1)
        side = wire[PAD + 88 : WIRE, :] * scale(LOCAL + 2)
        for g in range(7):
            rows = slice(GROUP * g, GROUP * g + GROUP)
            east = pltpu.roll(side, (64 - 18 * g) % 128, 1)
            west = pltpu.roll(side, (110 - 18 * g) % 128, 1)
            blocks[s, rows, 128:256] = jnp.where(
                lane < 64, scr[rows, 0:128], jnp.where(lane < 96, east, west)
            )
    mask = jnp.concatenate([wire[LOCAL : LOCAL + 1, :], wire[LOCAL + 3 : LOCAL + 4, :]], axis=1)
    for s in range(8):
        state[LOCAL * s : LOCAL * s + LOCAL, :] = blocks[s, 0:LOCAL, :]
    add_sources(state, mask, one, two, xs, h1, h2)
    n = K // 2
    odd = where_ref[2]
    for side in range(2):
        for f in range(NFREQ):
            first = NDIR * f + HALF * side
            own[side, HALF * f : HALF * f + HALF, :] = state[first : first + HALF, :]
    for side, out in ((odd, first_ref), (1 - odd, second_ref)):
        q, code = to_code(own[side, 0:n, :])
        scr[0:n, :] = q
        at = iota((SEND - n, 256), 0)
        scr[n:SEND, :] = jnp.where(at == 0, mask, jnp.where(at == 1, code, 0.0))
        out[...] = rounded(scr[...])
    own[0, n : n + 8, :] = jnp.broadcast_to(mask, (8, 256))
    own[1, n : n + 8, :] = jnp.broadcast_to(mask, (8, 256))


def spread(low, high, lane):
    out = []
    for body, by in ((low, 3), (pltpu.roll(low, 64, 1), 6)):
        side = jnp.where(lane < 96, pltpu.roll(high, 128 - by, 1), pltpu.roll(high, by, 1))
        out.append(jnp.where(lane < 64, body, side))
    return [out[0], out[1], high]


def advect_half(side, own, far_ref, geo_ref, out, scr, seas):
    lane = iota((8, 128), 1)
    lanes = iota((TRIP3, 128), 1)
    n = K // 2
    scr[...] = far_ref[...].astype(F32)
    scale = from_wire(scr[n + 1 : n + 2, :])
    far = jnp.broadcast_to(scr[n : n + 1, :], (8, 256))
    near = own[side, n : n + 8, :]
    south = side == 1

    def ordered(rows):
        return [jnp.where(south, rows[2], rows[0]), rows[1], jnp.where(south, rows[0], rows[2])]

    far, near = (spread(m[:, :128], m[:, 128:], lane) for m in (far, near))
    for i, row in enumerate(ordered(far) + ordered(near)):
        seas[i] = row
    scale = jnp.broadcast_to(scale, (TRIP3, 256))

    @pl.loop(0, n // TRIP3)
    def _(block):
        rows = pl.ds(pl.multiple_of(block * TRIP3, 8), TRIP3)
        geo = geo_ref[side, rows, :]

        def column(i):
            return jnp.broadcast_to(geo[:, i : i + 1], (TRIP3, 128))

        cx = [column(i) for i in range(LEVELS)]
        cy = column(6)
        east = column(7) > 0.5
        h = scr[rows, :] * scale
        e = own[side, rows, :]
        h, e = (spread(m[:, :128], m[:, 128:], lanes) for m in (h, e))
        levels = ordered(h) + ordered(e)
        sea = [jnp.tile(seas[i], (TRIP3 // 8, 1)) for i in range(LEVELS)]
        down = advected(levels, east, cx, cy, sea, 128)
        new = ordered(down)
        low = jnp.where(lanes < 64, new[0], pltpu.roll(new[1], 64, 1))
        high = jnp.where(lanes < 64, new[2], 0.0)
        out[rows, :] = jnp.concatenate([low, high], axis=1)


def half_kernel(where_ref, own, far_ref, geo_ref, out, scr, seas):
    advect_half(1 - where_ref[2], own, far_ref, geo_ref, out, scr, seas)


def third_kernel(where_ref, own, moved, far_ref, geo_ref, one, two, *rest):
    outs, (state, parts, blocks, xs, h1, h2, scr, seas) = rest[:8], rest[8:]
    chip, core = where_ref[0], where_ref[1]
    n = K // 2
    odd = where_ref[2]
    parts[1 - odd] = moved[...]
    advect_half(odd, own, far_ref, geo_ref, parts.at[odd], scr, seas)
    for side in range(2):
        for f in range(NFREQ):
            first = NDIR * f + HALF * side
            state[first : first + HALF, :] = parts[side, HALF * f : HALF * f + HALF, :]
    mask = own[0, n : n + 1, :]
    add_sources(state, mask, one, two, xs, h1, h2)
    for s in range(8):
        blocks[s, 0:LOCAL, :] = state[LOCAL * s : LOCAL * s + LOCAL, :]
        blocks[s, LOCAL:PAD, :] = jnp.zeros((PAD - LOCAL, 256), F32)
    for out, (k, t) in zip(outs, HOPS):
        s = ((chip + k) % 4) * 2 + lax.bitwise_xor(core, t)
        x = blocks[s]
        low, high = x[:, :128], x[:, 128:]
        paired = jnp.where(iota((88, 128), 1) < 64, high[0:88], pltpu.roll(high[80:168], 64, 1))
        for part, first, used in ((low, 0, LOCAL), (paired, PAD, 82)):
            size = part.shape[0]
            code = code_of(jnp.max(jnp.abs(part), axis=0, keepdims=True))
            q = jnp.where(iota((size, 128), 0) == used, code, part * to_wire(code))
            scr[first : first + size, 0:128] = q
        out[...] = rounded(scr[0:256, 0:128])


def last_kernel(where_ref, *refs):
    ins, (out, tiles, scr) = refs[:8], refs[8:]
    chip, core = where_ref[0], where_ref[1]
    for ref, (k, t) in zip(ins, HOPS):
        p = ((chip + 4 - k) % 4) * 2 + lax.bitwise_xor(core, t)
        scr[...] = ref[...].astype(F32)
        for first, size, used in ((0, PAD, LOCAL), (PAD, 88, 82)):
            scale = from_wire(scr[first + used : first + used + 1, :])
            tiles[p, first : first + size, :] = scr[first : first + size, :] * scale
    lane = iota((256, 128), 1)
    for t in range(4):
        a, b = tiles[2 * t], tiles[2 * t + 1]
        first = jnp.where(lane < 64, a, pltpu.roll(b, 64, 1))
        second = jnp.where(lane < 64, pltpu.roll(a, 64, 1), b)
        lanes = slice(128 * t, 128 * t + 128)
        out[0, :, lanes] = first[0:LOCAL]
        out[1, :, lanes] = second[0:LOCAL]
        out[2, 0:80, lanes] = first[PAD : PAD + 80]
        out[2, 80:LOCAL, lanes] = second[PAD : PAD + 82]


def call(kernel, out, ins, scratch, limit, weights=(), us=2):
    vmem = pl.BlockSpec(memory_space=pltpu.VMEM)
    smem = pl.BlockSpec(memory_space=pltpu.SMEM)
    return pl.pallas_call(
        kernel,
        out_shape=out,
        in_specs=[smem] + [vmem] * (len(ins) + len(weights) - 1),
        out_specs=jax.tree.map(lambda _: vmem, out),
        scratch_shapes=[pltpu.VMEM(s, d) for s, d in scratch],
        compiler_params=pltpu.CompilerParams(vmem_limit_bytes=limit << 20),
        cost_estimate=pl.CostEstimate(flops=0, bytes_accessed=us * 3_500_000, transcendentals=0),
    )(*ins, *weights)


def geometry(group_speed, first_row, total_rows):
    comp = np.arange(K)
    d = comp % NDIR
    theta = 2.0 * math.pi / NDIR * (d + 0.5)
    east = (4 * d + 2 < NDIR) | (4 * d + 2 > 3 * NDIR)
    north = 2 * d + 1 < NDIR
    speed = jnp.broadcast_to(group_speed[:, None], (NFREQ, NDIR)).reshape(K)
    along_x = speed * jnp.asarray(np.abs(np.cos(theta)), F32)
    along_y = speed * jnp.asarray(np.abs(np.sin(theta)), F32)
    step = jnp.arange(LEVELS, dtype=jnp.int32)
    rows = jnp.stack([first_row - ROWS + step, first_row + LEVELS - 1 - step]).astype(F32)
    cosine = jnp.cos(math.pi / 180.0 * (-70.0 + 140.0 * (rows + 0.5) / total_rows))
    across = jnp.where(jnp.asarray(north)[:, None], cosine[0], cosine[1])
    flags = np.stack([east, north, (comp // HALF) % 2 == 0], axis=1).astype(np.float32)
    return jnp.concatenate(
        [along_x[:, None] * across, along_y[:, None], jnp.asarray(flags), jnp.zeros((K, 6), F32)],
        axis=1,
    )


def exchanged(arrays):
    done = [arrays[0]]
    for x, (k, t) in list(zip(arrays, HOPS))[1:]:
        pairs = [
            (chip * 2 + core, ((chip + k) % 4) * 2 + (core ^ t)) for chip in range(4) for core in range(2)
        ]
        done.append(lax.ppermute(x, COMP, pairs))
    return done


def rows_swapped(first, second, pairs):
    second = lax.ppermute(second, "band", pairs[1])
    first = lax.ppermute(first, "band", pairs[0])
    return first, second


def body(energy, land_sea, group_speed, interp_one, interp_two):
    bands = lax.axis_size("band")
    band = lax.axis_index("band")
    chip = lax.axis_index("comp_0")
    core = lax.axis_index("comp_1")
    here = jnp.stack([chip, core, band % 2]).astype(jnp.int32)
    e = jnp.transpose(energy, (1, 0, 2))
    shape = jax.ShapeDtypeStruct

    own, first, second = call(
        halo_kernel,
        (
            shape((ROWS, PAD, NLON), F32),
            shape((ROWS, FAR, NLON), I16),
            shape((ROWS, FAR, NLON), I16),
        ),
        (here, e, land_sea),
        [((FAR, NLON), F32)],
        8,
    )
    pairs = [
        [(i + j, i + 1 - j) for i in range(start, bands - 1, 2) for j in range(2)] for start in range(2)
    ]
    first, second = rows_swapped(first, second, pairs)

    geo = geometry(group_speed, band * ROWS, bands * ROWS)
    geo_sides = geo.reshape(NFREQ, 2, HALF, 16).transpose(1, 0, 2, 3).reshape(2, K // 2, 16)
    geo_here = lax.dynamic_slice_in_dim(geo, (chip * 2 + core) * LOCAL, LOCAL, 0)
    local_a = (np.arange(LOCAL) // HALF % 2 == 0).astype(np.float32)
    geo_here = jnp.concatenate([geo_here[:, :9], jnp.asarray(local_a)[:, None], geo_here[:, 10:]], axis=1)
    geo_here = jnp.pad(geo_here, ((0, PAD - LOCAL), (0, 0)))

    packed = call(
        first_kernel,
        [shape((WIRE, 128), I16)] * 8,
        (here, own, first, second, geo_here),
        [
            ((ROWS, PAD, NLON), F32),
            ((8, PAD, 256), F32),
            ((WIRE, 128), F32),
        ],
        10,
        us=6,
    )
    nothing = jnp.minimum(packed[0][LOCAL, 0], 0).astype(jnp.bfloat16)
    weights = (interp_one + nothing, interp_two + nothing)
    packed = exchanged(packed)

    half = K // 2
    matmul_scratch = [((K, 256), jnp.bfloat16)] * 3
    own, first, second = call(
        second_kernel,
        (shape((2, half + 8, 256), F32), shape((SEND, 256), I16), shape((SEND, 256), I16)),
        (here, *packed),
        [((K, 256), F32), ((8, PAD, 256), F32)] + matmul_scratch + [((SEND, 256), F32), ((WIRE, 128), F32)],
        14,
        weights,
        8,
    )
    nothing = jnp.minimum(own[0, half, 0], 0).astype(jnp.bfloat16)
    weights = (interp_one + nothing, interp_two + nothing)
    first, second = rows_swapped(first, second, pairs)

    advect_scratch = [((SEND, 256), F32), ((LEVELS, 8, 128), F32)]
    moved = call(
        half_kernel,
        shape((half, 256), F32),
        (here, own, first, geo_sides),
        advect_scratch,
        8,
        us=5,
    )
    final = call(
        third_kernel,
        [shape((256, 128), I16)] * 8,
        (here, own, moved, second, geo_sides),
        [((K, 256), F32), ((2, half, 256), F32), ((8, PAD, 256), F32)]
        + matmul_scratch
        + advect_scratch,
        16,
        weights,
        16,
    )
    final = exchanged(final)
    out = call(
        last_kernel,
        shape((ROWS, LOCAL, NLON), F32),
        (here, *final),
        [((8, 256, 128), F32), ((256, 128), F32)],
        8,
    )
    return jnp.transpose(out, (1, 0, 2))


def solution(mesh):
    finer = Mesh(mesh.devices.reshape(mesh.shape["band"], 4, 2), EVERY)
    return jax.shard_map(
        body,
        mesh=finer,
        in_specs=(P(COMP, "band", None), P("band", None), P(), P(), P()),
        out_specs=P(COMP, "band", None),
        check_vma=False,
    )
```

```python
import functools
import math

import jax
import jax.numpy as jnp
import numpy as np
from jax import lax
from jax.experimental import pallas as pl
from jax.experimental.pallas import tpu as pltpu
from jax.sharding import Mesh
from jax.sharding import PartitionSpec as P

NDIR = 36
NFREQ = 36
K = NDIR * NFREQ
ROWS = 3
NLON = 512
HALF = NDIR // 2
LOCAL = 162
PAD = 168
SOURCE_RATE = 0.05
COMP = ("comp_0", "comp_1")
EVERY = ("band", "comp_0", "comp_1")
LEVELS = 2 * ROWS
HOPS = ((0, 0), (1, 0), (3, 0), (2, 0), (2, 1), (1, 1), (3, 1), (0, 1))
A_RUNS, B_RUNS = (0, 2, 4, 6, 8), (1, 3, 5, 7)
FAR = 96
WIRE = 280
GROUP = 24
TRIP1 = 56
TRIP3 = 216
TOP = 32767.0
F32 = jnp.float32
I16 = jnp.int16


def code_of(largest):
    return jnp.ceil(jnp.log2(jnp.maximum(largest, 1e-30)) * 128.0)


def to_wire(code):
    return jnp.exp2(code * (-1.0 / 128.0)) * TOP


def from_wire(code):
    return jnp.exp2(code * (1.0 / 128.0)) * (1.0 / TOP)


def to_code(values):
    code = code_of(jnp.max(jnp.abs(values), axis=0, keepdims=True))
    return values * to_wire(code), code


def rounded(values):
    return jnp.floor(values + 0.5).astype(jnp.int32).astype(I16)


def iota(shape, dim):
    return lax.broadcasted_iota(jnp.int32, shape, dim)


def halo_kernel(where_ref, e_ref, sea_ref, own, first_ref, second_ref, scr):
    core = where_ref[1]
    sea = [sea_ref[r : r + 1, :].astype(F32) for r in range(ROWS)]
    for row in range(ROWS):
        own[row, 0:LOCAL, :] = e_ref[row] * sea[row]
        own[row, LOCAL:PAD, :] = jnp.broadcast_to(sea[row], (PAD - LOCAL, NLON))
    a_first = core == where_ref[2]
    for level in range(ROWS):
        row_a = level + core * (2 - 2 * level)
        made = []
        for row, groups in ((row_a, A_RUNS), (2 - row_a, B_RUNS)):
            n = HALF * len(groups)
            for i, g in enumerate(groups):
                scr[HALF * i : HALF * i + HALF, :] = own[row, HALF * g : HALF * g + HALF, :]
            scr[n:FAR, :] = jnp.zeros((FAR - n, NLON), F32)
            q, code = to_code(scr[...])
            at = iota((FAR, NLON), 0)
            q = jnp.where(at == FAR - 6, own[row, LOCAL : LOCAL + 1, :], q)
            made.append(jnp.where(at == FAR - 5, code, q))
        first_ref[level] = rounded(jnp.where(a_first, made[0], made[1]))
        second_ref[level] = rounded(jnp.where(a_first, made[1], made[0]))


def geometry_kernel(where_ref, speed, after, turn, lat, geo_ref, sides_ref):
    chip, core = where_ref[0], where_ref[1]
    moving = [turn[side] * lat[2 * where_ref[3] + side] for side in range(2)]
    for side in range(2):
        for f in range(NFREQ):
            sides_ref[side, HALF * f : HALF * f + HALF, :] = speed[f] * moving[side] + turn[2 + side]
    for g in range(LOCAL // HALF):
        run = (chip * 2 + core) * (LOCAL // HALF) + g
        side = (core + g) % 2
        columns = speed[run // 2] * jnp.where(side == 0, moving[0], moving[1]) + turn[2 + side]
        if g in A_RUNS:
            columns = columns + jnp.where(iota((HALF, 16), 1) == 9, 1.0, 0.0)
        geo_ref[HALF * g : HALF * g + HALF, :] = columns
    geo_ref[LOCAL:PAD, :] = jnp.zeros((PAD - LOCAL, 16), F32)


def one_substep(level, here, upstream, east, cx, cy, sea, width):
    shifted = jnp.where(east, pltpu.roll(here, 1, 1), pltpu.roll(here, width - 1, 1))
    return (here - cx[level] * (here - shifted) - cy * (here - upstream)) * sea


def advected(levels, east, cx, cy, sea, width):
    for substep in range(ROWS):
        levels = [
            one_substep(i, levels[i], levels[i - 1], east, cx, cy, sea[i], width)
            if i > substep
            else levels[i]
            for i in range(LEVELS)
        ]
    return levels[ROWS:]


def first_kernel(where_ref, own, first_ref, second_ref, geo_ref, *rest):
    outs, (halo, wide, packed) = rest[:8], rest[8:]
    chip, core = where_ref[0], where_ref[1]
    a_second = core == where_ref[2]
    masks = {}
    for level in range(ROWS):
        for side in range(2):
            lanes = slice(256 * side, 256 * side + 256)
            came = [ref[level, :, lanes].astype(F32) for ref in (first_ref, second_ref)]
            for name, groups, x in (
                ("a", A_RUNS, jnp.where(a_second, came[1], came[0])),
                ("b", B_RUNS, jnp.where(a_second, came[0], came[1])),
            ):
                wide[0, 0:FAR, :] = x
                scale = from_wire(wide[0, FAR - 5 : FAR - 4, :])
                masks[name, level, side] = wide[0, FAR - 6 : FAR - 5, :]
                for i, g in enumerate(groups):
                    halo[level, HALF * g : HALF * g + HALF, lanes] = (
                        wide[0, HALF * i : HALF * i + HALF, :] * scale
                    )
    for level in range(ROWS):
        halo[level, LOCAL:PAD, :] = jnp.zeros((PAD - LOCAL, NLON), F32)
    mask_a = [jnp.concatenate([masks["a", r, 0], masks["a", r, 1]], axis=1) for r in range(ROWS)]
    mask_b = [jnp.concatenate([masks["b", r, 0], masks["b", r, 1]], axis=1) for r in range(ROWS)]
    sea_rows = [own[r, LOCAL : LOCAL + 1, :] for r in range(ROWS)]
    lane = iota((TRIP1, 128), 1)

    @pl.loop(0, PAD // TRIP1)
    def _(block):
        rows = pl.ds(pl.multiple_of(block * TRIP1, 8), TRIP1)
        geo = geo_ref[rows, :]

        def column(i, width):
            return jnp.broadcast_to(geo[:, i : i + 1], (TRIP1, width))

        cx = [column(i, NLON) for i in range(LEVELS)]
        cy = column(6, NLON)
        east = column(7, NLON) > 0.5
        north = column(8, NLON) > 0.5
        is_a = column(9, NLON) > 0.5
        e = [own[r, rows, :] for r in range(ROWS)]
        levels = [halo[r, rows, :] for r in range(ROWS)] + [
            jnp.where(north, e[0], e[2]),
            e[1],
            jnp.where(north, e[2], e[0]),
        ]
        sea = [jnp.where(is_a, mask_a[r], mask_b[r]) for r in range(ROWS)] + [
            jnp.where(north, sea_rows[0], sea_rows[2]),
            jnp.broadcast_to(sea_rows[1], (TRIP1, NLON)),
            jnp.where(north, sea_rows[2], sea_rows[0]),
        ]
        down = advected(levels, east, cx, cy, sea, NLON)
        new = [jnp.where(north, down[0], down[2]), down[1], jnp.where(north, down[2], down[0])]
        at = iota((TRIP1, NLON), 0) + block * TRIP1
        new = [jnp.where(at == LOCAL, sea_rows[r], new[r]) for r in range(ROWS)]
        tiles = [[new[r][:, 128 * t : 128 * t + 128] for t in range(4)] for r in range(ROWS)]
        turned = [[pltpu.roll(tiles[r][t], 64, 1) for t in range(4)] for r in range(ROWS)]
        for p in range(8):
            t = p // 2
            if p % 2 == 0:
                f = [jnp.where(lane < 96, tiles[r][t], tiles[r][(t + 3) % 4]) for r in range(ROWS)]
            else:
                f = [
                    jnp.where((lane >= 64) & (lane < 96), turned[r][(t + 1) % 4], turned[r][t])
                    for r in range(ROWS)
                ]
            low = jnp.where(lane < 64, f[0], pltpu.roll(f[1], 64, 1))
            high = f[2]
            high = jnp.where((lane >= 67) & (lane < 70), pltpu.roll(f[0], 3, 1), high)
            high = jnp.where((lane >= 70) & (lane < 73), pltpu.roll(f[1], 6, 1), high)
            high = jnp.where((lane >= 119) & (lane < 122), pltpu.roll(f[1], 122, 1), high)
            high = jnp.where((lane >= 122) & (lane < 125), pltpu.roll(f[0], 125, 1), high)
            wide[p, rows, 0:128] = low
            wide[p, rows, 128:256] = high

    at = iota((PAD, 128), 0)
    for out, (k, t) in zip(outs, HOPS):
        p = ((chip + k) % 4) * 2 + lax.bitwise_xor(core, t)
        low_mask, high_mask = (wide[p, LOCAL : LOCAL + 1, 128 * i : 128 * i + 128] for i in range(2))
        low, high = (jnp.where(at < LOCAL, wide[p, :, 128 * i : 128 * i + 128], 0.0) for i in range(2))
        q, code = to_code(low)
        paired = jnp.where(iota((88, 128), 1) < 64, high[0:88], pltpu.roll(high[80:168], 64, 1))
        q_pair, code_pair = to_code(paired)
        sides = jnp.where(iota((PAD, 128), 1) < 9, pltpu.roll(high, 64, 1), pltpu.roll(high, 18, 1))
        side_lane = iota((GROUP, 128), 1)
        side = jnp.zeros((GROUP, 128), F32)
        for g in range(7):
            part = sides[GROUP * g : GROUP * g + GROUP]
            part = pltpu.roll(part, 18 * g, 1) if g else part
            side = jnp.where((side_lane >= 18 * g) & (side_lane < 18 * g + 18), part, side)
        q_side, code_side = to_code(side)
        for i, row in enumerate((low_mask, code, code_side, high_mask)):
            q = jnp.where(at == LOCAL + i, row, q)
        packed[0:PAD, :] = q
        packed[PAD : PAD + 88, :] = jnp.where(iota((88, 128), 0) == 82, code_pair, q_pair)
        packed[PAD + 88 : WIRE, :] = q_side
        out[...] = rounded(packed[...])


CHUNK = 432


def add_sources(state, mask, one, two, xs, h1, h2):
    xs[...] = state[...].astype(jnp.bfloat16)

    @pl.loop(0, K // CHUNK)
    def _(i):
        rows = pl.ds(pl.multiple_of(i * CHUNK, 16), CHUNK)
        u = jnp.dot(one[rows, :], xs[...], preferred_element_type=F32)
        v = jnp.dot(two[rows, :], xs[...], preferred_element_type=F32)
        x = xs[rows, :].astype(F32)
        h1[rows, :] = (x * v * v).astype(jnp.bfloat16)
        h2[rows, :] = (x * u * u).astype(jnp.bfloat16)

    over = (((0,), (0,)), ((), ()))
    for first in range(0, K, 512):
        size = min(512, K - first)
        src = lax.dot_general(one[:, first : first + size], h1[...], over, preferred_element_type=F32)
        src = src - lax.dot_general(two[:, first : first + size], h2[...], over, preferred_element_type=F32)
        rows = slice(first, first + size)
        state[rows, :] = state[rows, :] + (SOURCE_RATE * mask) * src


SEND = 656


def second_kernel(where_ref, *refs):
    ins, (one, two), rest = refs[:8], refs[8:10], refs[10:]
    own, first_ref, second_ref, state, blocks, xs, h1, h2, scr, wire = rest
    lane = iota((GROUP, 128), 1)
    chip, core = where_ref[0], where_ref[1]
    for ref, (k, t) in zip(ins, HOPS):
        s = ((chip + 4 - k) % 4) * 2 + lax.bitwise_xor(core, t)
        wire[...] = ref[...].astype(F32)

        def scale(row):
            return from_wire(wire[row : row + 1, :])

        blocks[s, :, 0:128] = wire[0:PAD, :] * scale(LOCAL + 1)
        paired = wire[PAD : PAD + 88, :] * scale(PAD + 82)
        scr[0:88, 0:128] = paired
        scr[80:168, 0:128] = pltpu.roll(paired, 64, 1)
        side = wire[PAD + 88 : WIRE, :] * scale(LOCAL + 2)
        for g in range(7):
            rows = slice(GROUP * g, GROUP * g + GROUP)
            east = pltpu.roll(side, (64 - 18 * g) % 128, 1)
            west = pltpu.roll(side, (110 - 18 * g) % 128, 1)
            blocks[s, rows, 128:256] = jnp.where(
                lane < 64, scr[rows, 0:128], jnp.where(lane < 96, east, west)
            )
    mask = jnp.concatenate([wire[LOCAL : LOCAL + 1, :], wire[LOCAL + 3 : LOCAL + 4, :]], axis=1)
    for s in range(8):
        state[LOCAL * s : LOCAL * s + LOCAL, :] = blocks[s, 0:LOCAL, :]
    add_sources(state, mask, one, two, xs, h1, h2)
    n = K // 2
    odd = where_ref[2]
    for side in range(2):
        for f in range(NFREQ):
            first = NDIR * f + HALF * side
            own[side, HALF * f : HALF * f + HALF, :] = state[first : first + HALF, :]
    for side, out in ((odd, first_ref), (1 - odd, second_ref)):
        q, code = to_code(own[side, 0:n, :])
        scr[0:n, :] = q
        at = iota((SEND - n, 256), 0)
        scr[n:SEND, :] = jnp.where(at == 0, mask, jnp.where(at == 1, code, 0.0))
        out[...] = rounded(scr[...])
    own[0, n : n + 8, :] = jnp.broadcast_to(mask, (8, 256))
    own[1, n : n + 8, :] = jnp.broadcast_to(mask, (8, 256))


def spread(low, high, lane):
    out = []
    for body, by in ((low, 3), (pltpu.roll(low, 64, 1), 6)):
        side = jnp.where(lane < 96, pltpu.roll(high, 128 - by, 1), pltpu.roll(high, by, 1))
        out.append(jnp.where(lane < 64, body, side))
    return [out[0], out[1], high]


def advect_half(side, own, far_ref, geo_ref, out, scr, seas):
    lane = iota((8, 128), 1)
    lanes = iota((TRIP3, 128), 1)
    n = K // 2
    scr[...] = far_ref[...].astype(F32)
    scale = from_wire(scr[n + 1 : n + 2, :])
    far = jnp.broadcast_to(scr[n : n + 1, :], (8, 256))
    near = own[side, n : n + 8, :]
    south = side == 1

    def ordered(rows):
        return [jnp.where(south, rows[2], rows[0]), rows[1], jnp.where(south, rows[0], rows[2])]

    far, near = (spread(m[:, :128], m[:, 128:], lane) for m in (far, near))
    for i, row in enumerate(ordered(far) + ordered(near)):
        seas[i] = row
    scale = jnp.broadcast_to(scale, (TRIP3, 256))

    @pl.loop(0, n // TRIP3)
    def _(block):
        rows = pl.ds(pl.multiple_of(block * TRIP3, 8), TRIP3)
        geo = geo_ref[side, rows, :]

        def column(i):
            return jnp.broadcast_to(geo[:, i : i + 1], (TRIP3, 128))

        cx = [column(i) for i in range(LEVELS)]
        cy = column(6)
        east = column(7) > 0.5
        h = scr[rows, :] * scale
        e = own[side, rows, :]
        h, e = (spread(m[:, :128], m[:, 128:], lanes) for m in (h, e))
        levels = ordered(h) + ordered(e)
        sea = [jnp.tile(seas[i], (TRIP3 // 8, 1)) for i in range(LEVELS)]
        down = advected(levels, east, cx, cy, sea, 128)
        new = ordered(down)
        low = jnp.where(lanes < 64, new[0], pltpu.roll(new[1], 64, 1))
        high = jnp.where(lanes < 64, new[2], 0.0)
        out[rows, :] = jnp.concatenate([low, high], axis=1)


def half_kernel(where_ref, *refs):
    advect_half(1 - where_ref[2], *refs)


def third_kernel(where_ref, own, moved, far_ref, geo_ref, one, two, *rest):
    outs, (state, parts, blocks, xs, h1, h2, scr, seas) = rest[:8], rest[8:]
    chip, core = where_ref[0], where_ref[1]
    n = K // 2
    odd = where_ref[2]
    parts[1 - odd] = moved[...]
    advect_half(odd, own, far_ref, geo_ref, parts.at[odd], scr, seas)
    for side in range(2):
        for f in range(NFREQ):
            first = NDIR * f + HALF * side
            state[first : first + HALF, :] = parts[side, HALF * f : HALF * f + HALF, :]
    mask = own[0, n : n + 1, :]
    add_sources(state, mask, one, two, xs, h1, h2)
    for s in range(8):
        blocks[s, 0:LOCAL, :] = state[LOCAL * s : LOCAL * s + LOCAL, :]
        blocks[s, LOCAL:PAD, :] = jnp.zeros((PAD - LOCAL, 256), F32)
    for out, (k, t) in zip(outs, HOPS):
        s = ((chip + k) % 4) * 2 + lax.bitwise_xor(core, t)
        x = blocks[s]
        low, high = x[:, :128], x[:, 128:]
        paired = jnp.where(iota((88, 128), 1) < 64, high[0:88], pltpu.roll(high[80:168], 64, 1))
        for part, first, used in ((low, 0, LOCAL), (paired, PAD, 82)):
            size = part.shape[0]
            code = code_of(jnp.max(jnp.abs(part), axis=0, keepdims=True))
            q = jnp.where(iota((size, 128), 0) == used, code, part * to_wire(code))
            scr[first : first + size, 0:128] = q
        out[...] = rounded(scr[0:256, 0:128])


def last_kernel(where_ref, *refs):
    ins, (out, tiles, scr) = refs[:8], refs[8:]
    chip, core = where_ref[0], where_ref[1]
    for ref, (k, t) in zip(ins, HOPS):
        p = ((chip + 4 - k) % 4) * 2 + lax.bitwise_xor(core, t)
        scr[...] = ref[...].astype(F32)
        for first, size, used in ((0, PAD, LOCAL), (PAD, 88, 82)):
            scale = from_wire(scr[first + used : first + used + 1, :])
            tiles[p, first : first + size, :] = scr[first : first + size, :] * scale
    lane = iota((256, 128), 1)
    for t in range(4):
        a, b = tiles[2 * t], tiles[2 * t + 1]
        first = jnp.where(lane < 64, a, pltpu.roll(b, 64, 1))
        second = jnp.where(lane < 64, pltpu.roll(a, 64, 1), b)
        lanes = slice(128 * t, 128 * t + 128)
        out[0, :, lanes] = first[0:LOCAL]
        out[1, :, lanes] = second[0:LOCAL]
        out[2, 0:80, lanes] = first[PAD : PAD + 80]
        out[2, 80:LOCAL, lanes] = second[PAD : PAD + 82]


def call(kernel, out, ins, scratch, limit, weights=(), us=2, scalars=1):
    vmem = pl.BlockSpec(memory_space=pltpu.VMEM)
    smem = pl.BlockSpec(memory_space=pltpu.SMEM)
    return pl.pallas_call(
        kernel,
        out_shape=out,
        in_specs=[smem] * scalars + [vmem] * (len(ins) + len(weights) - scalars),
        out_specs=jax.tree.map(lambda _: vmem, out),
        scratch_shapes=[pltpu.VMEM(s, d) for s, d in scratch],
        compiler_params=pltpu.CompilerParams(vmem_limit_bytes=limit << 20),
        cost_estimate=pl.CostEstimate(flops=0, bytes_accessed=us * 3_500_000, transcendentals=0),
    )(*ins, *weights)


def tables(bands):
    turn = np.zeros((4, HALF, 16), np.float32)
    for side in range(2):
        d = np.arange(HALF) + HALF * side
        theta = 2.0 * math.pi / NDIR * (d + 0.5)
        turn[side, :, :LEVELS] = np.abs(np.cos(theta))[:, None]
        turn[side, :, 6] = np.abs(np.sin(theta))
        turn[2 + side, :, 7] = (4 * d + 2 < NDIR) | (4 * d + 2 > 3 * NDIR)
        turn[2 + side, :, 8] = 1 - side
    first = ROWS * np.arange(bands)[:, None]
    step = np.arange(LEVELS)[None]
    rows = np.stack([first - ROWS + step, first + LEVELS - 1 - step], axis=1)
    lat = np.zeros((bands, 2, 16), np.float32)
    lat[:, :, :LEVELS] = np.cos(math.pi / 180.0 * (-70.0 + 140.0 * (rows + 0.5) / (ROWS * bands)))
    lat[:, :, 6] = 1.0
    return turn, lat.reshape(2 * bands, 1, 16)


def exchanged(arrays):
    done = [arrays[0]]
    for x, (k, t) in list(zip(arrays, HOPS))[1:]:
        pairs = [
            (chip * 2 + core, ((chip + k) % 4) * 2 + (core ^ t)) for chip in range(4) for core in range(2)
        ]
        done.append(lax.ppermute(x, COMP, pairs))
    return done


def body(energy, land_sea, group_speed, interp_one, interp_two):
    bands = lax.axis_size("band")
    band = lax.axis_index("band")
    chip = lax.axis_index("comp_0")
    core = lax.axis_index("comp_1")
    here = jnp.stack([chip, core, band % 2, band]).astype(jnp.int32)
    e = jnp.transpose(energy, (1, 0, 2))
    shape = jax.ShapeDtypeStruct

    own, first, second = call(
        halo_kernel,
        (
            shape((ROWS, PAD, NLON), F32),
            shape((ROWS, FAR, NLON), I16),
            shape((ROWS, FAR, NLON), I16),
        ),
        (here, e, land_sea),
        [((FAR, NLON), F32)],
        8,
    )
    pairs = [
        [(i + j, i + 1 - j) for i in range(start, bands - 1, 2) for j in range(2)] for start in range(2)
    ]
    first = lax.ppermute(first, "band", pairs[0])
    second = lax.ppermute(second, "band", pairs[1])

    turn, lat = (jnp.asarray(t) for t in tables(bands))
    geo_here, geo_sides = call(
        geometry_kernel,
        (shape((PAD, 16), F32), shape((2, K // 2, 16), F32)),
        (here, group_speed, own, turn, lat),
        [],
        4,
        scalars=2,
    )

    packed = call(
        first_kernel,
        [shape((WIRE, 128), I16)] * 8,
        (here, own, first, second, geo_here),
        [
            ((ROWS, PAD, NLON), F32),
            ((8, PAD, 256), F32),
            ((WIRE, 128), F32),
        ],
        10,
        us=6,
    )
    nothing = jnp.minimum(packed[0][LOCAL, 0], 0).astype(jnp.bfloat16)
    weights = (interp_one + nothing, interp_two + nothing)
    packed = exchanged(packed)

    half = K // 2
    matmul_scratch = [((K, 256), jnp.bfloat16)] * 3
    own, first, second = call(
        second_kernel,
        (shape((2, half + 8, 256), F32), shape((SEND, 256), I16), shape((SEND, 256), I16)),
        (here, *packed),
        [((K, 256), F32), ((8, PAD, 256), F32)] + matmul_scratch + [((SEND, 256), F32), ((WIRE, 128), F32)],
        14,
        weights,
        8,
    )
    nothing = jnp.minimum(own[0, half, 0], 0).astype(jnp.bfloat16)
    weights = (interp_one + nothing, interp_two + nothing)
    first = lax.ppermute(first, "band", pairs[0])
    second = lax.ppermute(second, "band", pairs[1])

    advect_scratch = [((SEND, 256), F32), ((LEVELS, 8, 128), F32)]
    moved = call(
        half_kernel,
        shape((half, 256), F32),
        (here, own, first, geo_sides),
        advect_scratch,
        8,
        us=5,
    )
    final = call(
        third_kernel,
        [shape((256, 128), I16)] * 8,
        (here, own, moved, second, geo_sides),
        [((K, 256), F32), ((2, half, 256), F32), ((8, PAD, 256), F32)]
        + matmul_scratch
        + advect_scratch,
        16,
        weights,
        16,
    )
    final = exchanged(final)
    out = call(
        last_kernel,
        shape((ROWS, LOCAL, NLON), F32),
        (here, *final),
        [((8, 256, 128), F32), ((256, 128), F32)],
        8,
    )
    return jnp.transpose(out, (1, 0, 2))


def solution(mesh):
    finer = Mesh(mesh.devices.reshape(mesh.shape["band"], 4, 2), EVERY)
    return jax.shard_map(
        body,
        mesh=finer,
        in_specs=(P(COMP, "band", None), P("band", None), P(), P(), P()),
        out_specs=P(COMP, "band", None),
        check_vma=False,
    )
```

```python
import functools
import math

import jax
import jax.numpy as jnp
import numpy as np
from jax import lax
from jax.experimental import pallas as pl
from jax.experimental.pallas import tpu as pltpu
from jax.sharding import Mesh
from jax.sharding import PartitionSpec as P

NDIR = 36
NFREQ = 36
K = NDIR * NFREQ
ROWS = 3
NLON = 512
HALF = NDIR // 2
LOCAL = 162
PAD = 168
SOURCE_RATE = 0.05
COMP = ("comp_0", "comp_1")
EVERY = ("band", "comp_0", "comp_1")
LEVELS = 2 * ROWS
HOPS = ((0, 0), (1, 0), (3, 0), (2, 0), (2, 1), (1, 1), (3, 1), (0, 1))
A_RUNS, B_RUNS = (0, 2, 4, 6, 8), (1, 3, 5, 7)
FAR = 96
WIRE = 280
GROUP = 24
TRIP1, RUN1 = 168, 56
TRIP3 = 216
TOP = 32767.0
F32 = jnp.float32
I16 = jnp.int16


def code_of(largest):
    return jnp.ceil(jnp.log2(jnp.maximum(largest, 1e-30)) * 128.0)


def to_wire(code):
    return jnp.exp2(code * (-1.0 / 128.0)) * TOP


def from_wire(code):
    return jnp.exp2(code * (1.0 / 128.0)) * (1.0 / TOP)


def to_code(values):
    code = code_of(jnp.max(jnp.abs(values), axis=0, keepdims=True))
    return values * to_wire(code), code


def rounded(values):
    return jnp.floor(values + 0.5).astype(jnp.int32).astype(I16)


def iota(shape, dim):
    return lax.broadcasted_iota(jnp.int32, shape, dim)


def halo_kernel(where_ref, e_ref, sea_ref, own, first_ref, second_ref, scr):
    core = where_ref[1]
    sea = [sea_ref[r : r + 1, :].astype(F32) for r in range(ROWS)]
    for row in range(ROWS):
        own[row, 0:LOCAL, :] = e_ref[row] * sea[row]
        own[row, LOCAL:PAD, :] = jnp.broadcast_to(sea[row], (PAD - LOCAL, NLON))
    a_first = core == where_ref[2]
    for level in range(ROWS):
        row_a = level + core * (2 - 2 * level)
        made = []
        for row, groups in ((row_a, A_RUNS), (2 - row_a, B_RUNS)):
            n = HALF * len(groups)
            for i, g in enumerate(groups):
                scr[HALF * i : HALF * i + HALF, :] = own[row, HALF * g : HALF * g + HALF, :]
            scr[n:FAR, :] = jnp.zeros((FAR - n, NLON), F32)
            q, code = to_code(scr[...])
            at = iota((FAR, NLON), 0)
            q = jnp.where(at == FAR - 6, own[row, LOCAL : LOCAL + 1, :], q)
            made.append(jnp.where(at == FAR - 5, code, q))
        first_ref[level] = rounded(jnp.where(a_first, made[0], made[1]))
        second_ref[level] = rounded(jnp.where(a_first, made[1], made[0]))


COLUMNS = (1, 2, 3, 4, 5, 6, 7)


def geometry_kernel(where_ref, speed, after, turn, lat, geo_ref, sides_ref):
    chip, core = where_ref[0], where_ref[1]
    moving = [turn[side] * lat[2 * where_ref[3] + side] for side in range(2)]
    for side in range(2):
        flags = turn[2 + side]
        for i, column in enumerate(COLUMNS):
            factor, flag = (
                jnp.broadcast_to(t[:, column : column + 1], (HALF, 128)) for t in (moving[side], flags)
            )
            for f in range(NFREQ):
                sides_ref[side, i, HALF * f : HALF * f + HALF, :] = speed[f] * factor + flag
    for g in range(LOCAL // HALF):
        run = (chip * 2 + core) * (LOCAL // HALF) + g
        side = (core + g) % 2
        columns = speed[run // 2] * jnp.where(side == 0, moving[0], moving[1]) + turn[2 + side]
        if g in A_RUNS:
            columns = columns + jnp.where(iota((HALF, 16), 1) == 9, 1.0, 0.0)
        geo_ref[HALF * g : HALF * g + HALF, :] = columns
    geo_ref[LOCAL:PAD, :] = jnp.zeros((PAD - LOCAL, 16), F32)


def one_substep(level, here, upstream, east, cx, cy, sea, width):
    shifted = jnp.where(east, pltpu.roll(here, 1, 1), pltpu.roll(here, width - 1, 1))
    return (here - cx[level] * (here - shifted) - cy * (here - upstream)) * sea


def advected(levels, east, cx, cy, sea, width):
    for substep in range(ROWS):
        levels = [
            one_substep(i, levels[i], levels[i - 1], east, cx, cy, sea[i], width)
            if i > substep
            else levels[i]
            for i in range(LEVELS)
        ]
    return levels[ROWS:]


def first_kernel(where_ref, own, first_ref, second_ref, geo_ref, *rest):
    outs, (halo, wide, packed) = rest[:8], rest[8:]
    chip, core = where_ref[0], where_ref[1]
    a_second = core == where_ref[2]
    masks = {}
    for level in range(ROWS):
        for side in range(2):
            lanes = slice(256 * side, 256 * side + 256)
            came = [ref[level, :, lanes].astype(F32) for ref in (first_ref, second_ref)]
            for name, groups, x in (
                ("a", A_RUNS, jnp.where(a_second, came[1], came[0])),
                ("b", B_RUNS, jnp.where(a_second, came[0], came[1])),
            ):
                wide[0, 0:FAR, :] = x
                scale = from_wire(wide[0, FAR - 5 : FAR - 4, :])
                masks[name, level, side] = wide[0, FAR - 6 : FAR - 5, :]
                for i, g in enumerate(groups):
                    halo[level, HALF * g : HALF * g + HALF, lanes] = (
                        wide[0, HALF * i : HALF * i + HALF, :] * scale
                    )
    for level in range(ROWS):
        halo[level, LOCAL:PAD, :] = jnp.zeros((PAD - LOCAL, NLON), F32)
    mask_a = [jnp.concatenate([masks["a", r, 0], masks["a", r, 1]], axis=1) for r in range(ROWS)]
    mask_b = [jnp.concatenate([masks["b", r, 0], masks["b", r, 1]], axis=1) for r in range(ROWS)]
    sea_rows = [own[r, LOCAL : LOCAL + 1, :] for r in range(ROWS)]
    lane = iota((RUN1, 128), 1)

    def chain(start):
        rows = pl.ds(pl.multiple_of(start, 8), RUN1)
        geo = geo_ref[rows, :]

        def column(i, width):
            return jnp.broadcast_to(geo[:, i : i + 1], (RUN1, width))

        cx = [column(i, NLON) for i in range(LEVELS)]
        cy = column(6, NLON)
        east = column(7, NLON) > 0.5
        north = column(8, NLON) > 0.5
        is_a = column(9, NLON) > 0.5
        e = [own[r, rows, :] for r in range(ROWS)]
        levels = [halo[r, rows, :] for r in range(ROWS)] + [
            jnp.where(north, e[0], e[2]),
            e[1],
            jnp.where(north, e[2], e[0]),
        ]
        sea = [jnp.where(is_a, mask_a[r], mask_b[r]) for r in range(ROWS)] + [
            jnp.where(north, sea_rows[0], sea_rows[2]),
            jnp.broadcast_to(sea_rows[1], (RUN1, NLON)),
            jnp.where(north, sea_rows[2], sea_rows[0]),
        ]
        down = advected(levels, east, cx, cy, sea, NLON)
        new = [jnp.where(north, down[0], down[2]), down[1], jnp.where(north, down[2], down[0])]
        at = iota((RUN1, NLON), 0) + start
        new = [jnp.where(at == LOCAL, sea_rows[r], new[r]) for r in range(ROWS)]
        tiles = [[new[r][:, 128 * t : 128 * t + 128] for t in range(4)] for r in range(ROWS)]
        turned = [[pltpu.roll(tiles[r][t], 64, 1) for t in range(4)] for r in range(ROWS)]
        made = []
        for p in range(8):
            t = p // 2
            if p % 2 == 0:
                f = [jnp.where(lane < 96, tiles[r][t], tiles[r][(t + 3) % 4]) for r in range(ROWS)]
            else:
                f = [
                    jnp.where((lane >= 64) & (lane < 96), turned[r][(t + 1) % 4], turned[r][t])
                    for r in range(ROWS)
                ]
            low = jnp.where(lane < 64, f[0], pltpu.roll(f[1], 64, 1))
            high = f[2]
            high = jnp.where((lane >= 67) & (lane < 70), pltpu.roll(f[0], 3, 1), high)
            high = jnp.where((lane >= 70) & (lane < 73), pltpu.roll(f[1], 6, 1), high)
            high = jnp.where((lane >= 119) & (lane < 122), pltpu.roll(f[1], 122, 1), high)
            high = jnp.where((lane >= 122) & (lane < 125), pltpu.roll(f[0], 125, 1), high)
            made.append((p, rows, low, high))
        return made

    @pl.loop(0, PAD // TRIP1)
    def _(trip):
        done = [chain(trip * TRIP1 + i * RUN1) for i in range(TRIP1 // RUN1)]
        for p, rows, low, high in sum(done, []):
            wide[p, rows, 0:128] = low
            wide[p, rows, 128:256] = high

    at = iota((PAD, 128), 0)
    for out, (k, t) in zip(outs, HOPS):
        p = ((chip + k) % 4) * 2 + lax.bitwise_xor(core, t)
        low_mask, high_mask = (wide[p, LOCAL : LOCAL + 1, 128 * i : 128 * i + 128] for i in range(2))
        low, high = (jnp.where(at < LOCAL, wide[p, :, 128 * i : 128 * i + 128], 0.0) for i in range(2))
        q, code = to_code(low)
        paired = jnp.where(iota((88, 128), 1) < 64, high[0:88], pltpu.roll(high[80:168], 64, 1))
        q_pair, code_pair = to_code(paired)
        sides = jnp.where(iota((PAD, 128), 1) < 9, pltpu.roll(high, 64, 1), pltpu.roll(high, 18, 1))
        side_lane = iota((GROUP, 128), 1)
        side = jnp.zeros((GROUP, 128), F32)
        for g in range(7):
            part = sides[GROUP * g : GROUP * g + GROUP]
            part = pltpu.roll(part, 18 * g, 1) if g else part
            side = jnp.where((side_lane >= 18 * g) & (side_lane < 18 * g + 18), part, side)
        q_side, code_side = to_code(side)
        for i, row in enumerate((low_mask, code, code_side, high_mask)):
            q = jnp.where(at == LOCAL + i, row, q)
        packed[0:PAD, :] = q
        packed[PAD : PAD + 88, :] = jnp.where(iota((88, 128), 0) == 82, code_pair, q_pair)
        packed[PAD + 88 : WIRE, :] = q_side
        out[...] = rounded(packed[...])


CHUNK = 432


def add_sources(state, mask, one, two, xs, h1, h2):
    xs[...] = state[...].astype(jnp.bfloat16)

    @pl.loop(0, K // CHUNK)
    def _(i):
        rows = pl.ds(pl.multiple_of(i * CHUNK, 16), CHUNK)
        u = jnp.dot(one[rows, :], xs[...], preferred_element_type=F32)
        v = jnp.dot(two[rows, :], xs[...], preferred_element_type=F32)
        x = xs[rows, :].astype(F32)
        h1[rows, :] = (x * v * v).astype(jnp.bfloat16)
        h2[rows, :] = (x * u * u).astype(jnp.bfloat16)

    over = (((0,), (0,)), ((), ()))
    for first in range(0, K, 512):
        size = min(512, K - first)
        src = lax.dot_general(one[:, first : first + size], h1[...], over, preferred_element_type=F32)
        src = src - lax.dot_general(two[:, first : first + size], h2[...], over, preferred_element_type=F32)
        rows = slice(first, first + size)
        state[rows, :] = state[rows, :] + (SOURCE_RATE * mask) * src


SEND = 656


def second_kernel(where_ref, *refs):
    ins, (one, two), rest = refs[:8], refs[8:10], refs[10:]
    own, first_ref, second_ref, state, blocks, xs, h1, h2, scr, wire = rest
    lane = iota((GROUP, 128), 1)
    chip, core = where_ref[0], where_ref[1]
    for ref, (k, t) in zip(ins, HOPS):
        s = ((chip + 4 - k) % 4) * 2 + lax.bitwise_xor(core, t)
        wire[...] = ref[...].astype(F32)

        def scale(row):
            return from_wire(wire[row : row + 1, :])

        blocks[s, :, 0:128] = wire[0:PAD, :] * scale(LOCAL + 1)
        paired = wire[PAD : PAD + 88, :] * scale(PAD + 82)
        scr[0:88, 0:128] = paired
        scr[80:168, 0:128] = pltpu.roll(paired, 64, 1)
        side = wire[PAD + 88 : WIRE, :] * scale(LOCAL + 2)
        for g in range(7):
            rows = slice(GROUP * g, GROUP * g + GROUP)
            east = pltpu.roll(side, (64 - 18 * g) % 128, 1)
            west = pltpu.roll(side, (110 - 18 * g) % 128, 1)
            blocks[s, rows, 128:256] = jnp.where(
                lane < 64, scr[rows, 0:128], jnp.where(lane < 96, east, west)
            )
    mask = jnp.concatenate([wire[LOCAL : LOCAL + 1, :], wire[LOCAL + 3 : LOCAL + 4, :]], axis=1)
    for s in range(8):
        state[LOCAL * s : LOCAL * s + LOCAL, :] = blocks[s, 0:LOCAL, :]
    add_sources(state, mask, one, two, xs, h1, h2)
    n = K // 2
    odd = where_ref[2]
    for side in range(2):
        for f in range(NFREQ):
            first = NDIR * f + HALF * side
            own[side, HALF * f : HALF * f + HALF, :] = state[first : first + HALF, :]
    for side, out in ((odd, first_ref), (1 - odd, second_ref)):
        q, code = to_code(own[side, 0:n, :])
        scr[0:n, :] = q
        at = iota((SEND - n, 256), 0)
        scr[n:SEND, :] = jnp.where(at == 0, mask, jnp.where(at == 1, code, 0.0))
        out[...] = rounded(scr[...])
    own[0, n : n + 8, :] = jnp.broadcast_to(mask, (8, 256))
    own[1, n : n + 8, :] = jnp.broadcast_to(mask, (8, 256))


def spread(low, high, lane):
    out = []
    for body, by in ((low, 3), (pltpu.roll(low, 64, 1), 6)):
        side = jnp.where(lane < 96, pltpu.roll(high, 128 - by, 1), pltpu.roll(high, by, 1))
        out.append(jnp.where(lane < 64, body, side))
    return [out[0], out[1], high]


def advect_half(side, own, far_ref, geo_ref, out, scr, seas):
    lane = iota((8, 128), 1)
    lanes = iota((TRIP3, 128), 1)
    n = K // 2
    scr[...] = far_ref[...].astype(F32)
    scale = from_wire(scr[n + 1 : n + 2, :])
    far = jnp.broadcast_to(scr[n : n + 1, :], (8, 256))
    near = own[side, n : n + 8, :]
    south = side == 1

    def ordered(rows):
        return [jnp.where(south, rows[2], rows[0]), rows[1], jnp.where(south, rows[0], rows[2])]

    far, near = (spread(m[:, :128], m[:, 128:], lane) for m in (far, near))
    for i, row in enumerate(ordered(far) + ordered(near)):
        seas[i] = row
    scale = jnp.broadcast_to(scale, (TRIP3, 256))

    @pl.loop(0, n // TRIP3)
    def _(block):
        rows = pl.ds(pl.multiple_of(block * TRIP3, 8), TRIP3)
        cx = [None] + [geo_ref[side, i, rows, :] for i in range(5)]
        cy = geo_ref[side, 5, rows, :]
        east = geo_ref[side, 6, rows, :] > 0.5
        h = scr[rows, :] * scale
        e = own[side, rows, :]
        h, e = (spread(m[:, :128], m[:, 128:], lanes) for m in (h, e))
        levels = ordered(h) + ordered(e)
        sea = [jnp.tile(seas[i], (TRIP3 // 8, 1)) for i in range(LEVELS)]
        down = advected(levels, east, cx, cy, sea, 128)
        new = ordered(down)
        low = jnp.where(lanes < 64, new[0], pltpu.roll(new[1], 64, 1))
        high = jnp.where(lanes < 64, new[2], 0.0)
        out[rows, :] = jnp.concatenate([low, high], axis=1)


def half_kernel(where_ref, *refs):
    advect_half(1 - where_ref[2], *refs)


def third_kernel(where_ref, own, moved, far_ref, geo_ref, one, two, *rest):
    outs, (state, parts, blocks, xs, h1, h2, scr, seas) = rest[:8], rest[8:]
    chip, core = where_ref[0], where_ref[1]
    n = K // 2
    odd = where_ref[2]
    parts[1 - odd] = moved[...]
    advect_half(odd, own, far_ref, geo_ref, parts.at[odd], scr, seas)
    for side in range(2):
        for f in range(NFREQ):
            first = NDIR * f + HALF * side
            state[first : first + HALF, :] = parts[side, HALF * f : HALF * f + HALF, :]
    mask = own[0, n : n + 1, :]
    add_sources(state, mask, one, two, xs, h1, h2)
    for s in range(8):
        blocks[s, 0:LOCAL, :] = state[LOCAL * s : LOCAL * s + LOCAL, :]
        blocks[s, LOCAL:PAD, :] = jnp.zeros((PAD - LOCAL, 256), F32)
    for out, (k, t) in zip(outs, HOPS):
        s = ((chip + k) % 4) * 2 + lax.bitwise_xor(core, t)
        x = blocks[s]
        low, high = x[:, :128], x[:, 128:]
        paired = jnp.where(iota((88, 128), 1) < 64, high[0:88], pltpu.roll(high[80:168], 64, 1))
        for part, first, used in ((low, 0, LOCAL), (paired, PAD, 82)):
            size = part.shape[0]
            code = code_of(jnp.max(jnp.abs(part), axis=0, keepdims=True))
            q = jnp.where(iota((size, 128), 0) == used, code, part * to_wire(code))
            scr[first : first + size, 0:128] = q
        out[...] = rounded(scr[0:256, 0:128])


def last_kernel(where_ref, *refs):
    ins, (out, tiles, scr) = refs[:8], refs[8:]
    chip, core = where_ref[0], where_ref[1]
    for ref, (k, t) in zip(ins, HOPS):
        p = ((chip + 4 - k) % 4) * 2 + lax.bitwise_xor(core, t)
        scr[...] = ref[...].astype(F32)
        for first, size, used in ((0, PAD, LOCAL), (PAD, 88, 82)):
            scale = from_wire(scr[first + used : first + used + 1, :])
            tiles[p, first : first + size, :] = scr[first : first + size, :] * scale
    lane = iota((256, 128), 1)
    for t in range(4):
        a, b = tiles[2 * t], tiles[2 * t + 1]
        first = jnp.where(lane < 64, a, pltpu.roll(b, 64, 1))
        second = jnp.where(lane < 64, pltpu.roll(a, 64, 1), b)
        lanes = slice(128 * t, 128 * t + 128)
        out[0, :, lanes] = first[0:LOCAL]
        out[1, :, lanes] = second[0:LOCAL]
        out[2, 0:80, lanes] = first[PAD : PAD + 80]
        out[2, 80:LOCAL, lanes] = second[PAD : PAD + 82]


def call(kernel, out, ins, scratch, limit, weights=(), us=2, scalars=1):
    vmem = pl.BlockSpec(memory_space=pltpu.VMEM)
    smem = pl.BlockSpec(memory_space=pltpu.SMEM)
    return pl.pallas_call(
        kernel,
        out_shape=out,
        in_specs=[smem] * scalars + [vmem] * (len(ins) + len(weights) - scalars),
        out_specs=jax.tree.map(lambda _: vmem, out),
        scratch_shapes=[pltpu.VMEM(s, d) for s, d in scratch],
        compiler_params=pltpu.CompilerParams(vmem_limit_bytes=limit << 20),
        cost_estimate=pl.CostEstimate(flops=0, bytes_accessed=us * 3_500_000, transcendentals=0),
    )(*ins, *weights)


def tables(bands):
    turn = np.zeros((4, HALF, 16), np.float32)
    for side in range(2):
        d = np.arange(HALF) + HALF * side
        theta = 2.0 * math.pi / NDIR * (d + 0.5)
        turn[side, :, :LEVELS] = np.abs(np.cos(theta))[:, None]
        turn[side, :, 6] = np.abs(np.sin(theta))
        turn[2 + side, :, 7] = (4 * d + 2 < NDIR) | (4 * d + 2 > 3 * NDIR)
        turn[2 + side, :, 8] = 1 - side
    first = ROWS * np.arange(bands)[:, None]
    step = np.arange(LEVELS)[None]
    rows = np.stack([first - ROWS + step, first + LEVELS - 1 - step], axis=1)
    lat = np.zeros((bands, 2, 16), np.float32)
    lat[:, :, :LEVELS] = np.cos(math.pi / 180.0 * (-70.0 + 140.0 * (rows + 0.5) / (ROWS * bands)))
    lat[:, :, 6] = 1.0
    return turn, lat.reshape(2 * bands, 1, 16)


def exchanged(arrays):
    done = [arrays[0]]
    for x, (k, t) in list(zip(arrays, HOPS))[1:]:
        pairs = [
            (chip * 2 + core, ((chip + k) % 4) * 2 + (core ^ t)) for chip in range(4) for core in range(2)
        ]
        done.append(lax.ppermute(x, COMP, pairs))
    return done


def body(energy, land_sea, group_speed, interp_one, interp_two):
    bands = lax.axis_size("band")
    band = lax.axis_index("band")
    chip = lax.axis_index("comp_0")
    core = lax.axis_index("comp_1")
    here = jnp.stack([chip, core, band % 2, band]).astype(jnp.int32)
    e = jnp.transpose(energy, (1, 0, 2))
    shape = jax.ShapeDtypeStruct

    own, first, second = call(
        halo_kernel,
        (
            shape((ROWS, PAD, NLON), F32),
            shape((ROWS, FAR, NLON), I16),
            shape((ROWS, FAR, NLON), I16),
        ),
        (here, e, land_sea),
        [((FAR, NLON), F32)],
        8,
    )
    pairs = [
        [(i + j, i + 1 - j) for i in range(start, bands - 1, 2) for j in range(2)] for start in range(2)
    ]
    first = lax.ppermute(first, "band", pairs[0])
    second = lax.ppermute(second, "band", pairs[1])

    turn, lat = (jnp.asarray(t) for t in tables(bands))
    geo_here, geo_sides = call(
        geometry_kernel,
        (shape((PAD, 16), F32), shape((2, len(COLUMNS), K // 2, 128), F32)),
        (here, group_speed, own, turn, lat),
        [],
        8,
        scalars=2,
    )

    packed = call(
        first_kernel,
        [shape((WIRE, 128), I16)] * 8,
        (here, own, first, second, geo_here),
        [
            ((ROWS, PAD, NLON), F32),
            ((8, PAD, 256), F32),
            ((WIRE, 128), F32),
        ],
        10,
        us=6,
    )
    nothing = jnp.minimum(packed[0][LOCAL, 0], 0).astype(jnp.bfloat16)
    weights = (interp_one + nothing, interp_two + nothing)
    packed = exchanged(packed)

    half = K // 2
    matmul_scratch = [((K, 256), jnp.bfloat16)] * 3
    own, first, second = call(
        second_kernel,
        (shape((2, half + 8, 256), F32), shape((SEND, 256), I16), shape((SEND, 256), I16)),
        (here, *packed),
        [((K, 256), F32), ((8, PAD, 256), F32)] + matmul_scratch + [((SEND, 256), F32), ((WIRE, 128), F32)],
        14,
        weights,
        8,
    )
    nothing = jnp.minimum(own[0, half, 0], 0).astype(jnp.bfloat16)
    weights = (interp_one + nothing, interp_two + nothing)
    first = lax.ppermute(first, "band", pairs[0])
    second = lax.ppermute(second, "band", pairs[1])

    advect_scratch = [((SEND, 256), F32), ((LEVELS, 8, 128), F32)]
    moved = call(
        half_kernel,
        shape((half, 256), F32),
        (here, own, first, geo_sides),
        advect_scratch,
        8,
        us=5,
    )
    final = call(
        third_kernel,
        [shape((256, 128), I16)] * 8,
        (here, own, moved, second, geo_sides),
        [((K, 256), F32), ((2, half, 256), F32), ((8, PAD, 256), F32)]
        + matmul_scratch
        + advect_scratch,
        16,
        weights,
        16,
    )
    final = exchanged(final)
    out = call(
        last_kernel,
        shape((ROWS, LOCAL, NLON), F32),
        (here, *final),
        [((8, 256, 128), F32), ((256, 128), F32)],
        8,
    )
    return jnp.transpose(out, (1, 0, 2))


def solution(mesh):
    finer = Mesh(mesh.devices.reshape(mesh.shape["band"], 4, 2), EVERY)
    return jax.shard_map(
        body,
        mesh=finer,
        in_specs=(P(COMP, "band", None), P("band", None), P(), P(), P()),
        out_specs=P(COMP, "band", None),
        check_vma=False,
    )
```

```python
import functools
import math

import jax
import jax.numpy as jnp
import numpy as np
from jax import lax
from jax.experimental import pallas as pl
from jax.experimental.pallas import tpu as pltpu
from jax.sharding import Mesh
from jax.sharding import PartitionSpec as P

NDIR = 36
NFREQ = 36
K = NDIR * NFREQ
ROWS = 3
NLON = 512
HALF = NDIR // 2
LOCAL = 162
PAD = 168
SOURCE_RATE = 0.05
COMP = ("comp_0", "comp_1")
EVERY = ("band", "comp_0", "comp_1")
LEVELS = 2 * ROWS
HOPS = ((0, 0), (1, 0), (3, 0), (2, 0), (2, 1), (1, 1), (3, 1), (0, 1))
A_RUNS, B_RUNS = (0, 2, 4, 6, 8), (1, 3, 5, 7)
FAR = 96
WIRE = 280
GROUP = 24
TRIP1, RUN1 = 168, 56
TRIP3 = 216
TOP = 32767.0
F32 = jnp.float32
I16 = jnp.int16


def code_of(largest):
    return jnp.ceil(jnp.log2(jnp.maximum(largest, 1e-30)) * 128.0)


def to_wire(code):
    return jnp.exp2(code * (-1.0 / 128.0)) * TOP


def from_wire(code):
    return jnp.exp2(code * (1.0 / 128.0)) * (1.0 / TOP)


def to_code(values):
    code = code_of(jnp.max(jnp.abs(values), axis=0, keepdims=True))
    return values * to_wire(code), code


def rounded(values):
    return jnp.floor(values + 0.5).astype(jnp.int32).astype(I16)


def iota(shape, dim):
    return lax.broadcasted_iota(jnp.int32, shape, dim)


def halo_kernel(where_ref, e_ref, sea_ref, own, first_ref, second_ref, scr):
    core = where_ref[1]
    sea = [sea_ref[r : r + 1, :].astype(F32) for r in range(ROWS)]
    for row in range(ROWS):
        own[row, 0:LOCAL, :] = e_ref[row] * sea[row]
        own[row, LOCAL:PAD, :] = jnp.broadcast_to(sea[row], (PAD - LOCAL, NLON))
    a_first = core == where_ref[2]
    for level in range(ROWS):
        row_a = level + core * (2 - 2 * level)
        made = []
        for row, groups in ((row_a, A_RUNS), (2 - row_a, B_RUNS)):
            n = HALF * len(groups)
            for i, g in enumerate(groups):
                scr[HALF * i : HALF * i + HALF, :] = own[row, HALF * g : HALF * g + HALF, :]
            scr[n:FAR, :] = jnp.zeros((FAR - n, NLON), F32)
            q, code = to_code(scr[...])
            at = iota((FAR, NLON), 0)
            q = jnp.where(at == FAR - 6, own[row, LOCAL : LOCAL + 1, :], q)
            made.append(jnp.where(at == FAR - 5, code, q))
        first_ref[level] = rounded(jnp.where(a_first, made[0], made[1]))
        second_ref[level] = rounded(jnp.where(a_first, made[1], made[0]))


COLUMNS = (1, 2, 3, 4, 5, 6, 7)


def geometry_kernel(where_ref, speed, after, turn, lat, geo_ref, sides_ref):
    chip, core = where_ref[0], where_ref[1]
    moving = [turn[side] * lat[2 * where_ref[3] + side] for side in range(2)]
    for side in range(2):
        flags = turn[2 + side]
        for i, column in enumerate(COLUMNS):
            factor, flag = (
                jnp.broadcast_to(t[:, column : column + 1], (HALF, 128)) for t in (moving[side], flags)
            )
            for f in range(NFREQ):
                sides_ref[side, i, HALF * f : HALF * f + HALF, :] = speed[f] * factor + flag
    for g in range(LOCAL // HALF):
        run = (chip * 2 + core) * (LOCAL // HALF) + g
        side = (core + g) % 2
        columns = speed[run // 2] * jnp.where(side == 0, moving[0], moving[1]) + turn[2 + side]
        if g in A_RUNS:
            columns = columns + jnp.where(iota((HALF, 16), 1) == 9, 1.0, 0.0)
        geo_ref[HALF * g : HALF * g + HALF, :] = columns
    geo_ref[LOCAL:PAD, :] = jnp.zeros((PAD - LOCAL, 16), F32)


def one_substep(level, here, upstream, east, cx, cy, sea, width):
    shifted = jnp.where(east, pltpu.roll(here, 1, 1), pltpu.roll(here, width - 1, 1))
    return (here - cx[level] * (here - shifted) - cy * (here - upstream)) * sea


def advected(levels, east, cx, cy, sea, width):
    for substep in range(ROWS):
        levels = [
            one_substep(i, levels[i], levels[i - 1], east, cx, cy, sea[i], width)
            if i > substep
            else levels[i]
            for i in range(LEVELS)
        ]
    return levels[ROWS:]


def first_kernel(where_ref, own, first_ref, second_ref, geo_ref, *rest):
    outs, (halo, wide, packed) = rest[:8], rest[8:]
    chip, core = where_ref[0], where_ref[1]
    a_second = core == where_ref[2]
    masks = {}
    for level in range(ROWS):
        for side in range(2):
            lanes = slice(256 * side, 256 * side + 256)
            came = [ref[level, :, lanes].astype(F32) for ref in (first_ref, second_ref)]
            for name, groups, x in (
                ("a", A_RUNS, jnp.where(a_second, came[1], came[0])),
                ("b", B_RUNS, jnp.where(a_second, came[0], came[1])),
            ):
                wide[0, 0:FAR, :] = x
                scale = from_wire(wide[0, FAR - 5 : FAR - 4, :])
                masks[name, level, side] = wide[0, FAR - 6 : FAR - 5, :]
                for i, g in enumerate(groups):
                    halo[level, HALF * g : HALF * g + HALF, lanes] = (
                        wide[0, HALF * i : HALF * i + HALF, :] * scale
                    )
    for level in range(ROWS):
        halo[level, LOCAL:PAD, :] = jnp.zeros((PAD - LOCAL, NLON), F32)
    mask_a = [jnp.concatenate([masks["a", r, 0], masks["a", r, 1]], axis=1) for r in range(ROWS)]
    mask_b = [jnp.concatenate([masks["b", r, 0], masks["b", r, 1]], axis=1) for r in range(ROWS)]
    sea_rows = [own[r, LOCAL : LOCAL + 1, :] for r in range(ROWS)]
    lane = iota((RUN1, 128), 1)

    def chain(start):
        rows = pl.ds(pl.multiple_of(start, 8), RUN1)
        geo = geo_ref[rows, :]

        def column(i, width):
            return jnp.broadcast_to(geo[:, i : i + 1], (RUN1, width))

        cx = [column(i, NLON) for i in range(LEVELS)]
        cy = column(6, NLON)
        east = column(7, NLON) > 0.5
        north = column(8, NLON) > 0.5
        is_a = column(9, NLON) > 0.5
        e = [own[r, rows, :] for r in range(ROWS)]
        levels = [halo[r, rows, :] for r in range(ROWS)] + [
            jnp.where(north, e[0], e[2]),
            e[1],
            jnp.where(north, e[2], e[0]),
        ]
        sea = [jnp.where(is_a, mask_a[r], mask_b[r]) for r in range(ROWS)] + [
            jnp.where(north, sea_rows[0], sea_rows[2]),
            jnp.broadcast_to(sea_rows[1], (RUN1, NLON)),
            jnp.where(north, sea_rows[2], sea_rows[0]),
        ]
        down = advected(levels, east, cx, cy, sea, NLON)
        new = [jnp.where(north, down[0], down[2]), down[1], jnp.where(north, down[2], down[0])]
        at = iota((RUN1, NLON), 0) + start
        new = [jnp.where(at == LOCAL, sea_rows[r], new[r]) for r in range(ROWS)]
        tiles = [[new[r][:, 128 * t : 128 * t + 128] for t in range(4)] for r in range(ROWS)]
        turned = [[pltpu.roll(tiles[r][t], 64, 1) for t in range(4)] for r in range(ROWS)]
        made = []
        for p in range(8):
            t = p // 2
            if p % 2 == 0:
                f = [jnp.where(lane < 96, tiles[r][t], tiles[r][(t + 3) % 4]) for r in range(ROWS)]
            else:
                f = [
                    jnp.where((lane >= 64) & (lane < 96), turned[r][(t + 1) % 4], turned[r][t])
                    for r in range(ROWS)
                ]
            low = jnp.where(lane < 64, f[0], pltpu.roll(f[1], 64, 1))
            high = f[2]
            high = jnp.where((lane >= 67) & (lane < 70), pltpu.roll(f[0], 3, 1), high)
            high = jnp.where((lane >= 70) & (lane < 73), pltpu.roll(f[1], 6, 1), high)
            high = jnp.where((lane >= 119) & (lane < 122), pltpu.roll(f[1], 122, 1), high)
            high = jnp.where((lane >= 122) & (lane < 125), pltpu.roll(f[0], 125, 1), high)
            made.append((p, rows, low, high))
        return made

    @pl.loop(0, PAD // TRIP1)
    def _(trip):
        done = [chain(trip * TRIP1 + i * RUN1) for i in range(TRIP1 // RUN1)]
        for p, rows, low, high in sum(done, []):
            wide[p, rows, 0:128] = low
            wide[p, rows, 128:256] = high

    at = iota((PAD, 128), 0)
    for out, (k, t) in zip(outs, HOPS):
        p = ((chip + k) % 4) * 2 + lax.bitwise_xor(core, t)
        low_mask, high_mask = (wide[p, LOCAL : LOCAL + 1, 128 * i : 128 * i + 128] for i in range(2))
        low, high = (jnp.where(at < LOCAL, wide[p, :, 128 * i : 128 * i + 128], 0.0) for i in range(2))
        q, code = to_code(low)
        paired = jnp.where(iota((88, 128), 1) < 64, high[0:88], pltpu.roll(high[80:168], 64, 1))
        q_pair, code_pair = to_code(paired)
        sides = jnp.where(iota((PAD, 128), 1) < 9, pltpu.roll(high, 64, 1), pltpu.roll(high, 18, 1))
        side_lane = iota((GROUP, 128), 1)
        side = jnp.zeros((GROUP, 128), F32)
        for g in range(7):
            part = sides[GROUP * g : GROUP * g + GROUP]
            part = pltpu.roll(part, 18 * g, 1) if g else part
            side = jnp.where((side_lane >= 18 * g) & (side_lane < 18 * g + 18), part, side)
        q_side, code_side = to_code(side)
        for i, row in enumerate((low_mask, code, code_side, high_mask)):
            q = jnp.where(at == LOCAL + i, row, q)
        packed[0:PAD, :] = q
        packed[PAD : PAD + 88, :] = jnp.where(iota((88, 128), 0) == 82, code_pair, q_pair)
        packed[PAD + 88 : WIRE, :] = q_side
        out[...] = rounded(packed[...])


CHUNK = 1296


def add_sources(state, mask, one, two, xs, h1, h2):
    xs[...] = state[...].astype(jnp.bfloat16)

    @pl.loop(0, K // CHUNK)
    def _(i):
        rows = pl.ds(pl.multiple_of(i * CHUNK, 16), CHUNK)
        u = jnp.dot(one[rows, :], xs[...], preferred_element_type=F32)
        v = jnp.dot(two[rows, :], xs[...], preferred_element_type=F32)
        x = xs[rows, :].astype(F32)
        h1[rows, :] = (x * v * v).astype(jnp.bfloat16)
        h2[rows, :] = (x * u * u).astype(jnp.bfloat16)

    over = (((0,), (0,)), ((), ()))
    for first in range(0, K, 512):
        size = min(512, K - first)
        src = lax.dot_general(one[:, first : first + size], h1[...], over, preferred_element_type=F32)
        src = src - lax.dot_general(two[:, first : first + size], h2[...], over, preferred_element_type=F32)
        rows = slice(first, first + size)
        state[rows, :] = state[rows, :] + (SOURCE_RATE * mask) * src


SEND = 656


def second_kernel(where_ref, *refs):
    ins, (one, two), rest = refs[:8], refs[8:10], refs[10:]
    own, first_ref, second_ref, state, blocks, xs, h1, h2, scr, wire = rest
    lane = iota((GROUP, 128), 1)
    chip, core = where_ref[0], where_ref[1]
    for ref, (k, t) in zip(ins, HOPS):
        s = ((chip + 4 - k) % 4) * 2 + lax.bitwise_xor(core, t)
        wire[...] = ref[...].astype(F32)

        def scale(row):
            return from_wire(wire[row : row + 1, :])

        blocks[s, :, 0:128] = wire[0:PAD, :] * scale(LOCAL + 1)
        paired = wire[PAD : PAD + 88, :] * scale(PAD + 82)
        scr[0:88, 0:128] = paired
        scr[80:168, 0:128] = pltpu.roll(paired, 64, 1)
        side = wire[PAD + 88 : WIRE, :] * scale(LOCAL + 2)
        for g in range(7):
            rows = slice(GROUP * g, GROUP * g + GROUP)
            east = pltpu.roll(side, (64 - 18 * g) % 128, 1)
            west = pltpu.roll(side, (110 - 18 * g) % 128, 1)
            blocks[s, rows, 128:256] = jnp.where(
                lane < 64, scr[rows, 0:128], jnp.where(lane < 96, east, west)
            )
    mask = jnp.concatenate([wire[LOCAL : LOCAL + 1, :], wire[LOCAL + 3 : LOCAL + 4, :]], axis=1)
    for s in range(8):
        state[LOCAL * s : LOCAL * s + LOCAL, :] = blocks[s, 0:LOCAL, :]
    add_sources(state, mask, one, two, xs, h1, h2)
    n = K // 2
    odd = where_ref[2]
    for side in range(2):
        for f in range(NFREQ):
            first = NDIR * f + HALF * side
            own[side, HALF * f : HALF * f + HALF, :] = state[first : first + HALF, :]
    for side, out in ((odd, first_ref), (1 - odd, second_ref)):
        q, code = to_code(own[side, 0:n, :])
        scr[0:n, :] = q
        at = iota((SEND - n, 256), 0)
        scr[n:SEND, :] = jnp.where(at == 0, mask, jnp.where(at == 1, code, 0.0))
        out[...] = rounded(scr[...])
    own[0, n : n + 8, :] = jnp.broadcast_to(mask, (8, 256))
    own[1, n : n + 8, :] = jnp.broadcast_to(mask, (8, 256))


def spread(low, high, lane):
    out = []
    for body, by in ((low, 3), (pltpu.roll(low, 64, 1), 6)):
        side = jnp.where(lane < 96, pltpu.roll(high, 128 - by, 1), pltpu.roll(high, by, 1))
        out.append(jnp.where(lane < 64, body, side))
    return [out[0], out[1], high]


def advect_half(side, own, far_ref, geo_ref, out, scr, seas):
    lane = iota((8, 128), 1)
    lanes = iota((TRIP3, 128), 1)
    n = K // 2
    scr[...] = far_ref[...].astype(F32)
    scale = from_wire(scr[n + 1 : n + 2, :])
    far = jnp.broadcast_to(scr[n : n + 1, :], (8, 256))
    near = own[side, n : n + 8, :]
    south = side == 1

    def ordered(rows):
        return [jnp.where(south, rows[2], rows[0]), rows[1], jnp.where(south, rows[0], rows[2])]

    far, near = (spread(m[:, :128], m[:, 128:], lane) for m in (far, near))
    for i, row in enumerate(ordered(far) + ordered(near)):
        seas[i] = row
    scale = jnp.broadcast_to(scale, (TRIP3, 256))

    @pl.loop(0, n // TRIP3)
    def _(block):
        rows = pl.ds(pl.multiple_of(block * TRIP3, 8), TRIP3)
        cx = [None] + [geo_ref[side, i, rows, :] for i in range(5)]
        cy = geo_ref[side, 5, rows, :]
        east = geo_ref[side, 6, rows, :] > 0.5
        h = scr[rows, :] * scale
        e = own[side, rows, :]
        h, e = (spread(m[:, :128], m[:, 128:], lanes) for m in (h, e))
        levels = ordered(h) + ordered(e)
        sea = [jnp.tile(seas[i], (TRIP3 // 8, 1)) for i in range(LEVELS)]
        down = advected(levels, east, cx, cy, sea, 128)
        new = ordered(down)
        low = jnp.where(lanes < 64, new[0], pltpu.roll(new[1], 64, 1))
        high = jnp.where(lanes < 64, new[2], 0.0)
        out[rows, :] = jnp.concatenate([low, high], axis=1)


def half_kernel(where_ref, *refs):
    advect_half(1 - where_ref[2], *refs)


def third_kernel(where_ref, own, moved, far_ref, geo_ref, one, two, *rest):
    outs, (state, parts, blocks, xs, h1, h2, scr, seas) = rest[:8], rest[8:]
    chip, core = where_ref[0], where_ref[1]
    n = K // 2
    odd = where_ref[2]
    parts[1 - odd] = moved[...]
    advect_half(odd, own, far_ref, geo_ref, parts.at[odd], scr, seas)
    for side in range(2):
        for f in range(NFREQ):
            first = NDIR * f + HALF * side
            state[first : first + HALF, :] = parts[side, HALF * f : HALF * f + HALF, :]
    mask = own[0, n : n + 1, :]
    add_sources(state, mask, one, two, xs, h1, h2)
    for s in range(8):
        blocks[s, 0:LOCAL, :] = state[LOCAL * s : LOCAL * s + LOCAL, :]
        blocks[s, LOCAL:PAD, :] = jnp.zeros((PAD - LOCAL, 256), F32)
    for out, (k, t) in zip(outs, HOPS):
        s = ((chip + k) % 4) * 2 + lax.bitwise_xor(core, t)
        x = blocks[s]
        low, high = x[:, :128], x[:, 128:]
        paired = jnp.where(iota((88, 128), 1) < 64, high[0:88], pltpu.roll(high[80:168], 64, 1))
        for part, first, used in ((low, 0, LOCAL), (paired, PAD, 82)):
            size = part.shape[0]
            code = code_of(jnp.max(jnp.abs(part), axis=0, keepdims=True))
            q = jnp.where(iota((size, 128), 0) == used, code, part * to_wire(code))
            scr[first : first + size, 0:128] = q
        out[...] = rounded(scr[0:256, 0:128])


def last_kernel(where_ref, *refs):
    ins, (out, tiles, scr) = refs[:8], refs[8:]
    chip, core = where_ref[0], where_ref[1]
    for ref, (k, t) in zip(ins, HOPS):
        p = ((chip + 4 - k) % 4) * 2 + lax.bitwise_xor(core, t)
        scr[...] = ref[...].astype(F32)
        for first, size, used in ((0, PAD, LOCAL), (PAD, 88, 82)):
            scale = from_wire(scr[first + used : first + used + 1, :])
            tiles[p, first : first + size, :] = scr[first : first + size, :] * scale
    lane = iota((256, 128), 1)
    for t in range(4):
        a, b = tiles[2 * t], tiles[2 * t + 1]
        first = jnp.where(lane < 64, a, pltpu.roll(b, 64, 1))
        second = jnp.where(lane < 64, pltpu.roll(a, 64, 1), b)
        lanes = slice(128 * t, 128 * t + 128)
        out[0, :, lanes] = first[0:LOCAL]
        out[1, :, lanes] = second[0:LOCAL]
        out[2, 0:80, lanes] = first[PAD : PAD + 80]
        out[2, 80:LOCAL, lanes] = second[PAD : PAD + 82]


def call(kernel, out, ins, scratch, limit, weights=(), us=2, scalars=1):
    vmem = pl.BlockSpec(memory_space=pltpu.VMEM)
    smem = pl.BlockSpec(memory_space=pltpu.SMEM)
    return pl.pallas_call(
        kernel,
        out_shape=out,
        in_specs=[smem] * scalars + [vmem] * (len(ins) + len(weights) - scalars),
        out_specs=jax.tree.map(lambda _: vmem, out),
        scratch_shapes=[pltpu.VMEM(s, d) for s, d in scratch],
        compiler_params=pltpu.CompilerParams(vmem_limit_bytes=limit << 20),
        cost_estimate=pl.CostEstimate(flops=0, bytes_accessed=us * 3_500_000, transcendentals=0),
    )(*ins, *weights)


def tables(bands):
    turn = np.zeros((4, HALF, 16), np.float32)
    for side in range(2):
        d = np.arange(HALF) + HALF * side
        theta = 2.0 * math.pi / NDIR * (d + 0.5)
        turn[side, :, :LEVELS] = np.abs(np.cos(theta))[:, None]
        turn[side, :, 6] = np.abs(np.sin(theta))
        turn[2 + side, :, 7] = (4 * d + 2 < NDIR) | (4 * d + 2 > 3 * NDIR)
        turn[2 + side, :, 8] = 1 - side
    first = ROWS * np.arange(bands)[:, None]
    step = np.arange(LEVELS)[None]
    rows = np.stack([first - ROWS + step, first + LEVELS - 1 - step], axis=1)
    lat = np.zeros((bands, 2, 16), np.float32)
    lat[:, :, :LEVELS] = np.cos(math.pi / 180.0 * (-70.0 + 140.0 * (rows + 0.5) / (ROWS * bands)))
    lat[:, :, 6] = 1.0
    return turn, lat.reshape(2 * bands, 1, 16)


def exchanged(arrays):
    done = [arrays[0]]
    for x, (k, t) in list(zip(arrays, HOPS))[1:]:
        pairs = [
            (chip * 2 + core, ((chip + k) % 4) * 2 + (core ^ t)) for chip in range(4) for core in range(2)
        ]
        done.append(lax.ppermute(x, COMP, pairs))
    return done


def body(energy, land_sea, group_speed, interp_one, interp_two):
    bands = lax.axis_size("band")
    band = lax.axis_index("band")
    chip = lax.axis_index("comp_0")
    core = lax.axis_index("comp_1")
    here = jnp.stack([chip, core, band % 2, band]).astype(jnp.int32)
    e = jnp.transpose(energy, (1, 0, 2))
    shape = jax.ShapeDtypeStruct

    own, first, second = call(
        halo_kernel,
        (
            shape((ROWS, PAD, NLON), F32),
            shape((ROWS, FAR, NLON), I16),
            shape((ROWS, FAR, NLON), I16),
        ),
        (here, e, land_sea),
        [((FAR, NLON), F32)],
        8,
    )
    pairs = [
        [(i + j, i + 1 - j) for i in range(start, bands - 1, 2) for j in range(2)] for start in range(2)
    ]
    first = lax.ppermute(first, "band", pairs[0])
    second = lax.ppermute(second, "band", pairs[1])

    turn, lat = (jnp.asarray(t) for t in tables(bands))
    geo_here, geo_sides = call(
        geometry_kernel,
        (shape((PAD, 16), F32), shape((2, len(COLUMNS), K // 2, 128), F32)),
        (here, group_speed, own, turn, lat),
        [],
        8,
        scalars=2,
    )

    packed = call(
        first_kernel,
        [shape((WIRE, 128), I16)] * 8,
        (here, own, first, second, geo_here),
        [
            ((ROWS, PAD, NLON), F32),
            ((8, PAD, 256), F32),
            ((WIRE, 128), F32),
        ],
        10,
        us=6,
    )
    nothing = jnp.minimum(packed[0][LOCAL, 0], 0).astype(jnp.bfloat16)
    weights = (interp_one + nothing, interp_two + nothing)
    packed = exchanged(packed)

    half = K // 2
    matmul_scratch = [((K, 256), jnp.bfloat16)] * 3
    own, first, second = call(
        second_kernel,
        (shape((2, half + 8, 256), F32), shape((SEND, 256), I16), shape((SEND, 256), I16)),
        (here, *packed),
        [((K, 256), F32), ((8, PAD, 256), F32)] + matmul_scratch + [((SEND, 256), F32), ((WIRE, 128), F32)],
        14,
        weights,
        8,
    )
    nothing = jnp.minimum(own[0, half, 0], 0).astype(jnp.bfloat16)
    weights = (interp_one + nothing, interp_two + nothing)
    first = lax.ppermute(first, "band", pairs[0])
    second = lax.ppermute(second, "band", pairs[1])

    advect_scratch = [((SEND, 256), F32), ((LEVELS, 8, 128), F32)]
    moved = call(
        half_kernel,
        shape((half, 256), F32),
        (here, own, first, geo_sides),
        advect_scratch,
        8,
        us=5,
    )
    final = call(
        third_kernel,
        [shape((256, 128), I16)] * 8,
        (here, own, moved, second, geo_sides),
        [((K, 256), F32), ((2, half, 256), F32), ((8, PAD, 256), F32)]
        + matmul_scratch
        + advect_scratch,
        16,
        weights,
        16,
    )
    final = exchanged(final)
    out = call(
        last_kernel,
        shape((ROWS, LOCAL, NLON), F32),
        (here, *final),
        [((8, 256, 128), F32), ((256, 128), F32)],
        8,
    )
    return jnp.transpose(out, (1, 0, 2))


def solution(mesh):
    finer = Mesh(mesh.devices.reshape(mesh.shape["band"], 4, 2), EVERY)
    return jax.shard_map(
        body,
        mesh=finer,
        in_specs=(P(COMP, "band", None), P("band", None), P(), P(), P()),
        out_specs=P(COMP, "band", None),
        check_vma=False,
    )
```
